32 devices in a mesh: row: 4 (over y, x), col: 8 (over z, core).
Axes of the slice: x: 2, y: 2, z: 4, core: 2. Of those that a mesh axis runs over, the one named last changes fastest.
Arguments:
- activations: bfloat16 [8192, 1024], P(('row', 'col')), may hold values from -6 to 6
- out_grads: bfloat16 [28672, 1024], P(('row', 'col')), may hold values from -0.0059814453 to 0.0059814453
- accumulated: float32 [28672, 8192], P(('row', 'col')), may hold values from -0.18 to 0.18
- seed_basis: float32 [8192, 512], P('row'), may hold values from -6 to 6
- moment_first: float32 [28672, 512], P(('row', 'col')), may hold values from -0.6 to 0.6
- moment_second: float32 [28672, 512], P(('row', 'col')), may hold values from 0.001 to 0.1
Outputs:
- basis: bfloat16 [8192, 512], P(('row', 'col'))
- first_next: float32 [28672, 512], P(('row', 'col'))
- second_next: float32 [28672, 512], P(('row', 'col'))
- lifted: float32 [28672, 8192], P(('row', 'col'))
The draws below stay inside these ranges and needn't reach their ends.
All inputs are finite; a program needn't handle non-finite values.
Results may differ from the reference program's by a relative error of at most 0.0029.
Values may be sent and summed in bfloat16 or wider, within the bound.
A program may use at most 192 MiB of HBM per device.

```python
import math
import jax
import jax.numpy as jnp
from jax import lax

D = 8192
FF = 28672
R = 512
TOKENS = 1024


def draw_accumulated(key, part):
    inner = jax.random.fold_in(key, 7)
    values = jnp.clip(0.03 * jax.random.normal(inner, (FF, D), jnp.float32), -0.18, 0.18)
    return values.astype(jnp.float32)


def levels(own_key, extent, shards, low, largest):
    def one(dim, shards_of):
        steps = jax.random.uniform(jax.random.fold_in(jax.random.fold_in(own_key, 6), dim), (shards_of,), jnp.float32, low / len(shards), largest / len(shards))
        return jnp.repeat(jnp.exp(steps), extent[dim] // shards_of).reshape((-1,) + (1,) * (len(extent) - dim - 1))

    loudness = one(*shards[0])
    for cut in shards[1:]:
        loudness = loudness * one(*cut)
    return loudness


def centred(rng, dims, scale, limit, pieces=(), dtype=jnp.bfloat16):
    array = scale * jax.random.normal(rng, dims, jnp.float32)
    if pieces:
        array = array * levels(rng, dims, pieces, -0.22, 0.18)
    return jnp.clip(array, -limit, limit).astype(dtype)


def setup_inputs(seed: int = 0) -> dict:
    streams_of = jax.random.split(jax.random.key(seed), 7)
    activations = centred(streams_of[0], (D, TOKENS), 1.0, 6.0, ((0, 32),))
    out_grads = centred(streams_of[1], (FF, TOKENS), 0.001, 0.0059814453, ((0, 32),))
    accumulated = draw_accumulated(jax.random.fold_in(streams_of[6], 71), 0)
    seed_basis = centred(streams_of[3], (D, R), 1.0, 6.0, ((0, 4),), jnp.float32)
    moment_first = centred(streams_of[4], (FF, R), 0.1, 0.6, ((0, 32),), jnp.float32)
    moment_second = jnp.clip(jnp.exp(math.log(0.1) - 4.6051702 * jax.random.uniform(streams_of[5], (FF, R), jnp.float32) ** levels(streams_of[5], (FF, R), ((0, 32),), -0.2, 0.2)), 0.001, 0.1)
    return dict(activations=activations, out_grads=out_grads, accumulated=accumulated, seed_basis=seed_basis, moment_first=moment_first, moment_second=moment_second)


beta_first = 0.9
beta_second = 0.99
correct_first = 1.0 - 0.9 ** 10
correct_second = 1.0 - 0.99 ** 10
epsilon_value = 1e-08
lift_scale = 8.0

def reference(activations, out_grads, accumulated, seed_basis, moment_first, moment_second):
    highest = lax.Precision.HIGHEST
    grad_t = accumulated + jnp.dot(out_grads.astype(jnp.float32), activations.astype(jnp.float32).T, precision=highest)
    image_rows = jnp.dot(grad_t, seed_basis, precision=highest)
    power_rows = jnp.dot(grad_t.T, image_rows, precision=highest)
    gram_matrix = jnp.dot(power_rows.T, power_rows, precision=highest)
    lower_factor = jnp.linalg.cholesky(gram_matrix)
    solved = jax.scipy.linalg.solve_triangular(lower_factor, power_rows.T, lower=True)
    basis_rows = solved.T.astype(jnp.bfloat16)
    widened = basis_rows.astype(jnp.float32)
    projected = jnp.dot(grad_t, widened, precision=highest)
    first_next = beta_first * moment_first + (1.0 - beta_first) * projected
    second_next = beta_second * moment_second + (1.0 - beta_second) * projected * projected
    direction = first_next / correct_first / (jnp.sqrt(second_next / correct_second) + epsilon_value)
    lifted = lift_scale * jnp.dot(direction, widened.T, precision=highest)
    return (basis_rows, first_next, second_next, lifted)
```

```python
import functools

import jax
import jax.numpy as jnp
from jax import lax
from jax.experimental import pallas as pl
from jax.experimental.pallas import tpu as pltpu
from jax.sharding import PartitionSpec as P

beta_first = 0.9
beta_second = 0.99
correct_first = 1.0 - 0.9**10
correct_second = 1.0 - 0.99**10
epsilon_value = 1e-08
lift_scale = 8.0

every = ("row", "col")
highest = lax.Precision.HIGHEST
high = lax.Precision.HIGH
bf16 = jnp.bfloat16
f32 = jnp.float32
MESH = pl.DeviceIdType.MESH
ANY = pl.BlockSpec(memory_space=pl.ANY)
VMEM = pl.BlockSpec(memory_space=pltpu.VMEM)
DMA = pltpu.SemaphoreType.DMA
vmem_bytes = 63 * 2**20


def mul(left, right, dims, precision=None):
    return lax.dot_general(
        left, right, (dims, ((), ())), precision=precision, preferred_element_type=jnp.float32
    )


rows_cols = ((1,), (0,))
rows_rows = ((0,), (0,))
cols_cols = ((1,), (1,))


def split(value):
    upper = value.astype(bf16)
    return upper, (value - upper.astype(f32)).astype(bf16)


class Grid:
    def __init__(self, rows, cols):
        self.rows, self.chips = rows, cols // 2
        self.stages = rows.bit_length() - 1
        self.r = lax.axis_index("row")
        c = lax.axis_index("col")
        self.z, self.k = c // 2, c % 2
        self.c = c
        self.partner = (self.r, self.z * 2 + 1 - self.k)

    def flip(self, bit):
        return self.r + bit * (1 - 2 * ((self.r // bit) % 2))

    def peer_row(self, s):
        low, high_bit = 2**s, 2 ** (self.stages - 1 - s)
        return (1 - self.k) * self.flip(low) + self.k * self.flip(high_bit)

    def peer(self, s):
        return (self.peer_row(s), self.c)

    def count(self, s):
        return 2 ** (self.stages - 1 - s)

    def block(self, s, j, base):
        n = self.count(s)
        first = base % 2 ** (s + 1) + j * 2 ** (s + 1)
        second = (base // n) * n + j
        return (1 - self.k) * first + self.k * second

    def chip(self, w):
        n = self.chips
        return (self.z + 1 + w) % n, (self.z + n - 1 - w) % n

    def chip_device(self, z):
        return (self.r, z * 2 + self.k)

    def greet(self):
        barrier = pltpu.get_barrier_semaphore()
        peers = [self.partner]
        peers += [self.peer(s) for s in range(self.stages)]
        peers += [self.chip_device(self.chip(w)[0]) for w in range(self.chips - 1)]
        for peer in peers:
            pl.semaphore_signal(barrier, inc=1, device_id=peer, device_id_type=MESH)
        pl.semaphore_wait(barrier, len(peers))


def remote(source, target, send, recv, device):
    return pltpu.make_async_remote_copy(
        src_ref=source, dst_ref=target, send_sem=send, recv_sem=recv,
        device_id=device, device_id_type=MESH,
    )


class AllReduce:
    def __init__(self, grid, part, full, half_in, stage_in, chip_in, send, recv):
        self.g, self.part, self.full = grid, part, full
        self.half_in, self.stage_in, self.chip_in = half_in, stage_in, chip_in
        self.send, self.recv = send, recv
        self.half = part.shape[0] // 2
        self.chunk = self.half // grid.rows
        self.unit = self.chunk // grid.chips
        self.pending = []
        self.used = 0
        self.phases = (
            [self.pair_out]
            + [functools.partial(self.halve, s) for s in range(grid.stages)]
            + [self.chips_out, self.chips_back]
            + [functools.partial(self.double, s) for s in reversed(range(grid.stages))]
            + [self.pair_back, self.finish]
        )
        self.arrived = []

    @staticmethod
    def scratch(rows, width, grid_rows, chips):
        half = rows // 2
        chunk = half // grid_rows
        stages = grid_rows.bit_length() - 1
        copies = 2 + 2 * (grid_rows - 1) + 2 * (chips - 1)
        return [
            pltpu.VMEM((rows, width), f32),
            pltpu.VMEM((rows, width), f32),
            pltpu.VMEM((half, width), f32),
            pltpu.VMEM((grid_rows - 1, chunk, width), f32),
            pltpu.VMEM((chips - 1, chunk // chips, width), f32),
            DMA((copies,)),
            DMA((copies,)),
        ]

    def start(self, source, target, device):
        i = self.used
        self.used += 1
        copy = remote(source, target, self.send.at[i], self.recv.at[i], device)
        copy.start()
        self.pending.append(copy)
        self.arrived.append(copy)

    def landed(self):
        arrived, self.arrived = self.arrived, []
        for copy in arrived:
            copy.wait_recv()

    def rows_of(self, r):
        return pl.ds(pl.multiple_of((self.g.k * self.g.rows + r) * self.chunk, self.chunk), self.chunk)

    def unit_of(self, r, z):
        at = ((self.g.k * self.g.rows + r) * self.g.chips + z) * self.unit
        return pl.ds(pl.multiple_of(at, self.unit), self.unit)

    def pair_out(self):
        g = self.g
        other = pl.ds(pl.multiple_of((1 - g.k) * self.half, self.half), self.half)
        self.start(self.part.at[other], self.half_in, g.partner)

    def stage_base(self, s):
        return self.g.rows - 2 ** (self.g.stages - s)

    def halve(self, s):
        g = self.g
        self.landed()
        if s == 0:
            mine = pl.ds(pl.multiple_of(g.k * self.half, self.half), self.half)
            self.part[mine] += self.half_in[...]
        else:
            self.take(s - 1)
        for j in range(g.count(s)):
            rows = self.rows_of(g.block(s, j, g.peer_row(s)))
            self.start(self.part.at[rows], self.stage_in.at[self.stage_base(s) + j], g.peer(s))

    def take(self, s):
        g = self.g
        for j in range(g.count(s)):
            self.part[self.rows_of(g.block(s, j, g.r))] += self.stage_in[self.stage_base(s) + j]

    def chips_out(self):
        g = self.g
        self.landed()
        self.take(g.stages - 1)
        for w in range(g.chips - 1):
            z = g.chip(w)[0]
            self.start(self.part.at[self.unit_of(g.r, z)], self.chip_in.at[w], g.chip_device(z))

    def chips_back(self):
        g = self.g
        self.landed()
        own = self.unit_of(g.r, g.z)
        total = self.part[own]
        for w in range(g.chips - 1):
            total = total + self.chip_in[w]
        self.full[own] = total
        for w in range(g.chips - 1):
            self.start(self.full.at[own], self.full.at[own], g.chip_device(g.chip(w)[0]))

    def double(self, s):
        g = self.g
        self.landed()
        for j in range(g.count(s)):
            rows = self.rows_of(g.block(s, j, g.r))
            self.start(self.full.at[rows], self.full.at[rows], g.peer(s))

    def pair_back(self):
        g = self.g
        self.landed()
        mine = pl.ds(pl.multiple_of(g.k * self.half, self.half), self.half)
        self.start(self.full.at[mine], self.full.at[mine], g.partner)

    def finish(self):
        self.landed()

    def drain(self):
        for copy in self.pending:
            copy.wait_send()


def reduce_kernel(rows, cols, part_ref, out_ref, *scratch):
    grid = Grid(rows, cols)
    grid.greet()
    part, full, *rest = scratch
    part[...] = part_ref[...]
    total = AllReduce(grid, part, full, *rest)
    for phase in total.phases:
        phase()
    out_ref[...] = full[...]
    total.drain()


def all_reduce(value, rows, cols, collective_id):
    return pl.pallas_call(
        functools.partial(reduce_kernel, rows, cols),
        out_shape=jax.ShapeDtypeStruct(value.shape, f32),
        in_specs=[VMEM],
        out_specs=VMEM,
        scratch_shapes=AllReduce.scratch(*value.shape, rows, cols // 2),
        compiler_params=pltpu.CompilerParams(
            collective_id=collective_id, has_side_effects=True, vmem_limit_bytes=vmem_bytes
        ),
        name="all_reduce",
    )(value)


def power_kernel(
    rows, cols, acc, pair_ref, grads_ref, acts_ref, out_ref,
    tiles, mine, theirs, pair_in, stage_in, chip_in,
    tile_sem, pair_sems, stage_sems, chip_sems, *reduce_scratch,
):
    g = Grid(rows, cols)
    blk = acts_ref.shape[0]
    rank = out_ref.shape[0]
    chips, stages = g.chips, g.stages

    def chip_of(w):
        return g.chip(w)[0]

    def fetch(w, rp, kind):
        core = (1 - g.k) if kind == 0 else g.k
        at = ((rp * chips + (g.z + 1 + w) % chips) * 2 + core) * blk
        columns = pl.ds(pl.multiple_of(at, blk), blk)
        slot = (w * rows + rp) % 2
        return pltpu.make_async_copy(
            acc.at[:, columns], tiles.at[kind * 2 + slot], tile_sem.at[kind * 2 + slot]
        )

    for rp in range(2):
        fetch(0, rp, 0).start()
        fetch(0, rp, 1).start()
    g.greet()

    part, full, *rest = reduce_scratch
    part[...] = mul(pair_ref[:rank], grads_ref[...], rows_cols) + mul(
        pair_ref[rank:], grads_ref[...], rows_cols
    )
    tokens = AllReduce(g, part, full, *rest)
    phases = iter(tokens.phases)

    def tick():
        phase = next(phases, None)
        if phase is not None:
            phase()

    tick()

    def product(slot):
        upper, lower = split(tiles[slot])
        both = mul(pair_ref[...], upper, rows_cols)
        return both[:rank] + both[rank:] + mul(pair_ref[:rank], lower, rows_cols)

    def pair_copy(w, rp):
        i = w * rows + rp
        return remote(theirs.at[i], pair_in.at[i], pair_sems.at[0, i], pair_sems.at[1, i], g.partner)

    def stage_copy(w, s, j):
        i = w * (rows - 1) + rows - 2 ** (stages - s) + j
        source = mine.at[w * rows + g.block(s, j, g.peer_row(s))]
        return remote(source, stage_in.at[i], stage_sems.at[0, i], stage_sems.at[1, i], g.peer(s))

    def chip_copy(w):
        return remote(
            mine.at[w * rows + g.r], chip_in.at[w], chip_sems.at[0, w], chip_sems.at[1, w],
            g.chip_device(chip_of(w)),
        )

    def compute(w):
        def step(rp, carry):
            i = w * rows + rp
            slot = i % 2
            for kind, store in ((0, theirs), (1, mine)):
                fetch(w, rp, kind).wait()
                store[i] = product(kind * 2 + slot)
                if kind == 0:
                    pair_copy(w, rp).start()

                @pl.when(i + 2 < chips * rows)
                def _():
                    fetch((i + 2) // rows, (i + 2) % rows, kind).start()
            return carry

        lax.fori_loop(0, rows, step, 0)

    def add(index, value_ref, at):
        mine[index] += value_ref[at]

    def halve(w, s):
        if s == 0:
            for base, send in ((g.peer_row(0), True), (g.r, False)):
                for j in range(g.count(0)):
                    rp = g.block(0, j, base)
                    pair_copy(w, rp).wait_recv()
                    add(w * rows + rp, pair_in, w * rows + rp)
                    if send:
                        stage_copy(w, 0, j).start()
            return
        for j in range(g.count(s - 1)):
            i = w * (rows - 1) + rows - 2 ** (stages - s + 1) + j
            stage_copy(w, s - 1, j).wait_recv()
            add(w * rows + g.block(s - 1, j, g.r), stage_in, i)
        for j in range(g.count(s)):
            stage_copy(w, s, j).start()

    def leave(w):
        i = w * (rows - 1) + rows - 2
        stage_copy(w, stages - 1, 0).wait_recv()
        add(w * rows + g.r, stage_in, i)
        if w < chips - 1:
            chip_copy(w).start()

    for at in range(chips + stages + 1):
        if at < chips:
            compute(at)
        for later in range(1, stages + 1):
            w = at - later
            if 0 <= w < chips:
                tick()
                halve(w, later - 1)
        w = at - stages - 1
        if 0 <= w < chips:
            tick()
            leave(w)
    for phase in phases:
        phase()
    upper, lower = split(full[...])
    total = mul(upper, acts_ref[...], cols_cols) + mul(lower, acts_ref[...], cols_cols)
    total = total + mine[(chips - 1) * rows + g.r]
    for w in range(chips - 1):
        chip_copy(w).wait_recv()
        total = total + chip_in[w]
    out_ref[...] = total

    tokens.drain()
    for w in range(chips):
        def done(rp, carry):
            pair_copy(w, rp).wait_send()
            return carry

        lax.fori_loop(0, rows, done, 0)
        for s in range(stages):
            for j in range(g.count(s)):
                stage_copy(w, s, j).wait_send()
        if w < chips - 1:
            chip_copy(w).wait_send()


def power_scatter(accumulated, pair, grads, acts, rows, cols, collective_id):
    rank = pair.shape[0] // 2
    blk = acts.shape[0]
    chips = cols // 2
    blocks = chips * rows
    passed = chips * (rows - 1)
    return pl.pallas_call(
        functools.partial(power_kernel, rows, cols),
        out_shape=jax.ShapeDtypeStruct((rank, blk), f32),
        in_specs=[ANY, VMEM, VMEM, VMEM],
        out_specs=VMEM,
        scratch_shapes=[
            pltpu.VMEM((4, accumulated.shape[0], blk), f32),
            pltpu.VMEM((blocks, rank, blk), f32),
            pltpu.VMEM((blocks, rank, blk), f32),
            pltpu.VMEM((blocks, rank, blk), f32),
            pltpu.VMEM((passed, rank, blk), f32),
            pltpu.VMEM((chips - 1, rank, blk), f32),
            DMA((4,)),
            DMA((2, blocks)),
            DMA((2, passed)),
            DMA((2, chips - 1)),
            *AllReduce.scratch(rank, acts.shape[1], rows, chips),
        ],
        compiler_params=pltpu.CompilerParams(
            collective_id=collective_id, has_side_effects=True, vmem_limit_bytes=vmem_bytes
        ),
        name="power_scatter",
    )(accumulated, pair, grads, acts)


def solve_lower(gram_matrix, right):
    rank = gram_matrix.shape[0]
    step = 128 if rank % 128 == 0 else rank
    count = rank // step
    cut = lambda n: slice(n * step, (n + 1) * step)
    trailing = {
        (i, j): gram_matrix[cut(i), cut(j)] for i in range(count) for j in range(i + 1)
    }
    rests = [right[cut(i)] for i in range(count)]
    solved = []
    for j in range(count):
        factor = lax.linalg.cholesky(trailing[j, j], symmetrize_input=False)
        inverse = jax.scipy.linalg.solve_triangular(
            factor, jnp.eye(step, dtype=jnp.float32), lower=True
        )
        panel = {
            i: mul(trailing[i, j], inverse, cols_cols, highest) for i in range(j + 1, count)
        }
        solved.append(mul(inverse, rests[j], rows_cols, highest))
        for i in range(j + 1, count):
            rests[i] = rests[i] - mul(panel[i], solved[j], rows_cols, highest)
            for k in range(j + 1, i + 1):
                trailing[i, k] = trailing[i, k] - mul(panel[i], panel[k], cols_cols, highest)
    return jnp.concatenate(solved, axis=0)


def finish(moment_first, moment_second, projected, full_basis):
    first_next = beta_first * moment_first + (1.0 - beta_first) * projected
    second_next = beta_second * moment_second + (1.0 - beta_second) * projected * projected
    direction = (
        first_next / correct_first / (jnp.sqrt(second_next / correct_second) + epsilon_value)
    )
    lifted = lift_scale * mul(direction.astype(bf16), full_basis, cols_cols)
    return first_next, second_next, lifted


def plain_body(activations, out_grads, accumulated, seed_basis, moment_first, moment_second):
    share_rows = activations.shape[0]
    acts = activations.astype(jnp.float32)
    grads = out_grads.astype(jnp.float32)
    own_seed = lax.dynamic_slice_in_dim(
        seed_basis, lax.axis_index("col") * share_rows, share_rows, 0
    )
    full_seed = lax.all_gather(own_seed, every, axis=0, tiled=True)
    seed_tokens = lax.psum(mul(acts, own_seed, rows_rows, highest), every)
    image_rows = mul(accumulated, full_seed, rows_cols, high) + mul(
        grads, seed_tokens, rows_cols, high
    )
    image_tokens = lax.psum(mul(grads, image_rows, rows_rows, high), every)
    power_part = mul(accumulated, image_rows, rows_rows, high)
    power_rows = lax.psum_scatter(
        power_part, every, scatter_dimension=0, tiled=True
    ) + mul(acts, image_tokens, rows_cols, highest)
    gram_matrix = lax.psum(mul(power_rows, power_rows, rows_rows, highest), every)
    gram_matrix, held_acts = lax.optimization_barrier((gram_matrix, activations))
    full_acts = lax.all_gather(held_acts, every, axis=0, tiled=True)
    solved = solve_lower(gram_matrix, power_rows.T)
    basis_rows = solved.T.astype(jnp.bfloat16)
    sent_rows, full_acts = lax.optimization_barrier((basis_rows, full_acts))
    full_basis = lax.all_gather(sent_rows, every, axis=0, tiled=True)
    basis_tokens = mul(full_acts, full_basis, rows_rows)
    projected = mul(accumulated.astype(jnp.bfloat16), full_basis, rows_cols) + mul(
        grads, basis_tokens, rows_cols, high
    )
    return (basis_rows, *finish(moment_first, moment_second, projected, full_basis))


def body(rows, cols, activations, out_grads, accumulated, seed_basis, moment_first, moment_second):
    share_rows = activations.shape[0]
    reduce = functools.partial(all_reduce, rows=rows, cols=cols)
    grads = out_grads.astype(jnp.float32)
    own_seed = lax.dynamic_slice_in_dim(
        seed_basis, lax.axis_index("col") * share_rows, share_rows, 0
    )
    acts = activations.astype(jnp.float32)
    full_seed = lax.all_gather(own_seed, every, axis=0, tiled=True)
    seed_tokens = reduce(mul(own_seed, acts, rows_rows, highest), collective_id=1)
    image_turned = mul(full_seed, accumulated, ((0,), (1,)), high) + mul(
        seed_tokens, grads, cols_cols, high
    )
    upper = lax.reduce_precision(image_turned, 8, 7)
    pair = jnp.concatenate([upper, image_turned - upper], axis=0).astype(bf16)
    power_turned = power_scatter(accumulated, pair, out_grads, activations, rows, cols, 2)
    gram_matrix = reduce(mul(power_turned, power_turned, cols_cols, highest), collective_id=3)
    solved = solve_lower(gram_matrix, power_turned)
    basis_rows = solved.T.astype(jnp.bfloat16)
    full_basis = lax.all_gather(basis_rows, every, axis=0, tiled=True)
    basis_tokens = reduce(
        mul(basis_rows, activations, rows_rows), collective_id=4
    )
    projected = mul(accumulated.astype(jnp.bfloat16), full_basis, rows_cols) + mul(
        grads, basis_tokens, cols_cols, high
    )
    return (basis_rows, *finish(moment_first, moment_second, projected, full_basis))


def solution(mesh):
    rows, cols = mesh.shape["row"], mesh.shape["col"]

    def place(activations, *others):
        rank = others[2].shape[1]
        fits = rows & (rows - 1) == 0 and rows > 1 and cols % 2 == 0 and cols > 2
        fits = fits and activations.shape[0] % 128 == 0 and rank % (8 * rows * cols) == 0
        if fits:
            return body(rows, cols, activations, *others)
        return plain_body(activations, *others)

    split_rows = P(("row", "col"), None)
    in_specs = (split_rows, split_rows, split_rows, P("row", None), split_rows, split_rows)
    return jax.shard_map(
        place, mesh=mesh, in_specs=in_specs, out_specs=(split_rows,) * 4, check_vma=False
    )
```

```python
import functools

import jax
import jax.numpy as jnp
from jax import lax
from jax.experimental import pallas as pl
from jax.experimental.pallas import tpu as pltpu
from jax.sharding import PartitionSpec as P

beta_first = 0.9
beta_second = 0.99
correct_first = 1.0 - 0.9**10
correct_second = 1.0 - 0.99**10
epsilon_value = 1e-08
lift_scale = 8.0

every = ("row", "col")
highest = lax.Precision.HIGHEST
high = lax.Precision.HIGH
bf16 = jnp.bfloat16
f32 = jnp.float32
MESH = pl.DeviceIdType.MESH
ANY = pl.BlockSpec(memory_space=pl.ANY)
VMEM = pl.BlockSpec(memory_space=pltpu.VMEM)
DMA = pltpu.SemaphoreType.DMA
vmem_bytes = 63 * 2**20


def mul(left, right, dims, precision=None):
    return lax.dot_general(
        left, right, (dims, ((), ())), precision=precision, preferred_element_type=jnp.float32
    )


rows_cols = ((1,), (0,))
rows_rows = ((0,), (0,))
cols_cols = ((1,), (1,))


def split(value):
    upper = value.astype(bf16)
    return upper, (value - upper.astype(f32)).astype(bf16)


class Grid:
    def __init__(self, rows, cols):
        self.rows, self.chips = rows, cols // 2
        self.stages = rows.bit_length() - 1
        self.r = lax.axis_index("row")
        c = lax.axis_index("col")
        self.z, self.k = c // 2, c % 2
        self.c = c
        self.partner = (self.r, self.z * 2 + 1 - self.k)

    def flip(self, bit):
        return self.r + bit * (1 - 2 * ((self.r // bit) % 2))

    def peer_row(self, s):
        low, high_bit = 2**s, 2 ** (self.stages - 1 - s)
        return (1 - self.k) * self.flip(low) + self.k * self.flip(high_bit)

    def peer(self, s):
        return (self.peer_row(s), self.c)

    def count(self, s):
        return 2 ** (self.stages - 1 - s)

    def block(self, s, j, base):
        n = self.count(s)
        first = base % 2 ** (s + 1) + j * 2 ** (s + 1)
        second = (base // n) * n + j
        return (1 - self.k) * first + self.k * second

    def chip(self, w):
        n = self.chips
        return (self.z + 1 + w) % n, (self.z + n - 1 - w) % n

    def chip_device(self, z):
        return (self.r, z * 2 + self.k)

    def greet(self):
        barrier = pltpu.get_barrier_semaphore()
        peers = [self.partner]
        peers += [self.peer(s) for s in range(self.stages)]
        peers += [self.chip_device(self.chip(w)[0]) for w in range(self.chips - 1)]
        for peer in peers:
            pl.semaphore_signal(barrier, inc=1, device_id=peer, device_id_type=MESH)
        pl.semaphore_wait(barrier, len(peers))


def remote(source, target, send, recv, device):
    return pltpu.make_async_remote_copy(
        src_ref=source, dst_ref=target, send_sem=send, recv_sem=recv,
        device_id=device, device_id_type=MESH,
    )


class AllReduce:
    def __init__(self, grid, part, full, half_in, stage_in, chip_in, send, recv):
        self.g, self.part, self.full = grid, part, full
        self.half_in, self.stage_in, self.chip_in = half_in, stage_in, chip_in
        self.send, self.recv = send, recv
        self.half = part.shape[0] // 2
        self.chunk = self.half // grid.rows
        self.unit = self.chunk // grid.chips
        self.pending = []
        self.used = 0
        self.phases = (
            [self.pair_out]
            + [functools.partial(self.halve, s) for s in range(grid.stages)]
            + [self.chips_out, self.chips_back]
            + [functools.partial(self.double, s) for s in reversed(range(grid.stages))]
            + [self.pair_back, self.finish]
        )
        self.arrived = []

    @staticmethod
    def scratch(rows, width, grid_rows, chips):
        half = rows // 2
        chunk = half // grid_rows
        stages = grid_rows.bit_length() - 1
        copies = 2 + 2 * (grid_rows - 1) + 2 * (chips - 1)
        return [
            pltpu.VMEM((rows, width), f32),
            pltpu.VMEM((rows, width), f32),
            pltpu.VMEM((half, width), f32),
            pltpu.VMEM((grid_rows - 1, chunk, width), f32),
            pltpu.VMEM((chips - 1, chunk // chips, width), f32),
            DMA((copies,)),
            DMA((copies,)),
        ]

    def start(self, source, target, device):
        i = self.used
        self.used += 1
        copy = remote(source, target, self.send.at[i], self.recv.at[i], device)
        copy.start()
        self.pending.append(copy)
        self.arrived.append(copy)

    def landed(self):
        arrived, self.arrived = self.arrived, []
        for copy in arrived:
            copy.wait_recv()

    def rows_of(self, r):
        return pl.ds(pl.multiple_of((self.g.k * self.g.rows + r) * self.chunk, self.chunk), self.chunk)

    def unit_of(self, r, z):
        at = ((self.g.k * self.g.rows + r) * self.g.chips + z) * self.unit
        return pl.ds(pl.multiple_of(at, self.unit), self.unit)

    def pair_out(self):
        g = self.g
        other = pl.ds(pl.multiple_of((1 - g.k) * self.half, self.half), self.half)
        self.start(self.part.at[other], self.half_in, g.partner)

    def stage_base(self, s):
        return self.g.rows - 2 ** (self.g.stages - s)

    def halve(self, s):
        g = self.g
        self.landed()
        if s == 0:
            mine = pl.ds(pl.multiple_of(g.k * self.half, self.half), self.half)
            self.part[mine] += self.half_in[...]
        else:
            self.take(s - 1)
        for j in range(g.count(s)):
            rows = self.rows_of(g.block(s, j, g.peer_row(s)))
            self.start(self.part.at[rows], self.stage_in.at[self.stage_base(s) + j], g.peer(s))

    def take(self, s):
        g = self.g
        for j in range(g.count(s)):
            self.part[self.rows_of(g.block(s, j, g.r))] += self.stage_in[self.stage_base(s) + j]

    def chips_out(self):
        g = self.g
        self.landed()
        self.take(g.stages - 1)
        for w in range(g.chips - 1):
            z = g.chip(w)[0]
            self.start(self.part.at[self.unit_of(g.r, z)], self.chip_in.at[w], g.chip_device(z))

    def chips_back(self):
        g = self.g
        self.landed()
        own = self.unit_of(g.r, g.z)
        total = self.part[own]
        for w in range(g.chips - 1):
            total = total + self.chip_in[w]
        self.full[own] = total
        for w in range(g.chips - 1):
            self.start(self.full.at[own], self.full.at[own], g.chip_device(g.chip(w)[0]))

    def double(self, s):
        g = self.g
        self.landed()
        for j in range(g.count(s)):
            rows = self.rows_of(g.block(s, j, g.r))
            self.start(self.full.at[rows], self.full.at[rows], g.peer(s))

    def pair_back(self):
        g = self.g
        self.landed()
        mine = pl.ds(pl.multiple_of(g.k * self.half, self.half), self.half)
        self.start(self.full.at[mine], self.full.at[mine], g.partner)

    def finish(self):
        self.landed()

    def drain(self):
        for copy in self.pending:
            copy.wait_send()


def reduce_kernel(rows, cols, part_ref, out_ref, *scratch):
    grid = Grid(rows, cols)
    grid.greet()
    part, full, *rest = scratch
    part[...] = part_ref[...]
    total = AllReduce(grid, part, full, *rest)
    for phase in total.phases:
        phase()
    out_ref[...] = full[...]
    total.drain()


def all_reduce(value, rows, cols, collective_id):
    return pl.pallas_call(
        functools.partial(reduce_kernel, rows, cols),
        out_shape=jax.ShapeDtypeStruct(value.shape, f32),
        in_specs=[VMEM],
        out_specs=VMEM,
        scratch_shapes=AllReduce.scratch(*value.shape, rows, cols // 2),
        compiler_params=pltpu.CompilerParams(
            collective_id=collective_id, has_side_effects=True, vmem_limit_bytes=vmem_bytes
        ),
        name="all_reduce",
    )(value)


def power_kernel(
    rows, cols, acc, pair_ref, grads_ref, acts_ref, out_ref,
    tiles, mine, theirs, pair_in, stage_in, chip_in,
    tile_sem, pair_sems, stage_sems, chip_sems, *reduce_scratch,
):
    g = Grid(rows, cols)
    blk = acts_ref.shape[0]
    rank = out_ref.shape[0]
    chips, stages = g.chips, g.stages

    def chip_of(w):
        return g.chip(w)[0]

    def fetch(w, rp, kind):
        core = (1 - g.k) if kind == 0 else g.k
        at = ((rp * chips + (g.z + 1 + w) % chips) * 2 + core) * blk
        columns = pl.ds(pl.multiple_of(at, blk), blk)
        slot = (w * rows + rp) % 2
        return pltpu.make_async_copy(
            acc.at[:, columns], tiles.at[kind * 2 + slot], tile_sem.at[kind * 2 + slot]
        )

    for rp in range(2):
        fetch(0, rp, 0).start()
        fetch(0, rp, 1).start()
    g.greet()

    part, full, *rest = reduce_scratch
    part[...] = mul(pair_ref[:rank], grads_ref[...], rows_cols) + mul(
        pair_ref[rank:], grads_ref[...], rows_cols
    )
    tokens = AllReduce(g, part, full, *rest)
    phases = iter(tokens.phases)

    def tick():
        phase = next(phases, None)
        if phase is not None:
            phase()

    tick()

    def product(slot):
        upper, lower = split(tiles[slot])
        both = mul(pair_ref[...], upper, rows_cols)
        return both[:rank] + both[rank:] + mul(pair_ref[:rank], lower, rows_cols)

    def pair_copy(w, rp):
        i = w * rows + rp
        return remote(theirs.at[i], pair_in.at[i], pair_sems.at[0, i], pair_sems.at[1, i], g.partner)

    def stage_copy(w, s, j):
        i = w * (rows - 1) + rows - 2 ** (stages - s) + j
        source = mine.at[w * rows + g.block(s, j, g.peer_row(s))]
        return remote(source, stage_in.at[i], stage_sems.at[0, i], stage_sems.at[1, i], g.peer(s))

    def chip_copy(w):
        return remote(
            mine.at[w * rows + g.r], chip_in.at[w], chip_sems.at[0, w], chip_sems.at[1, w],
            g.chip_device(chip_of(w)),
        )

    def compute(w):
        def step(rp, carry):
            i = w * rows + rp
            slot = i % 2
            for kind, store in ((0, theirs), (1, mine)):
                fetch(w, rp, kind).wait()
                store[i] = product(kind * 2 + slot)
                if kind == 0:
                    pair_copy(w, rp).start()

                @pl.when(i + 2 < chips * rows)
                def _():
                    fetch((i + 2) // rows, (i + 2) % rows, kind).start()
            return carry

        lax.fori_loop(0, rows, step, 0)

    def add(index, value_ref, at):
        mine[index] += value_ref[at]

    def halve(w, s):
        if s == 0:
            for base, send in ((g.peer_row(0), True), (g.r, False)):
                for j in range(g.count(0)):
                    rp = g.block(0, j, base)
                    pair_copy(w, rp).wait_recv()
                    add(w * rows + rp, pair_in, w * rows + rp)
                    if send:
                        stage_copy(w, 0, j).start()
            return
        for j in range(g.count(s - 1)):
            i = w * (rows - 1) + rows - 2 ** (stages - s + 1) + j
            stage_copy(w, s - 1, j).wait_recv()
            add(w * rows + g.block(s - 1, j, g.r), stage_in, i)
        for j in range(g.count(s)):
            stage_copy(w, s, j).start()

    def leave(w):
        i = w * (rows - 1) + rows - 2
        stage_copy(w, stages - 1, 0).wait_recv()
        add(w * rows + g.r, stage_in, i)
        if w < chips - 1:
            chip_copy(w).start()

    for at in range(chips + stages + 1):
        if at < chips:
            compute(at)
        for later in range(1, stages + 1):
            w = at - later
            if 0 <= w < chips:
                tick()
                halve(w, later - 1)
        w = at - stages - 1
        if 0 <= w < chips:
            tick()
            leave(w)
    for phase in phases:
        phase()
    upper, lower = split(full[...])
    total = mul(upper, acts_ref[...], cols_cols) + mul(lower, acts_ref[...], cols_cols)
    total = total + mine[(chips - 1) * rows + g.r]
    for w in range(chips - 1):
        chip_copy(w).wait_recv()
        total = total + chip_in[w]
    out_ref[...] = total

    tokens.drain()
    for w in range(chips):
        def done(rp, carry):
            pair_copy(w, rp).wait_send()
            return carry

        lax.fori_loop(0, rows, done, 0)
        for s in range(stages):
            for j in range(g.count(s)):
                stage_copy(w, s, j).wait_send()
        if w < chips - 1:
            chip_copy(w).wait_send()


def power_scatter(accumulated, pair, grads, acts, rows, cols, collective_id):
    rank = pair.shape[0] // 2
    blk = acts.shape[0]
    chips = cols // 2
    blocks = chips * rows
    passed = chips * (rows - 1)
    return pl.pallas_call(
        functools.partial(power_kernel, rows, cols),
        out_shape=jax.ShapeDtypeStruct((rank, blk), f32),
        in_specs=[ANY, VMEM, VMEM, VMEM],
        out_specs=VMEM,
        scratch_shapes=[
            pltpu.VMEM((4, accumulated.shape[0], blk), f32),
            pltpu.VMEM((blocks, rank, blk), f32),
            pltpu.VMEM((blocks, rank, blk), f32),
            pltpu.VMEM((blocks, rank, blk), f32),
            pltpu.VMEM((passed, rank, blk), f32),
            pltpu.VMEM((chips - 1, rank, blk), f32),
            DMA((4,)),
            DMA((2, blocks)),
            DMA((2, passed)),
            DMA((2, chips - 1)),
            *AllReduce.scratch(rank, acts.shape[1], rows, chips),
        ],
        compiler_params=pltpu.CompilerParams(
            collective_id=collective_id, has_side_effects=True, vmem_limit_bytes=vmem_bytes
        ),
        name="power_scatter",
    )(accumulated, pair, grads, acts)


class Interleaved:
    def __init__(self, phases):
        self.left = list(phases)

    def tick(self, count=1):
        for _ in range(count):
            if self.left:
                self.left.pop(0)()

    def rest(self):
        self.tick(len(self.left))


def image_kernel(
    rows, cols, acc, seed_ref, grads_ref, acts_ref, out_ref,
    tiles, image, seeds, tile_sem, pair_sems, stage_sems, *reduce_scratch,
):
    g = Grid(rows, cols)
    stages = g.stages
    blk, rank = seeds.shape[2], seeds.shape[3]
    own_rows = seed_ref.shape[0]
    pieces = own_rows // (2 * blk)
    tokens_rows = acts_ref.shape[0]

    def piece(rp, h, i):
        return (rp * 2 + h) * pieces + i

    def fetch(p, slot):
        columns = pl.ds(pl.multiple_of(p * blk, blk), blk)
        return pltpu.make_async_copy(acc.at[:, columns], tiles.at[slot], tile_sem.at[slot])

    def order(t):
        u = t - 2 * pieces
        wave = u // (2 * (rows - 1))
        inner = u % (2 * (rows - 1))
        other = piece((g.r + 1 + inner // 2) % rows, inner % 2, wave)
        own = piece(g.r, t // pieces, t % pieces)
        return jnp.where(t < 2 * pieces, own, other)

    count = 2 * pieces * rows
    depth = tiles.shape[0]
    for t in range(depth - 1):
        fetch(order(t), t).start()
    g.greet()

    own = pl.ds(pl.multiple_of(g.c * tokens_rows, tokens_rows), tokens_rows)
    turned = seed_ref[own].T
    part, full, *rest = reduce_scratch
    upper, lower = split(turned)
    part[...] = mul(upper, acts_ref[...], rows_cols) + mul(lower, acts_ref[...], rows_cols)
    tokens = AllReduce(g, part, full, *rest)
    small = Interleaved(tokens.phases)
    small.tick()

    def spread(q, carry):
        at = pl.ds(pl.multiple_of(q * blk, blk), blk)
        upper, lower = split(seed_ref[at])
        target = g.r * 2 * pieces + q
        seeds[target, 0] = upper
        seeds[target, 1] = lower
        return carry

    lax.fori_loop(0, 2 * pieces, spread, 0)

    def pair_copy(rp, i):
        p = piece(rp, g.k, i)
        at = i * rows + rp
        return remote(seeds.at[p], seeds.at[p], pair_sems.at[0, at], pair_sems.at[1, at], g.partner)

    def pair_wait(rp, i):
        at = i * rows + rp
        p = piece(rp, 1 - g.k, i)
        remote(seeds.at[p], seeds.at[p], pair_sems.at[0, at], pair_sems.at[1, at], g.partner).wait_recv()

    def stage_copy(i, s, j, base):
        at = i * (rows - 1) + rows - 2 ** (stages - s) + j
        p = piece(g.block(s, j, base), g.k, i)
        return remote(seeds.at[p], seeds.at[p], stage_sems.at[0, at], stage_sems.at[1, at], g.peer(s))

    def send(i, s):
        for j in range(g.count(s)):
            stage_copy(i, s, j, g.r).start()

    def land(i, s):
        for j in range(g.count(s)):
            stage_copy(i, s, j, g.peer_row(s)).wait_recv()
            pair_copy(g.block(s, j, g.peer_row(s)), i).start()

    def compute(t):
        slot = t % depth
        p = order(t)
        fetch(p, slot).wait()

        @pl.when(t + depth - 1 < count)
        def _():
            fetch(order(t + depth - 1), (t + depth - 1) % depth).start()

        upper, lower = split(tiles[slot])
        image[...] += (
            mul(upper, seeds[p, 0], rows_cols)
            + mul(lower, seeds[p, 0], rows_cols)
            + mul(upper, seeds[p, 1], rows_cols)
        )

    def own_step(t, carry):
        compute(t)
        return carry

    def other_step(t, carry):
        inner = (t - 2 * pieces) % (2 * (rows - 1))
        wave = (t - 2 * pieces) // (2 * (rows - 1))
        rp = (g.r + 1 + inner // 2) % rows

        @pl.when(inner % 2 == 1 - g.k)
        def _():
            pair_wait(rp, wave)

        compute(t)
        return carry

    image[...] = jnp.zeros_like(image)
    for i in range(pieces):
        send(i, stages - 1)
    first = 2 * pieces // (stages + 1)
    done = 0
    lag = stages
    for at in range(pieces + lag):
        small.tick(2)
        for late in range(stages):
            i = at - late
            if 0 <= i < pieces:
                s = stages - 1 - late
                land(i, s)
                if s > 0:
                    send(i, s - 1)
        if done < 2 * pieces:
            stop = min(2 * pieces, done + first)
            lax.fori_loop(done, stop, own_step, 0)
            done = stop
        i = at - lag
        if 0 <= i < pieces:
            lax.fori_loop(done, 2 * pieces, own_step, 0)
            done = 2 * pieces
            start = 2 * pieces + i * 2 * (rows - 1)
            lax.fori_loop(start, start + 2 * (rows - 1), other_step, 0)
    small.rest()
    upper, lower = split(full[...])
    total = image[...] + mul(grads_ref[...], upper, cols_cols) + mul(grads_ref[...], lower, cols_cols)
    upper, lower = split(total.T)
    out_ref[:rank] = upper
    out_ref[rank:] = lower

    tokens.drain()
    for i in range(pieces):
        for s in range(stages):
            for j in range(g.count(s)):
                stage_copy(i, s, j, g.r).wait_send()
                pair_copy(g.block(s, j, g.peer_row(s)), i).wait_send()


def image_pair(accumulated, seed, grads, acts, rows, cols, collective_id):
    rank = seed.shape[1]
    height, width = accumulated.shape
    blk = 256 if seed.shape[0] % 512 == 0 else seed.shape[0] // 2
    total = width // blk
    pieces = total // (2 * rows)
    return pl.pallas_call(
        functools.partial(image_kernel, rows, cols),
        out_shape=jax.ShapeDtypeStruct((2 * rank, height), bf16),
        in_specs=[ANY, VMEM, VMEM, VMEM],
        out_specs=VMEM,
        scratch_shapes=[
            pltpu.VMEM((4, height, blk), f32),
            pltpu.VMEM((height, rank), f32),
            pltpu.VMEM((total, 2, blk, rank), bf16),
            DMA((4,)),
            DMA((2, pieces * rows)),
            DMA((2, pieces * (rows - 1))),
            *AllReduce.scratch(rank, acts.shape[1], rows, cols // 2),
        ],
        compiler_params=pltpu.CompilerParams(
            collective_id=collective_id, has_side_effects=True, vmem_limit_bytes=vmem_bytes
        ),
        name="image_pair",
    )(accumulated, seed, grads, acts)


def project_kernel(
    rows, cols, acc, basis_ref, turned_ref, grads_ref, acts_ref, out_ref, full_ref,
    tiles, tile_sem, pair_sems, stage_sems, chip_sems, *reduce_scratch,
):
    g = Grid(rows, cols)
    chips, stages = g.chips, g.stages
    blk = basis_ref.shape[0]
    count = chips * rows

    def chip_of(w):
        return (g.z + chips - w) % chips

    def at_of(rp, w, core):
        at = ((rp * chips + chip_of(w)) * 2 + core) * blk
        return full_ref.at[pl.ds(pl.multiple_of(at, blk), blk)]

    def fetch(t):
        w, rp = t // rows, t % rows
        at = (rp * chips + chip_of(w)) * 2 * blk
        columns = pl.ds(pl.multiple_of(at, 2 * blk), 2 * blk)
        return pltpu.make_async_copy(acc.at[:, columns], tiles.at[t % 2], tile_sem.at[t % 2])

    fetch(0).start()
    fetch(1).start()
    g.greet()
    own_rows = pl.ds(pl.multiple_of(((g.r * chips + g.z) * 2 + g.k) * blk, blk), blk)
    full_ref[own_rows] = basis_ref[...]

    def pair_copy(rp, w):
        i = w * rows + rp
        ref = at_of(rp, w, g.k)
        return remote(ref, ref, pair_sems.at[0, i], pair_sems.at[1, i], g.partner)

    def pair_wait(rp, w):
        i = w * rows + rp
        ref = at_of(rp, w, 1 - g.k)
        remote(ref, ref, pair_sems.at[0, i], pair_sems.at[1, i], g.partner).wait_recv()

    def stage_copy(w, s, j, base):
        i = w * (rows - 1) + rows - 2 ** (stages - s) + j
        ref = at_of(g.block(s, j, base), w, g.k)
        return remote(ref, ref, stage_sems.at[0, i], stage_sems.at[1, i], g.peer(s))

    def chip_copy(w, z):
        at = ((g.r * chips + z) * 2 + g.k) * blk
        ref = full_ref.at[pl.ds(pl.multiple_of(at, blk), blk)]
        return remote(
            ref, ref, chip_sems.at[0, w], chip_sems.at[1, w], g.chip_device(g.chip(w)[0])
        )

    def enter(w):
        if w > 0:
            chip_copy(w - 1, chip_of(w)).wait_recv()
        stage_copy(w, stages - 1, 0, g.r).start()
        pair_copy(g.r, w).start()

    def land(w, s):
        for j in range(g.count(s)):
            stage_copy(w, s, j, g.peer_row(s)).wait_recv()
        if s > 0:
            for j in range(g.count(s - 1)):
                stage_copy(w, s - 1, j, g.r).start()
        for j in range(g.count(s)):
            pair_copy(g.block(s, j, g.peer_row(s)), w).start()

    for w in range(chips - 1):
        chip_copy(w, g.z).start()
    part, full, *rest = reduce_scratch
    enter(0)
    part[...] = mul(turned_ref[...], acts_ref[...], rows_cols)
    tokens = AllReduce(g, part, full, *rest)
    small = Interleaved(tokens.phases)
    small.tick()
    out_ref[...] = jnp.zeros_like(out_ref)

    def step(t, carry):
        w, rp = t // rows, t % rows
        fetch(t).wait()
        pair_wait(rp, w)
        at = (rp * chips + chip_of(w)) * 2 * blk
        block = full_ref[pl.ds(pl.multiple_of(at, 2 * blk), 2 * blk)]
        out_ref[...] += mul(tiles[t % 2].astype(bf16), block, rows_cols)

        @pl.when(t + 2 < count)
        def _():
            fetch(t + 2).start()

        return carry

    for at in range(chips + stages + 1):
        small.tick()
        for late in range(stages + 1):
            w = at - late
            if 0 <= w < chips:
                if late == 0:
                    if w > 0:
                        enter(w)
                else:
                    land(w, stages - late)
        w = at - stages
        if 0 <= w < chips:
            lax.fori_loop(w * rows, (w + 1) * rows, step, 0)
    small.rest()
    upper, lower = split(full[...])
    out_ref[...] += mul(grads_ref[...], upper, cols_cols) + mul(grads_ref[...], lower, cols_cols)

    tokens.drain()
    for w in range(chips - 1):
        chip_copy(w, g.z).wait_send()
    for w in range(chips):
        pair_copy(g.r, w).wait_send()
        for s in range(stages):
            for j in range(g.count(s)):
                stage_copy(w, s, j, g.r).wait_send()
                pair_copy(g.block(s, j, g.peer_row(s)), w).wait_send()


def project(accumulated, basis, turned, grads, acts, rows, cols, collective_id):
    height, width = accumulated.shape
    blk, rank = basis.shape
    chips = cols // 2
    return pl.pallas_call(
        functools.partial(project_kernel, rows, cols),
        out_shape=(
            jax.ShapeDtypeStruct((height, rank), f32),
            jax.ShapeDtypeStruct((width, rank), bf16),
        ),
        in_specs=[ANY, VMEM, VMEM, VMEM, VMEM],
        out_specs=(VMEM, VMEM),
        scratch_shapes=[
            pltpu.VMEM((2, height, 2 * blk), f32),
            DMA((2,)),
            DMA((2, chips * rows)),
            DMA((2, chips * (rows - 1))),
            DMA((2, chips - 1)),
            *AllReduce.scratch(rank, acts.shape[1], rows, chips),
        ],
        compiler_params=pltpu.CompilerParams(
            collective_id=collective_id, has_side_effects=True, vmem_limit_bytes=vmem_bytes
        ),
        name="project",
    )(accumulated, basis, turned, grads, acts)


def solve_lower(gram_matrix, right):
    rank = gram_matrix.shape[0]
    step = 128 if rank % 128 == 0 else rank
    count = rank // step
    cut = lambda n: slice(n * step, (n + 1) * step)
    trailing = {
        (i, j): gram_matrix[cut(i), cut(j)] for i in range(count) for j in range(i + 1)
    }
    rests = [right[cut(i)] for i in range(count)]
    solved = []
    for j in range(count):
        factor = lax.linalg.cholesky(trailing[j, j], symmetrize_input=False)
        inverse = jax.scipy.linalg.solve_triangular(
            factor, jnp.eye(step, dtype=jnp.float32), lower=True
        )
        panel = {
            i: mul(trailing[i, j], inverse, cols_cols, highest) for i in range(j + 1, count)
        }
        solved.append(mul(inverse, rests[j], rows_cols, highest))
        for i in range(j + 1, count):
            rests[i] = rests[i] - mul(panel[i], solved[j], rows_cols, highest)
            for k in range(j + 1, i + 1):
                trailing[i, k] = trailing[i, k] - mul(panel[i], panel[k], cols_cols, highest)
    return jnp.concatenate(solved, axis=0)


def finish(moment_first, moment_second, projected, full_basis):
    first_next = beta_first * moment_first + (1.0 - beta_first) * projected
    second_next = beta_second * moment_second + (1.0 - beta_second) * projected * projected
    direction = (
        first_next / correct_first / (jnp.sqrt(second_next / correct_second) + epsilon_value)
    )
    lifted = lift_scale * mul(direction.astype(bf16), full_basis, cols_cols)
    return first_next, second_next, lifted


def plain_body(activations, out_grads, accumulated, seed_basis, moment_first, moment_second):
    share_rows = activations.shape[0]
    acts = activations.astype(jnp.float32)
    grads = out_grads.astype(jnp.float32)
    own_seed = lax.dynamic_slice_in_dim(
        seed_basis, lax.axis_index("col") * share_rows, share_rows, 0
    )
    full_seed = lax.all_gather(own_seed, every, axis=0, tiled=True)
    seed_tokens = lax.psum(mul(acts, own_seed, rows_rows, highest), every)
    image_rows = mul(accumulated, full_seed, rows_cols, high) + mul(
        grads, seed_tokens, rows_cols, high
    )
    image_tokens = lax.psum(mul(grads, image_rows, rows_rows, high), every)
    power_part = mul(accumulated, image_rows, rows_rows, high)
    power_rows = lax.psum_scatter(
        power_part, every, scatter_dimension=0, tiled=True
    ) + mul(acts, image_tokens, rows_cols, highest)
    gram_matrix = lax.psum(mul(power_rows, power_rows, rows_rows, highest), every)
    gram_matrix, held_acts = lax.optimization_barrier((gram_matrix, activations))
    full_acts = lax.all_gather(held_acts, every, axis=0, tiled=True)
    solved = solve_lower(gram_matrix, power_rows.T)
    basis_rows = solved.T.astype(jnp.bfloat16)
    sent_rows, full_acts = lax.optimization_barrier((basis_rows, full_acts))
    full_basis = lax.all_gather(sent_rows, every, axis=0, tiled=True)
    basis_tokens = mul(full_acts, full_basis, rows_rows)
    projected = mul(accumulated.astype(jnp.bfloat16), full_basis, rows_cols) + mul(
        grads, basis_tokens, rows_cols, high
    )
    return (basis_rows, *finish(moment_first, moment_second, projected, full_basis))


def body(rows, cols, activations, out_grads, accumulated, seed_basis, moment_first, moment_second):
    common = (out_grads, activations, rows, cols)
    pair = image_pair(accumulated, seed_basis, *common, 1)
    power_turned = power_scatter(accumulated, pair, *common, 2)
    gram_matrix = all_reduce(
        mul(power_turned, power_turned, cols_cols, highest), rows, cols, 3
    )
    turned = solve_lower(gram_matrix, power_turned).astype(bf16)
    basis_rows = turned.T
    projected, full_basis = project(accumulated, basis_rows, turned, *common, 4)
    return (basis_rows, *finish(moment_first, moment_second, projected, full_basis))


def solution(mesh):
    rows, cols = mesh.shape["row"], mesh.shape["col"]

    def place(activations, *others):
        rank = others[2].shape[1]
        fits = rows & (rows - 1) == 0 and rows > 1 and cols % 2 == 0 and cols > 2
        fits = fits and activations.shape[0] % 128 == 0 and rank % (8 * rows * cols) == 0
        if fits:
            return body(rows, cols, activations, *others)
        return plain_body(activations, *others)

    split_rows = P(("row", "col"), None)
    in_specs = (split_rows, split_rows, split_rows, P("row", None), split_rows, split_rows)
    return jax.shard_map(
        place, mesh=mesh, in_specs=in_specs, out_specs=(split_rows,) * 4, check_vma=False
    )
```

```python
import functools

import jax
import jax.numpy as jnp
from jax import lax
from jax.experimental import pallas as pl
from jax.experimental.pallas import tpu as pltpu
from jax.sharding import PartitionSpec as P

beta_first = 0.9
beta_second = 0.99
correct_first = 1.0 - 0.9**10
correct_second = 1.0 - 0.99**10
epsilon_value = 1e-08
lift_scale = 8.0

every = ("row", "col")
highest = lax.Precision.HIGHEST
high = lax.Precision.HIGH
bf16 = jnp.bfloat16
f32 = jnp.float32
MESH = pl.DeviceIdType.MESH
ANY = pl.BlockSpec(memory_space=pl.ANY)
VMEM = pl.BlockSpec(memory_space=pltpu.VMEM)
DMA = pltpu.SemaphoreType.DMA
vmem_bytes = 63 * 2**20
image_ticks = (1, 0, 2, 2, 1, 1)
power_lag, power_gap, power_ticks = 7, 4, (1, 3, 5, 7, 9, 11, 13, 15, 16)


def mul(left, right, dims, precision=None):
    return lax.dot_general(
        left, right, (dims, ((), ())), precision=precision, preferred_element_type=jnp.float32
    )


rows_cols = ((1,), (0,))
rows_rows = ((0,), (0,))
cols_cols = ((1,), (1,))


def split(value):
    upper = value.astype(bf16)
    return upper, (value - upper.astype(f32)).astype(bf16)


class Grid:
    def __init__(self, rows, cols):
        self.rows, self.chips = rows, cols // 2
        self.stages = rows.bit_length() - 1
        self.r = lax.axis_index("row")
        c = lax.axis_index("col")
        self.z, self.k = c // 2, c % 2
        self.c = c
        self.partner = (self.r, self.z * 2 + 1 - self.k)
        n = self.chips
        self.offsets = sorted(range(1, n), key=lambda d: -min(d, n - d))

    def flip(self, bit):
        return self.r + bit * (1 - 2 * ((self.r // bit) % 2))

    def peer_row(self, s, k=None):
        k = self.k if k is None else k
        low, high_bit = 2**s, 2 ** (self.stages - 1 - s)
        return (1 - k) * self.flip(low) + k * self.flip(high_bit)

    def peer(self, s):
        return (self.peer_row(s), self.c)

    def count(self, s):
        return 2 ** (self.stages - 1 - s)

    def block(self, s, j, base, k=None):
        k = self.k if k is None else k
        n = self.count(s)
        first = base % 2 ** (s + 1) + j * 2 ** (s + 1)
        second = (base // n) * n + j
        return (1 - k) * first + k * second

    def chip(self, w, far_first=False):
        n, step = self.chips, self.offsets[w] if far_first else w + 1
        return (self.z + step) % n, (self.z + n - step) % n

    def chip_device(self, z):
        return (self.r, z * 2 + self.k)

    def greet(self):
        barrier = pltpu.get_barrier_semaphore()
        peers = [self.partner]
        peers += [self.peer(s) for s in range(self.stages)]
        peers += [self.chip_device(self.chip(w)[0]) for w in range(self.chips - 1)]
        for peer in peers:
            pl.semaphore_signal(barrier, inc=1, device_id=peer, device_id_type=MESH)
        pl.semaphore_wait(barrier, len(peers))


def remote(source, target, send, recv, device):
    return pltpu.make_async_remote_copy(
        src_ref=source, dst_ref=target, send_sem=send, recv_sem=recv,
        device_id=device, device_id_type=MESH,
    )


class AllReduce:
    def __init__(self, grid, part, full, half_in, stage_in, chip_in, send, recv):
        self.g, self.part, self.full = grid, part, full
        self.half_in, self.stage_in, self.chip_in = half_in, stage_in, chip_in
        self.send, self.recv = send, recv
        self.half = part.shape[0] // 2
        self.chunk = self.half // grid.rows
        self.unit = self.chunk // grid.chips
        self.pending = []
        self.used = 0
        self.phases = (
            [self.pair_out]
            + [functools.partial(self.halve, s) for s in range(grid.stages)]
            + [self.chips_out, self.chips_back]
            + [functools.partial(self.double, s) for s in reversed(range(grid.stages))]
            + [self.pair_back, self.finish]
        )
        self.arrived = []

    @staticmethod
    def scratch(rows, width, grid_rows, chips):
        half = rows // 2
        chunk = half // grid_rows
        stages = grid_rows.bit_length() - 1
        copies = 2 + 2 * (grid_rows - 1) + 2 * (chips - 1)
        return [
            pltpu.VMEM((rows, width), f32),
            pltpu.VMEM((rows, width), f32),
            pltpu.VMEM((half, width), f32),
            pltpu.VMEM((grid_rows - 1, chunk, width), f32),
            pltpu.VMEM((chips - 1, chunk // chips, width), f32),
            DMA((copies,)),
            DMA((copies,)),
        ]

    def start(self, source, target, device):
        i = self.used
        self.used += 1
        copy = remote(source, target, self.send.at[i], self.recv.at[i], device)
        copy.start()
        self.pending.append(copy)
        self.arrived.append(copy)

    def landed(self):
        arrived, self.arrived = self.arrived, []
        for copy in arrived:
            copy.wait_recv()

    def rows_of(self, r):
        return pl.ds(pl.multiple_of((self.g.k * self.g.rows + r) * self.chunk, self.chunk), self.chunk)

    def unit_of(self, r, z):
        at = ((self.g.k * self.g.rows + r) * self.g.chips + z) * self.unit
        return pl.ds(pl.multiple_of(at, self.unit), self.unit)

    def pair_out(self):
        g = self.g
        other = pl.ds(pl.multiple_of((1 - g.k) * self.half, self.half), self.half)
        self.start(self.part.at[other], self.half_in, g.partner)

    def stage_base(self, s):
        return self.g.rows - 2 ** (self.g.stages - s)

    def halve(self, s):
        g = self.g
        self.landed()
        if s == 0:
            mine = pl.ds(pl.multiple_of(g.k * self.half, self.half), self.half)
            self.part[mine] += self.half_in[...]
        else:
            self.take(s - 1)
        for j in range(g.count(s)):
            rows = self.rows_of(g.block(s, j, g.peer_row(s)))
            self.start(self.part.at[rows], self.stage_in.at[self.stage_base(s) + j], g.peer(s))

    def take(self, s):
        g = self.g
        for j in range(g.count(s)):
            self.part[self.rows_of(g.block(s, j, g.r))] += self.stage_in[self.stage_base(s) + j]

    def chips_out(self):
        g = self.g
        self.landed()
        self.take(g.stages - 1)
        for w in range(g.chips - 1):
            z = g.chip(w)[0]
            self.start(self.part.at[self.unit_of(g.r, z)], self.chip_in.at[w], g.chip_device(z))

    def chips_back(self):
        g = self.g
        self.landed()
        own = self.unit_of(g.r, g.z)
        total = self.part[own]
        for w in range(g.chips - 1):
            total = total + self.chip_in[w]
        self.full[own] = total
        for w in range(g.chips - 1):
            self.start(self.full.at[own], self.full.at[own], g.chip_device(g.chip(w)[0]))

    def double(self, s):
        g = self.g
        self.landed()
        for j in range(g.count(s)):
            rows = self.rows_of(g.block(s, j, g.r))
            self.start(self.full.at[rows], self.full.at[rows], g.peer(s))

    def pair_back(self):
        g = self.g
        self.landed()
        mine = pl.ds(pl.multiple_of(g.k * self.half, self.half), self.half)
        self.start(self.full.at[mine], self.full.at[mine], g.partner)

    def finish(self):
        self.landed()

    def drain(self):
        for copy in self.pending:
            copy.wait_send()


class ChipsFirst(AllReduce):
    def __init__(self, grid, *refs):
        super().__init__(grid, *refs)
        self.chunk = self.half // grid.chips
        self.unit = self.chunk // grid.rows
        self.phases = (
            [self.pair_out, self.chips_out]
            + [functools.partial(self.halve, s) for s in range(grid.stages)]
            + [functools.partial(self.double, s) for s in reversed(range(grid.stages))]
            + [self.chips_back, self.pair_back, self.finish]
        )

    @staticmethod
    def scratch(rows, width, grid_rows, chips):
        shapes = AllReduce.scratch(rows, width, grid_rows, chips)
        half = rows // 2
        unit = half // (chips * grid_rows)
        shapes[3] = pltpu.VMEM((grid_rows - 1, unit, width), f32)
        shapes[4] = pltpu.VMEM((chips - 1, half // chips, width), f32)
        return shapes

    def rows_of(self, r):
        at = ((self.g.k * self.g.chips + self.g.z) * self.g.rows + r) * self.unit
        return pl.ds(pl.multiple_of(at, self.unit), self.unit)

    def chunk_of(self, z):
        at = (self.g.k * self.g.chips + z) * self.chunk
        return pl.ds(pl.multiple_of(at, self.chunk), self.chunk)

    def chips_out(self):
        g = self.g
        self.landed()
        mine = pl.ds(pl.multiple_of(g.k * self.half, self.half), self.half)
        self.part[mine] += self.half_in[...]
        for w in range(g.chips - 1):
            z = g.chip(w)[0]
            self.start(self.part.at[self.chunk_of(z)], self.chip_in.at[w], g.chip_device(z))

    def halve(self, s):
        g = self.g
        self.landed()
        if s == 0:
            own = self.chunk_of(g.z)
            total = self.part[own]
            for w in range(g.chips - 1):
                total = total + self.chip_in[w]
            self.part[own] = total
        else:
            self.take(s - 1)
        for j in range(g.count(s)):
            rows = self.rows_of(g.block(s, j, g.peer_row(s)))
            self.start(self.part.at[rows], self.stage_in.at[self.stage_base(s) + j], g.peer(s))

    def double(self, s):
        g = self.g
        if s == g.stages - 1:
            self.landed()
            self.take(s)
            self.full[self.rows_of(g.r)] = self.part[self.rows_of(g.r)]
        super().double(s)

    def chips_back(self):
        g = self.g
        self.landed()
        own = self.chunk_of(g.z)
        for w in range(g.chips - 1):
            self.start(self.full.at[own], self.full.at[own], g.chip_device(g.chip(w)[0]))


def reduce_kernel(rows, cols, part_ref, out_ref, *scratch):
    grid = Grid(rows, cols)
    grid.greet()
    part, full, *rest = scratch
    part[...] = part_ref[...]
    total = AllReduce(grid, part, full, *rest)
    for phase in total.phases:
        phase()
    out_ref[...] = full[...]
    total.drain()


def all_reduce(value, rows, cols, collective_id):
    return pl.pallas_call(
        functools.partial(reduce_kernel, rows, cols),
        out_shape=jax.ShapeDtypeStruct(value.shape, f32),
        in_specs=[VMEM],
        out_specs=VMEM,
        scratch_shapes=AllReduce.scratch(*value.shape, rows, cols // 2),
        compiler_params=pltpu.CompilerParams(
            collective_id=collective_id, has_side_effects=True, vmem_limit_bytes=vmem_bytes
        ),
        name="all_reduce",
    )(value)


def power_kernel(
    rows, cols, acc, pair_ref, grads_ref, acts_ref, out_ref,
    tiles, mine, theirs, pair_in, stage_in, chip_in,
    tile_sem, pair_sems, stage_sems, chip_sems, *reduce_scratch,
):
    g = Grid(rows, cols)
    blk = acts_ref.shape[0]
    rank = out_ref.shape[0]
    chips, stages = g.chips, g.stages

    half = g.count(0)

    def chip_of(w):
        return g.chip(w, True)[0] if w < chips - 1 else g.z

    def block_of(t, kind=1):
        w, i = t // rows, t % rows
        core = (1 - g.k) if kind == 0 else g.k
        return w, g.block(0, i % half, g.peer_row(0, core) if i < half else g.r, core)

    def fetch(t, kind):
        w, rp = block_of(t, kind)
        core = (1 - g.k) if kind == 0 else g.k
        at = ((rp * chips + chip_of(w)) * 2 + core) * blk
        columns = pl.ds(pl.multiple_of(at, blk), blk)
        slot = kind * 2 + t % 2
        return pltpu.make_async_copy(acc.at[:, columns], tiles.at[slot], tile_sem.at[slot])

    for t in range(2):
        fetch(t, 0).start()
        fetch(t, 1).start()
    g.greet()

    part, full, *rest = reduce_scratch
    part[...] = mul(pair_ref[:rank], grads_ref[...], rows_cols) + mul(
        pair_ref[rank:], grads_ref[...], rows_cols
    )
    tokens = AllReduce(g, part, full, *rest)
    phases = iter(tokens.phases)

    def tick():
        phase = next(phases, None)
        if phase is not None:
            phase()

    tick()

    def product(slot):
        upper, lower = split(tiles[slot])
        both = mul(pair_ref[...], upper, rows_cols)
        return both[:rank] + both[rank:] + mul(pair_ref[:rank], lower, rows_cols)

    def pair_copy(w, rp):
        i = w * rows + rp
        return remote(theirs.at[i], pair_in.at[i], pair_sems.at[0, i], pair_sems.at[1, i], g.partner)

    def stage_copy(w, s, j):
        i = w * (rows - 1) + rows - 2 ** (stages - s) + j
        source = mine.at[w * rows + g.block(s, j, g.peer_row(s))]
        return remote(source, stage_in.at[i], stage_sems.at[0, i], stage_sems.at[1, i], g.peer(s))

    def chip_copy(w):
        return remote(
            mine.at[w * rows + g.r], chip_in.at[w], chip_sems.at[0, w], chip_sems.at[1, w],
            g.chip_device(chip_of(w)),
        )

    def compute(t):
        for kind, store in ((0, theirs), (1, mine)):
            w, rp = block_of(t, kind)
            fetch(t, kind).wait()
            store[w * rows + rp] = product(kind * 2 + t % 2)
            if kind == 0:
                pair_copy(w, rp).start()
            if t + 2 < chips * rows:
                fetch(t + 2, kind).start()

    def pair(t):
        w, rp = block_of(t)
        pair_copy(w, rp).wait_recv()
        mine[w * rows + rp] += pair_in[w * rows + rp]
        if t % rows < half:
            stage_copy(w, 0, t % rows).start()

    def halve(w, s):
        for j in range(g.count(s - 1)):
            i = w * (rows - 1) + rows - 2 ** (stages - s + 1) + j
            stage_copy(w, s - 1, j).wait_recv()
            mine[w * rows + g.block(s - 1, j, g.r)] += stage_in[i]
        for j in range(g.count(s)):
            stage_copy(w, s, j).start()

    def leave(w):
        i = w * (rows - 1) + rows - 2
        stage_copy(w, stages - 1, 0).wait_recv()
        mine[w * rows + g.r] += stage_in[i]
        if w < chips - 1:
            chip_copy(w).start()

    steps = chips * rows
    lag, gap, ticks = power_lag, power_gap, power_ticks
    later = {}
    for w in range(chips):
        for s in range(1, stages):
            later.setdefault(min(lag + gap * w + 3 * (s - 1), steps + 2 * w + s), []).append(
                functools.partial(halve, w, s)
            )
    for w in range(chips):
        later.setdefault(min(lag + gap * w + gap, steps + 2 * w + 3), []).append(
            functools.partial(leave, w)
        )
    for t in range(max(max(later), steps) + 1):
        if t in ticks:
            tick()
        if t < steps:
            compute(t)
        if 0 < t <= steps:
            pair(t - 1)
        for event in later.get(t, ()):
            event()
    for phase in phases:
        phase()
    upper, lower = split(full[...])
    total = mul(upper, acts_ref[...], cols_cols) + mul(lower, acts_ref[...], cols_cols)
    total = total + mine[(chips - 1) * rows + g.r]
    for w in range(chips - 1):
        chip_copy(w).wait_recv()
        total = total + chip_in[w]
    out_ref[...] = total

    tokens.drain()
    for w in range(chips):
        def done(rp, carry):
            pair_copy(w, rp).wait_send()
            return carry

        lax.fori_loop(0, rows, done, 0)
        for s in range(stages):
            for j in range(g.count(s)):
                stage_copy(w, s, j).wait_send()
        if w < chips - 1:
            chip_copy(w).wait_send()


def power_scatter(accumulated, pair, grads, acts, rows, cols, collective_id):
    rank = pair.shape[0] // 2
    blk = acts.shape[0]
    chips = cols // 2
    blocks = chips * rows
    passed = chips * (rows - 1)
    return pl.pallas_call(
        functools.partial(power_kernel, rows, cols),
        out_shape=jax.ShapeDtypeStruct((rank, blk), f32),
        in_specs=[ANY, VMEM, VMEM, VMEM],
        out_specs=VMEM,
        scratch_shapes=[
            pltpu.VMEM((4, accumulated.shape[0], blk), f32),
            pltpu.VMEM((blocks, rank, blk), f32),
            pltpu.VMEM((blocks, rank, blk), f32),
            pltpu.VMEM((blocks, rank, blk), f32),
            pltpu.VMEM((passed, rank, blk), f32),
            pltpu.VMEM((chips - 1, rank, blk), f32),
            DMA((4,)),
            DMA((2, blocks)),
            DMA((2, passed)),
            DMA((2, chips - 1)),
            *AllReduce.scratch(rank, acts.shape[1], rows, chips),
        ],
        compiler_params=pltpu.CompilerParams(
            collective_id=collective_id, has_side_effects=True, vmem_limit_bytes=vmem_bytes
        ),
        name="power_scatter",
    )(accumulated, pair, grads, acts)


class Interleaved:
    def __init__(self, phases):
        self.left = list(phases)

    def tick(self, count=1):
        for _ in range(count):
            if self.left:
                self.left.pop(0)()

    def rest(self):
        self.tick(len(self.left))


def image_kernel(
    rows, cols, acc, seed_ref, grads_ref, acts_ref, out_ref,
    tiles, image, seeds, tile_sem, pair_sems, stage_sems, *reduce_scratch,
):
    g = Grid(rows, cols)
    stages = g.stages
    blk, rank = seeds.shape[2], seeds.shape[3]
    own_rows = seed_ref.shape[0]
    pieces = own_rows // (2 * blk)
    tokens_rows = acts_ref.shape[0]

    def piece(rp, h, i):
        return (rp * 2 + h) * pieces + i

    def fetch(p, slot):
        columns = pl.ds(pl.multiple_of(p * blk, blk), blk)
        return pltpu.make_async_copy(acc.at[:, columns], tiles.at[slot], tile_sem.at[slot])

    def order(t):
        u = t - 2 * pieces
        wave = u // (2 * (rows - 1))
        inner = u % (2 * (rows - 1))
        other = piece((g.r + 1 + inner // 2) % rows, inner % 2, wave)
        own = piece(g.r, t // pieces, t % pieces)
        return jnp.where(t < 2 * pieces, own, other)

    count = 2 * pieces * rows
    depth = tiles.shape[0]
    for t in range(depth - 1):
        fetch(order(t), t).start()
    g.greet()

    own = pl.ds(pl.multiple_of(g.c * tokens_rows, tokens_rows), tokens_rows)
    turned = seed_ref[own].T
    part, full, *rest = reduce_scratch
    upper, lower = split(turned)
    part[...] = mul(upper, acts_ref[...], rows_cols) + mul(lower, acts_ref[...], rows_cols)
    tokens = ChipsFirst(g, part, full, *rest)
    small = Interleaved(tokens.phases)
    small.tick()

    def spread(q, carry):
        at = pl.ds(pl.multiple_of(q * blk, blk), blk)
        upper, lower = split(seed_ref[at])
        target = g.r * 2 * pieces + q
        seeds[target, 0] = upper
        seeds[target, 1] = lower
        return carry

    lax.fori_loop(0, 2 * pieces, spread, 0)

    def pair_copy(rp, i):
        p = piece(rp, g.k, i)
        at = i * rows + rp
        return remote(seeds.at[p], seeds.at[p], pair_sems.at[0, at], pair_sems.at[1, at], g.partner)

    def pair_wait(rp, i):
        at = i * rows + rp
        p = piece(rp, 1 - g.k, i)
        remote(seeds.at[p], seeds.at[p], pair_sems.at[0, at], pair_sems.at[1, at], g.partner).wait_recv()

    def stage_copy(i, s, j, base):
        at = i * (rows - 1) + rows - 2 ** (stages - s) + j
        p = piece(g.block(s, j, base), g.k, i)
        return remote(seeds.at[p], seeds.at[p], stage_sems.at[0, at], stage_sems.at[1, at], g.peer(s))

    def send(i, s):
        for j in range(g.count(s)):
            stage_copy(i, s, j, g.r).start()

    def land(i, s):
        for j in range(g.count(s)):
            stage_copy(i, s, j, g.peer_row(s)).wait_recv()
            pair_copy(g.block(s, j, g.peer_row(s)), i).start()

    def compute(t):
        slot = t % depth
        p = order(t)
        fetch(p, slot).wait()

        @pl.when(t + depth - 1 < count)
        def _():
            fetch(order(t + depth - 1), (t + depth - 1) % depth).start()

        upper, lower = split(tiles[slot])
        image[...] += (
            mul(upper, seeds[p, 0], rows_cols)
            + mul(lower, seeds[p, 0], rows_cols)
            + mul(upper, seeds[p, 1], rows_cols)
        )

    def own_step(t, carry):
        compute(t)
        return carry

    def other_step(t, carry):
        inner = (t - 2 * pieces) % (2 * (rows - 1))
        wave = (t - 2 * pieces) // (2 * (rows - 1))
        rp = (g.r + 1 + inner // 2) % rows

        @pl.when(inner % 2 == 1 - g.k)
        def _():
            pair_wait(rp, wave)

        compute(t)
        return carry

    image[...] = jnp.zeros_like(image)
    for i in range(pieces):
        send(i, stages - 1)
    first = 2 * pieces // (stages + 1)
    done = 0
    lag = stages
    for at in range(pieces + lag):
        small.tick(image_ticks[at] if at < len(image_ticks) else 1)
        for late in range(stages):
            i = at - late
            if 0 <= i < pieces:
                s = stages - 1 - late
                land(i, s)
                if s > 0:
                    send(i, s - 1)
        if done < 2 * pieces:
            stop = min(2 * pieces, done + first)
            lax.fori_loop(done, stop, own_step, 0)
            done = stop
        i = at - lag
        if 0 <= i < pieces:
            lax.fori_loop(done, 2 * pieces, own_step, 0)
            done = 2 * pieces
            start = 2 * pieces + i * 2 * (rows - 1)
            lax.fori_loop(start, start + 2 * (rows - 1), other_step, 0)
    small.rest()
    upper, lower = split(full[...])
    total = image[...] + mul(grads_ref[...], upper, cols_cols) + mul(grads_ref[...], lower, cols_cols)
    upper, lower = split(total.T)
    out_ref[:rank] = upper
    out_ref[rank:] = lower

    tokens.drain()
    for i in range(pieces):
        for s in range(stages):
            for j in range(g.count(s)):
                stage_copy(i, s, j, g.r).wait_send()
                pair_copy(g.block(s, j, g.peer_row(s)), i).wait_send()


def image_pair(accumulated, seed, grads, acts, rows, cols, collective_id):
    rank = seed.shape[1]
    height, width = accumulated.shape
    blk = 256 if seed.shape[0] % 512 == 0 else seed.shape[0] // 2
    total = width // blk
    pieces = total // (2 * rows)
    return pl.pallas_call(
        functools.partial(image_kernel, rows, cols),
        out_shape=jax.ShapeDtypeStruct((2 * rank, height), bf16),
        in_specs=[ANY, VMEM, VMEM, VMEM],
        out_specs=VMEM,
        scratch_shapes=[
            pltpu.VMEM((4, height, blk), f32),
            pltpu.VMEM((height, rank), f32),
            pltpu.VMEM((total, 2, blk, rank), bf16),
            DMA((4,)),
            DMA((2, pieces * rows)),
            DMA((2, pieces * (rows - 1))),
            *ChipsFirst.scratch(rank, acts.shape[1], rows, cols // 2),
        ],
        compiler_params=pltpu.CompilerParams(
            collective_id=collective_id, has_side_effects=True, vmem_limit_bytes=vmem_bytes
        ),
        name="image_pair",
    )(accumulated, seed, grads, acts)


def project_kernel(
    rows, cols, acc, basis_ref, turned_ref, grads_ref, acts_ref, out_ref, full_ref,
    tiles, tile_sem, pair_sems, stage_sems, chip_sems, *reduce_scratch,
):
    g = Grid(rows, cols)
    chips, stages = g.chips, g.stages
    blk = basis_ref.shape[0]
    count = chips * rows

    def chip_of(w):
        return (g.z + chips - w) % chips

    def at_of(rp, w, core):
        at = ((rp * chips + chip_of(w)) * 2 + core) * blk
        return full_ref.at[pl.ds(pl.multiple_of(at, blk), blk)]

    def fetch(t):
        w, rp = t // rows, t % rows
        at = (rp * chips + chip_of(w)) * 2 * blk
        columns = pl.ds(pl.multiple_of(at, 2 * blk), 2 * blk)
        return pltpu.make_async_copy(acc.at[:, columns], tiles.at[t % 2], tile_sem.at[t % 2])

    fetch(0).start()
    fetch(1).start()
    g.greet()
    own_rows = pl.ds(pl.multiple_of(((g.r * chips + g.z) * 2 + g.k) * blk, blk), blk)
    full_ref[own_rows] = basis_ref[...]

    def pair_copy(rp, w):
        i = w * rows + rp
        ref = at_of(rp, w, g.k)
        return remote(ref, ref, pair_sems.at[0, i], pair_sems.at[1, i], g.partner)

    def pair_wait(rp, w):
        i = w * rows + rp
        ref = at_of(rp, w, 1 - g.k)
        remote(ref, ref, pair_sems.at[0, i], pair_sems.at[1, i], g.partner).wait_recv()

    def stage_copy(w, s, j, base):
        i = w * (rows - 1) + rows - 2 ** (stages - s) + j
        ref = at_of(g.block(s, j, base), w, g.k)
        return remote(ref, ref, stage_sems.at[0, i], stage_sems.at[1, i], g.peer(s))

    def chip_copy(w, z):
        at = ((g.r * chips + z) * 2 + g.k) * blk
        ref = full_ref.at[pl.ds(pl.multiple_of(at, blk), blk)]
        device = g.chip_device(g.chip(w)[0])
        return remote(ref, ref, chip_sems.at[0, w], chip_sems.at[1, w], device)

    def enter(w):
        if w > 0:
            chip_copy(w - 1, chip_of(w)).wait_recv()
        stage_copy(w, stages - 1, 0, g.r).start()
        pair_copy(g.r, w).start()

    def land(w, s):
        for j in range(g.count(s)):
            stage_copy(w, s, j, g.peer_row(s)).wait_recv()
        if s > 0:
            for j in range(g.count(s - 1)):
                stage_copy(w, s - 1, j, g.r).start()
        for j in range(g.count(s)):
            pair_copy(g.block(s, j, g.peer_row(s)), w).start()

    for w in range(chips - 1):
        chip_copy(w, g.z).start()
    part, full, *rest = reduce_scratch
    enter(0)
    part[...] = mul(turned_ref[...], acts_ref[...], rows_cols)
    tokens = AllReduce(g, part, full, *rest)
    small = Interleaved(tokens.phases)
    small.tick()
    out_ref[...] = jnp.zeros_like(out_ref)

    def step(t, carry):
        w, rp = t // rows, t % rows
        fetch(t).wait()
        pair_wait(rp, w)
        at = (rp * chips + chip_of(w)) * 2 * blk
        block = full_ref[pl.ds(pl.multiple_of(at, 2 * blk), 2 * blk)]
        out_ref[...] += mul(tiles[t % 2].astype(bf16), block, rows_cols)

        @pl.when(t + 2 < count)
        def _():
            fetch(t + 2).start()

        return carry

    for at in range(chips + stages + 1):
        small.tick()
        for late in range(stages + 1):
            w = at - late
            if 0 <= w < chips:
                if late == 0:
                    if w > 0:
                        enter(w)
                else:
                    land(w, stages - late)
        w = at - stages
        if 0 <= w < chips:
            lax.fori_loop(w * rows, (w + 1) * rows, step, 0)
    small.rest()
    upper, lower = split(full[...])
    out_ref[...] += mul(grads_ref[...], upper, cols_cols) + mul(grads_ref[...], lower, cols_cols)

    tokens.drain()
    for w in range(chips - 1):
        chip_copy(w, g.z).wait_send()
    for w in range(chips):
        pair_copy(g.r, w).wait_send()
        for s in range(stages):
            for j in range(g.count(s)):
                stage_copy(w, s, j, g.r).wait_send()
                pair_copy(g.block(s, j, g.peer_row(s)), w).wait_send()


def project(accumulated, basis, turned, grads, acts, rows, cols, collective_id):
    height, width = accumulated.shape
    blk, rank = basis.shape
    chips = cols // 2
    return pl.pallas_call(
        functools.partial(project_kernel, rows, cols),
        out_shape=(
            jax.ShapeDtypeStruct((height, rank), f32),
            jax.ShapeDtypeStruct((width, rank), bf16),
        ),
        in_specs=[ANY, VMEM, VMEM, VMEM, VMEM],
        out_specs=(VMEM, VMEM),
        scratch_shapes=[
            pltpu.VMEM((2, height, 2 * blk), f32),
            DMA((2,)),
            DMA((2, chips * rows)),
            DMA((2, chips * (rows - 1))),
            DMA((2, chips - 1)),
            *AllReduce.scratch(rank, acts.shape[1], rows, chips),
        ],
        compiler_params=pltpu.CompilerParams(
            collective_id=collective_id, has_side_effects=True, vmem_limit_bytes=vmem_bytes
        ),
        name="project",
    )(accumulated, basis, turned, grads, acts)


def orthogonal_kernel(rows, cols, step, power_ref, out_ref, turned_ref, gram, rest, *reduce_scratch):
    g = Grid(rows, cols)
    g.greet()
    part, full, *others = reduce_scratch
    rank = gram.shape[0]
    count = rank // step
    product = mul(power_ref[...], power_ref[...], cols_cols, highest)
    across = part.shape[1] // step
    lower_blocks = [(i, j) for i in range(count) for j in range(i + 1)]

    def cut(n):
        return slice(n * step, (n + 1) * step)

    for n in range(count * across):
        i, j = lower_blocks[n] if n < len(lower_blocks) else (0, 0)
        part[cut(n // across), cut(n % across)] = product[cut(i), cut(j)]
    total = AllReduce(g, part, full, *others)
    for phase in total.phases:
        phase()
    rest[...] = power_ref[...]
    for n, (i, j) in enumerate(lower_blocks):
        gram[cut(i), cut(j)] = full[cut(n // across), cut(n % across)]
        if i > j:
            gram[cut(j), cut(i)] = jnp.zeros((step, step), f32)
    lanes = lax.broadcasted_iota(jnp.int32, (step, step), 1)
    lines = lax.broadcasted_iota(jnp.int32, (step, step), 0)

    def eliminate(j, carry):
        at = pl.ds(pl.multiple_of(j * step, step), step)
        left = gram[at, at]
        right = (lanes == lines).astype(f32)
        left_parts = [left[8 * i : 8 * i + 8] for i in range(step // 8)]
        right_parts = [right[8 * i : 8 * i + 8] for i in range(step // 8)]
        eights = lax.broadcasted_iota(jnp.int32, (8, step), 0)
        for n in range(step):
            q, o = n // 8, n % 8
            pivot_row = left_parts[q][o : o + 1]
            pivot_right = right_parts[q][o : o + 1]
            scale = 1.0 / pivot_row[:, n : n + 1]
            pivot_row = pivot_row * scale
            pivot_right = pivot_right * scale
            for i in range(q, step // 8):
                if i == q:
                    if o == 7:
                        continue
                    column = jnp.where(eights > o, left_parts[i][:, n : n + 1], 0.0)
                else:
                    column = left_parts[i][:, n : n + 1]
                left_parts[i] = left_parts[i] - column * pivot_row
                right_parts[i] = right_parts[i] - column * pivot_right
        left = jnp.concatenate(left_parts, axis=0)
        right = jnp.concatenate(right_parts, axis=0)
        diagonal = jnp.sum(jnp.where(lanes == lines, left, 0.0), axis=1, keepdims=True)
        inverse = right * lax.rsqrt(diagonal)
        panel = mul(gram[:, at], inverse, cols_cols, highest)
        below = lax.broadcasted_iota(jnp.int32, panel.shape, 0) >= (j + 1) * step
        panel = jnp.where(below, panel, 0.0)
        gram[...] -= mul(panel, panel, cols_cols, highest)
        solved = mul(inverse, rest[at], rows_cols, highest)
        rest[...] -= mul(panel, solved, rows_cols, highest)
        turned_ref[at] = solved.astype(bf16)
        return carry

    lax.fori_loop(0, rank // step, eliminate, 0)
    out_ref[...] = turned_ref[...].astype(f32).T.astype(bf16)
    total.drain()


def orthogonal(power_turned, rows, cols, collective_id):
    rank, blk = power_turned.shape
    blocks = rank // 128
    return pl.pallas_call(
        functools.partial(orthogonal_kernel, rows, cols, 128),
        out_shape=(
            jax.ShapeDtypeStruct((blk, rank), bf16),
            jax.ShapeDtypeStruct((rank, blk), bf16),
        ),
        in_specs=[VMEM],
        out_specs=(VMEM, VMEM),
        scratch_shapes=[
            pltpu.VMEM((rank, rank), f32),
            pltpu.VMEM((rank, blk), f32),
            *AllReduce.scratch(rank, 128 * -(-blocks * (blocks + 1) // (2 * blocks)), rows, cols // 2),
        ],
        compiler_params=pltpu.CompilerParams(
            collective_id=collective_id, has_side_effects=True, vmem_limit_bytes=vmem_bytes
        ),
        name="orthogonal",
    )(power_turned)


def solve_lower(gram_matrix, right):
    rank = gram_matrix.shape[0]
    step = 128 if rank % 128 == 0 else rank
    count = rank // step
    cut = lambda n: slice(n * step, (n + 1) * step)
    trailing = {
        (i, j): gram_matrix[cut(i), cut(j)] for i in range(count) for j in range(i + 1)
    }
    rests = [right[cut(i)] for i in range(count)]
    solved = []
    for j in range(count):
        factor = lax.linalg.cholesky(trailing[j, j], symmetrize_input=False)
        inverse = jax.scipy.linalg.solve_triangular(
            factor, jnp.eye(step, dtype=jnp.float32), lower=True
        )
        panel = {
            i: mul(trailing[i, j], inverse, cols_cols, highest) for i in range(j + 1, count)
        }
        solved.append(mul(inverse, rests[j], rows_cols, highest))
        for i in range(j + 1, count):
            rests[i] = rests[i] - mul(panel[i], solved[j], rows_cols, highest)
            for k in range(j + 1, i + 1):
                trailing[i, k] = trailing[i, k] - mul(panel[i], panel[k], cols_cols, highest)
    return jnp.concatenate(solved, axis=0)


def finish(moment_first, moment_second, projected, full_basis):
    first_next = beta_first * moment_first + (1.0 - beta_first) * projected
    second_next = beta_second * moment_second + (1.0 - beta_second) * projected * projected
    direction = (
        first_next / correct_first / (jnp.sqrt(second_next / correct_second) + epsilon_value)
    )
    lifted = lift_scale * mul(direction.astype(bf16), full_basis, cols_cols)
    return first_next, second_next, lifted


def plain_body(activations, out_grads, accumulated, seed_basis, moment_first, moment_second):
    share_rows = activations.shape[0]
    acts = activations.astype(jnp.float32)
    grads = out_grads.astype(jnp.float32)
    own_seed = lax.dynamic_slice_in_dim(
        seed_basis, lax.axis_index("col") * share_rows, share_rows, 0
    )
    full_seed = lax.all_gather(own_seed, every, axis=0, tiled=True)
    seed_tokens = lax.psum(mul(acts, own_seed, rows_rows, highest), every)
    image_rows = mul(accumulated, full_seed, rows_cols, high) + mul(
        grads, seed_tokens, rows_cols, high
    )
    image_tokens = lax.psum(mul(grads, image_rows, rows_rows, high), every)
    power_part = mul(accumulated, image_rows, rows_rows, high)
    power_rows = lax.psum_scatter(
        power_part, every, scatter_dimension=0, tiled=True
    ) + mul(acts, image_tokens, rows_cols, highest)
    gram_matrix = lax.psum(mul(power_rows, power_rows, rows_rows, highest), every)
    gram_matrix, held_acts = lax.optimization_barrier((gram_matrix, activations))
    full_acts = lax.all_gather(held_acts, every, axis=0, tiled=True)
    solved = solve_lower(gram_matrix, power_rows.T)
    basis_rows = solved.T.astype(jnp.bfloat16)
    sent_rows, full_acts = lax.optimization_barrier((basis_rows, full_acts))
    full_basis = lax.all_gather(sent_rows, every, axis=0, tiled=True)
    basis_tokens = mul(full_acts, full_basis, rows_rows)
    projected = mul(accumulated.astype(jnp.bfloat16), full_basis, rows_cols) + mul(
        grads, basis_tokens, rows_cols, high
    )
    return (basis_rows, *finish(moment_first, moment_second, projected, full_basis))


def body(rows, cols, activations, out_grads, accumulated, seed_basis, moment_first, moment_second):
    common = (out_grads, activations, rows, cols)
    pair = image_pair(accumulated, seed_basis, *common, 1)
    power_turned = power_scatter(accumulated, pair, *common, 2)
    basis_rows, turned = orthogonal(power_turned, rows, cols, 3)
    projected, full_basis = project(accumulated, basis_rows, turned, *common, 4)
    return (basis_rows, *finish(moment_first, moment_second, projected, full_basis))


def solution(mesh):
    rows, cols = mesh.shape["row"], mesh.shape["col"]

    def place(activations, *others):
        rank = others[2].shape[1]
        fits = rows & (rows - 1) == 0 and rows > 1 and cols % 2 == 0 and cols > 2
        fits = fits and activations.shape[0] % 128 == 0 and rank % (8 * rows * cols) == 0
        fits = fits and rank % 128 == 0
        if fits:
            return body(rows, cols, activations, *others)
        return plain_body(activations, *others)

    split_rows = P(("row", "col"), None)
    in_specs = (split_rows, split_rows, split_rows, P("row", None), split_rows, split_rows)
    return jax.shard_map(
        place, mesh=mesh, in_specs=in_specs, out_specs=(split_rows,) * 4, check_vma=False
    )
```

```python
import functools

import jax
import jax.numpy as jnp
from jax import lax
from jax.experimental import pallas as pl
from jax.experimental.pallas import tpu as pltpu
from jax.sharding import PartitionSpec as P

beta_first = 0.9
beta_second = 0.99
correct_first = 1.0 - 0.9**10
correct_second = 1.0 - 0.99**10
epsilon_value = 1e-08
lift_scale = 8.0

every = ("row", "col")
highest = lax.Precision.HIGHEST
high = lax.Precision.HIGH
bf16 = jnp.bfloat16
f32 = jnp.float32
MESH = pl.DeviceIdType.MESH
ANY = pl.BlockSpec(memory_space=pl.ANY)
VMEM = pl.BlockSpec(memory_space=pltpu.VMEM)
DMA = pltpu.SemaphoreType.DMA
vmem_bytes = 63 * 2**20
image_gather = 4
image_ticks = (1, 0, 2, 2, 1, 1)
power_lag, power_gap, power_ticks = 7, 4, (1, 3, 5, 7, 9, 11, 13, 15, 16)


def mul(left, right, dims, precision=None):
    return lax.dot_general(
        left, right, (dims, ((), ())), precision=precision, preferred_element_type=jnp.float32
    )


rows_cols = ((1,), (0,))
rows_rows = ((0,), (0,))
cols_cols = ((1,), (1,))


def split(value):
    upper = value.astype(bf16)
    return upper, (value - upper.astype(f32)).astype(bf16)


class Grid:
    def __init__(self, rows, cols):
        self.rows, self.chips = rows, cols // 2
        self.stages = rows.bit_length() - 1
        self.r = lax.axis_index("row")
        c = lax.axis_index("col")
        self.z, self.k = c // 2, c % 2
        self.c = c
        self.partner = (self.r, self.z * 2 + 1 - self.k)
        n = self.chips
        self.offsets = sorted(range(1, n), key=lambda d: -min(d, n - d))

    def flip(self, bit):
        return self.r + bit * (1 - 2 * ((self.r // bit) % 2))

    def peer_row(self, s, k=None):
        k = self.k if k is None else k
        low, high_bit = 2**s, 2 ** (self.stages - 1 - s)
        return (1 - k) * self.flip(low) + k * self.flip(high_bit)

    def peer(self, s):
        return (self.peer_row(s), self.c)

    def count(self, s):
        return 2 ** (self.stages - 1 - s)

    def block(self, s, j, base, k=None):
        k = self.k if k is None else k
        n = self.count(s)
        first = base % 2 ** (s + 1) + j * 2 ** (s + 1)
        second = (base // n) * n + j
        return (1 - k) * first + k * second

    def chip(self, w, far_first=False):
        n, step = self.chips, self.offsets[w] if far_first else w + 1
        return (self.z + step) % n, (self.z + n - step) % n

    def chip_device(self, z):
        return (self.r, z * 2 + self.k)

    def greet(self):
        barrier = pltpu.get_barrier_semaphore()
        peers = [self.partner]
        peers += [self.peer(s) for s in range(self.stages)]
        peers += [self.chip_device(self.chip(w)[0]) for w in range(self.chips - 1)]
        for peer in peers:
            pl.semaphore_signal(barrier, inc=1, device_id=peer, device_id_type=MESH)
        pl.semaphore_wait(barrier, len(peers))


def remote(source, target, send, recv, device):
    return pltpu.make_async_remote_copy(
        src_ref=source, dst_ref=target, send_sem=send, recv_sem=recv,
        device_id=device, device_id_type=MESH,
    )


class AllReduce:
    def __init__(self, grid, part, full, half_in, stage_in, chip_in, send, recv):
        self.g, self.part, self.full = grid, part, full
        self.half_in, self.stage_in, self.chip_in = half_in, stage_in, chip_in
        self.send, self.recv = send, recv
        self.half = part.shape[0] // 2
        self.chunk = self.half // grid.rows
        self.unit = self.chunk // grid.chips
        self.pending = []
        self.used = 0
        self.phases = (
            [self.pair_out]
            + [functools.partial(self.halve, s) for s in range(grid.stages)]
            + [self.chips_out, self.chips_back]
            + [functools.partial(self.double, s) for s in reversed(range(grid.stages))]
            + [self.pair_back, self.finish]
        )
        self.arrived = []

    @staticmethod
    def scratch(rows, width, grid_rows, chips):
        half = rows // 2
        chunk = half // grid_rows
        stages = grid_rows.bit_length() - 1
        copies = 2 + 2 * (grid_rows - 1) + 2 * (chips - 1)
        return [
            pltpu.VMEM((rows, width), f32),
            pltpu.VMEM((rows, width), f32),
            pltpu.VMEM((half, width), f32),
            pltpu.VMEM((grid_rows - 1, chunk, width), f32),
            pltpu.VMEM((chips - 1, chunk // chips, width), f32),
            DMA((copies,)),
            DMA((copies,)),
        ]

    def start(self, source, target, device):
        i = self.used
        self.used += 1
        copy = remote(source, target, self.send.at[i], self.recv.at[i], device)
        copy.start()
        self.pending.append(copy)
        self.arrived.append(copy)

    def landed(self):
        arrived, self.arrived = self.arrived, []
        for copy in arrived:
            copy.wait_recv()

    def rows_of(self, r):
        return pl.ds(pl.multiple_of((self.g.k * self.g.rows + r) * self.chunk, self.chunk), self.chunk)

    def unit_of(self, r, z):
        at = ((self.g.k * self.g.rows + r) * self.g.chips + z) * self.unit
        return pl.ds(pl.multiple_of(at, self.unit), self.unit)

    def pair_out(self):
        g = self.g
        other = pl.ds(pl.multiple_of((1 - g.k) * self.half, self.half), self.half)
        self.start(self.part.at[other], self.half_in, g.partner)

    def stage_base(self, s):
        return self.g.rows - 2 ** (self.g.stages - s)

    def halve(self, s):
        g = self.g
        self.landed()
        if s == 0:
            mine = pl.ds(pl.multiple_of(g.k * self.half, self.half), self.half)
            self.part[mine] += self.half_in[...]
        else:
            self.take(s - 1)
        for j in range(g.count(s)):
            rows = self.rows_of(g.block(s, j, g.peer_row(s)))
            self.start(self.part.at[rows], self.stage_in.at[self.stage_base(s) + j], g.peer(s))

    def take(self, s):
        g = self.g
        for j in range(g.count(s)):
            self.part[self.rows_of(g.block(s, j, g.r))] += self.stage_in[self.stage_base(s) + j]

    def chips_out(self):
        g = self.g
        self.landed()
        self.take(g.stages - 1)
        for w in range(g.chips - 1):
            z = g.chip(w)[0]
            self.start(self.part.at[self.unit_of(g.r, z)], self.chip_in.at[w], g.chip_device(z))

    def chips_back(self):
        g = self.g
        self.landed()
        own = self.unit_of(g.r, g.z)
        total = self.part[own]
        for w in range(g.chips - 1):
            total = total + self.chip_in[w]
        self.full[own] = total
        for w in range(g.chips - 1):
            self.start(self.full.at[own], self.full.at[own], g.chip_device(g.chip(w)[0]))

    def double(self, s):
        g = self.g
        self.landed()
        for j in range(g.count(s)):
            rows = self.rows_of(g.block(s, j, g.r))
            self.start(self.full.at[rows], self.full.at[rows], g.peer(s))

    def pair_back(self):
        g = self.g
        self.landed()
        mine = pl.ds(pl.multiple_of(g.k * self.half, self.half), self.half)
        self.start(self.full.at[mine], self.full.at[mine], g.partner)

    def finish(self):
        self.landed()

    def drain(self):
        for copy in self.pending:
            copy.wait_send()


class ChipsFirst(AllReduce):
    def __init__(self, grid, *refs):
        super().__init__(grid, *refs)
        self.chunk = self.half // grid.chips
        self.unit = self.chunk // grid.rows
        self.phases = (
            [self.pair_out, self.chips_out]
            + [functools.partial(self.halve, s) for s in range(grid.stages)]
            + [functools.partial(self.double, s) for s in reversed(range(grid.stages))]
            + [self.chips_back, self.pair_back, self.finish]
        )

    @staticmethod
    def scratch(rows, width, grid_rows, chips):
        shapes = AllReduce.scratch(rows, width, grid_rows, chips)
        half = rows // 2
        unit = half // (chips * grid_rows)
        shapes[3] = pltpu.VMEM((grid_rows - 1, unit, width), f32)
        shapes[4] = pltpu.VMEM((chips - 1, half // chips, width), f32)
        return shapes

    def rows_of(self, r):
        at = ((self.g.k * self.g.chips + self.g.z) * self.g.rows + r) * self.unit
        return pl.ds(pl.multiple_of(at, self.unit), self.unit)

    def chunk_of(self, z):
        at = (self.g.k * self.g.chips + z) * self.chunk
        return pl.ds(pl.multiple_of(at, self.chunk), self.chunk)

    def chips_out(self):
        g = self.g
        self.landed()
        mine = pl.ds(pl.multiple_of(g.k * self.half, self.half), self.half)
        self.part[mine] += self.half_in[...]
        for w in range(g.chips - 1):
            z = g.chip(w)[0]
            self.start(self.part.at[self.chunk_of(z)], self.chip_in.at[w], g.chip_device(z))

    def halve(self, s):
        g = self.g
        self.landed()
        if s == 0:
            own = self.chunk_of(g.z)
            total = self.part[own]
            for w in range(g.chips - 1):
                total = total + self.chip_in[w]
            self.part[own] = total
        else:
            self.take(s - 1)
        for j in range(g.count(s)):
            rows = self.rows_of(g.block(s, j, g.peer_row(s)))
            self.start(self.part.at[rows], self.stage_in.at[self.stage_base(s) + j], g.peer(s))

    def double(self, s):
        g = self.g
        if s == g.stages - 1:
            self.landed()
            self.take(s)
            self.full[self.rows_of(g.r)] = self.part[self.rows_of(g.r)]
        super().double(s)

    def chips_back(self):
        g = self.g
        self.landed()
        own = self.chunk_of(g.z)
        for w in range(g.chips - 1):
            self.start(self.full.at[own], self.full.at[own], g.chip_device(g.chip(w)[0]))


def reduce_kernel(rows, cols, part_ref, out_ref, *scratch):
    grid = Grid(rows, cols)
    grid.greet()
    part, full, *rest = scratch
    part[...] = part_ref[...]
    total = AllReduce(grid, part, full, *rest)
    for phase in total.phases:
        phase()
    out_ref[...] = full[...]
    total.drain()


def all_reduce(value, rows, cols, collective_id):
    return pl.pallas_call(
        functools.partial(reduce_kernel, rows, cols),
        out_shape=jax.ShapeDtypeStruct(value.shape, f32),
        in_specs=[VMEM],
        out_specs=VMEM,
        scratch_shapes=AllReduce.scratch(*value.shape, rows, cols // 2),
        compiler_params=pltpu.CompilerParams(
            collective_id=collective_id, has_side_effects=True, vmem_limit_bytes=vmem_bytes
        ),
        name="all_reduce",
    )(value)


def power_kernel(
    rows, cols, acc, pair_ref, grads_ref, acts_ref, out_ref,
    tiles, mine, theirs, pair_in, stage_in, chip_in,
    tile_sem, pair_sems, stage_sems, chip_sems, *reduce_scratch,
):
    g = Grid(rows, cols)
    blk = acts_ref.shape[0]
    rank = out_ref.shape[0]
    chips, stages = g.chips, g.stages

    half = g.count(0)

    def chip_of(w):
        return g.chip(w, True)[0] if w < chips - 1 else g.z

    def block_of(t, kind=1):
        w, i = t // rows, t % rows
        core = (1 - g.k) if kind == 0 else g.k
        return w, g.block(0, i % half, g.peer_row(0, core) if i < half else g.r, core)

    def fetch(t, kind):
        w, rp = block_of(t, kind)
        core = (1 - g.k) if kind == 0 else g.k
        at = ((rp * chips + chip_of(w)) * 2 + core) * blk
        columns = pl.ds(pl.multiple_of(at, blk), blk)
        slot = kind * 2 + t % 2
        return pltpu.make_async_copy(acc.at[:, columns], tiles.at[slot], tile_sem.at[slot])

    for t in range(2):
        fetch(t, 0).start()
        fetch(t, 1).start()
    g.greet()

    def product(slot):
        upper, lower = split(tiles[slot])
        both = mul(pair_ref[...], upper, rows_cols)
        return both[:rank] + both[rank:] + mul(pair_ref[:rank], lower, rows_cols)

    def pair_copy(w, rp):
        i = w * rows + rp
        return remote(theirs.at[i], pair_in.at[i], pair_sems.at[0, i], pair_sems.at[1, i], g.partner)

    def stage_copy(w, s, j):
        i = w * (rows - 1) + rows - 2 ** (stages - s) + j
        source = mine.at[w * rows + g.block(s, j, g.peer_row(s))]
        return remote(source, stage_in.at[i], stage_sems.at[0, i], stage_sems.at[1, i], g.peer(s))

    def chip_copy(w):
        return remote(
            mine.at[w * rows + g.r], chip_in.at[w], chip_sems.at[0, w], chip_sems.at[1, w],
            g.chip_device(chip_of(w)),
        )

    def compute(t):
        for kind, store in ((0, theirs), (1, mine)):
            w, rp = block_of(t, kind)
            fetch(t, kind).wait()
            store[w * rows + rp] = product(kind * 2 + t % 2)
            if kind == 0:
                pair_copy(w, rp).start()
            if t + 2 < chips * rows:
                fetch(t + 2, kind).start()

    def pair(t):
        w, rp = block_of(t)
        pair_copy(w, rp).wait_recv()
        mine[w * rows + rp] += pair_in[w * rows + rp]
        if t % rows < half:
            stage_copy(w, 0, t % rows).start()

    def halve(w, s):
        for j in range(g.count(s - 1)):
            i = w * (rows - 1) + rows - 2 ** (stages - s + 1) + j
            stage_copy(w, s - 1, j).wait_recv()
            mine[w * rows + g.block(s - 1, j, g.r)] += stage_in[i]
        for j in range(g.count(s)):
            stage_copy(w, s, j).start()

    def leave(w):
        i = w * (rows - 1) + rows - 2
        stage_copy(w, stages - 1, 0).wait_recv()
        mine[w * rows + g.r] += stage_in[i]
        if w < chips - 1:
            chip_copy(w).start()

    part, full, *rest = reduce_scratch

    part[...] = mul(pair_ref[:rank], grads_ref[...], rows_cols) + mul(
        pair_ref[rank:], grads_ref[...], rows_cols
    )
    tokens = AllReduce(g, part, full, *rest)
    phases = iter(tokens.phases)

    def tick():
        phase = next(phases, None)
        if phase is not None:
            phase()

    tick()
    steps = chips * rows
    lag, gap, ticks = power_lag, power_gap, power_ticks
    later = {}
    for w in range(chips):
        for s in range(1, stages):
            later.setdefault(min(lag + gap * w + 3 * (s - 1), steps + 2 * w + s), []).append(
                functools.partial(halve, w, s)
            )
    for w in range(chips):
        later.setdefault(min(lag + gap * w + gap, steps + 2 * w + 3), []).append(
            functools.partial(leave, w)
        )
    for t in range(max(max(later), steps) + 1):
        if t in ticks:
            tick()
        if t < steps:
            compute(t)
        if 0 < t <= steps:
            pair(t - 1)
        for event in later.get(t, ()):
            event()
    for phase in phases:
        phase()
    upper, lower = split(full[...])
    total = mul(upper, acts_ref[...], cols_cols) + mul(lower, acts_ref[...], cols_cols)
    total = total + mine[(chips - 1) * rows + g.r]
    for w in range(chips - 1):
        chip_copy(w).wait_recv()
        total = total + chip_in[w]
    out_ref[...] = total

    tokens.drain()
    for w in range(chips):
        def done(rp, carry):
            pair_copy(w, rp).wait_send()
            return carry

        lax.fori_loop(0, rows, done, 0)
        for s in range(stages):
            for j in range(g.count(s)):
                stage_copy(w, s, j).wait_send()
        if w < chips - 1:
            chip_copy(w).wait_send()


def power_scatter(accumulated, pair, grads, acts, rows, cols, collective_id):
    rank = pair.shape[0] // 2
    blk = acts.shape[0]
    chips = cols // 2
    blocks = chips * rows
    passed = chips * (rows - 1)
    return pl.pallas_call(
        functools.partial(power_kernel, rows, cols),
        out_shape=jax.ShapeDtypeStruct((rank, blk), f32),
        in_specs=[ANY, VMEM, VMEM, VMEM],
        out_specs=VMEM,
        scratch_shapes=[
            pltpu.VMEM((4, accumulated.shape[0], blk), f32),
            pltpu.VMEM((blocks, rank, blk), f32),
            pltpu.VMEM((blocks, rank, blk), f32),
            pltpu.VMEM((blocks, rank, blk), f32),
            pltpu.VMEM((passed, rank, blk), f32),
            pltpu.VMEM((chips - 1, rank, blk), f32),
            DMA((4,)),
            DMA((2, blocks)),
            DMA((2, passed)),
            DMA((2, chips - 1)),
            *AllReduce.scratch(rank, acts.shape[1], rows, chips),
        ],
        compiler_params=pltpu.CompilerParams(
            collective_id=collective_id, has_side_effects=True, vmem_limit_bytes=vmem_bytes
        ),
        name="power_scatter",
    )(accumulated, pair, grads, acts)


class Interleaved:
    def __init__(self, phases):
        self.left = list(phases)

    def tick(self, count=1):
        for _ in range(count):
            if self.left:
                self.left.pop(0)()

    def rest(self):
        self.tick(len(self.left))


def image_kernel(
    rows, cols, acc, seed_ref, grads_ref, acts_ref, out_ref,
    tiles, image, seeds, tile_sem, pair_sems, stage_sems, share_sems, *reduce_scratch,
):
    g = Grid(rows, cols)
    stages = g.stages
    blk, rank = seeds.shape[2], seeds.shape[3]
    own_rows = seed_ref.shape[0]
    pieces = own_rows // (2 * blk)
    tokens_rows = acts_ref.shape[0]

    def piece(rp, h, i):
        return (rp * 2 + h) * pieces + i

    def fetch(p, slot):
        columns = pl.ds(pl.multiple_of(p * blk, blk), blk)
        return pltpu.make_async_copy(acc.at[:, columns], tiles.at[slot], tile_sem.at[slot])

    def order(t):
        u = t - 2 * pieces
        wave = u // (2 * (rows - 1))
        inner = u % (2 * (rows - 1))
        other = piece((g.r + 1 + inner // 2) % rows, inner % 2, (wave + 1) % pieces)
        own = piece(g.r, t // pieces, t % pieces)
        return jnp.where(t < 2 * pieces, own, other)

    count = 2 * pieces * rows
    depth = tiles.shape[0]
    for t in range(depth - 1):
        fetch(order(t), t).start()
    g.greet()

    def spread(q):
        at = pl.ds(pl.multiple_of(q * blk, blk), blk)
        upper, lower = split(seed_ref[at])
        target = g.r * 2 * pieces + q
        seeds[target, 0] = upper
        seeds[target, 1] = lower

    share = blk // g.chips

    def shared(p, z):
        return seeds.at[p, :, pl.ds(pl.multiple_of(z * share, share), share)]

    def share_copy(s, j, w, z):
        at = (rows - 2 ** (stages - s) + j) * (g.chips - 1) + w
        ref = shared(piece(g.block(s, j, g.peer_row(s)), g.k, 0), z)
        device = g.chip_device(g.chip(w)[0])
        return remote(ref, ref, share_sems.at[0, at], share_sems.at[1, at], device)

    def pair_copy(rp, i):
        p = piece(rp, g.k, i)
        at = i * rows + rp
        return remote(seeds.at[p], seeds.at[p], pair_sems.at[0, at], pair_sems.at[1, at], g.partner)

    def pair_wait(rp, i):
        at = i * rows + rp
        p = piece(rp, 1 - g.k, i)
        remote(seeds.at[p], seeds.at[p], pair_sems.at[0, at], pair_sems.at[1, at], g.partner).wait_recv()

    def stage_copy(i, s, j, base):
        at = i * (rows - 1) + rows - 2 ** (stages - s) + j
        p = piece(g.block(s, j, base), g.k, i)
        ref = seeds.at[p] if i else shared(p, g.z)
        return remote(ref, ref, stage_sems.at[0, at], stage_sems.at[1, at], g.peer(s))

    def send(i, s):
        for j in range(g.count(s)):
            stage_copy(i, s, j, g.r).start()

    def land(i, s):
        for j in range(g.count(s)):
            stage_copy(i, s, j, g.peer_row(s)).wait_recv()
            if i:
                pair_copy(g.block(s, j, g.peer_row(s)), i).start()
            else:
                for w in range(g.chips - 1):
                    share_copy(s, j, w, g.z).start()

    def gather():
        for s in reversed(range(stages)):
            for j in range(g.count(s)):
                for w in range(g.chips - 1):
                    share_copy(s, j, w, g.chip(w)[1]).wait_recv()
                pair_copy(g.block(s, j, g.peer_row(s)), 0).start()

    def compute(t):
        slot = t % depth
        p = order(t)
        fetch(p, slot).wait()

        @pl.when(t + depth - 1 < count)
        def _():
            fetch(order(t + depth - 1), (t + depth - 1) % depth).start()

        upper, lower = split(tiles[slot])
        image[...] += (
            mul(upper, seeds[p, 0], rows_cols)
            + mul(lower, seeds[p, 0], rows_cols)
            + mul(upper, seeds[p, 1], rows_cols)
        )

    def own_step(t, carry):
        compute(t)
        return carry

    def other_step(t, carry):
        inner = (t - 2 * pieces) % (2 * (rows - 1))
        wave = (t - 2 * pieces) // (2 * (rows - 1))
        rp = (g.r + 1 + inner // 2) % rows

        @pl.when(inner % 2 == 1 - g.k)
        def _():
            pair_wait(rp, (wave + 1) % pieces)

        compute(t)
        return carry

    for i in range(pieces):
        spread(g.k * pieces + i)
        send(i, stages - 1)
    own = pl.ds(pl.multiple_of(g.c * tokens_rows, tokens_rows), tokens_rows)
    turned = seed_ref[own].T
    part, full, *rest = reduce_scratch
    upper, lower = split(turned)
    part[...] = mul(upper, acts_ref[...], rows_cols) + mul(lower, acts_ref[...], rows_cols)
    tokens = ChipsFirst(g, part, full, *rest)
    small = Interleaved(tokens.phases)
    small.tick()

    def spread_other(i, carry):
        spread((1 - g.k) * pieces + i)
        return carry

    lax.fori_loop(0, pieces, spread_other, 0)
    image[...] = jnp.zeros_like(image)
    first = 2 * pieces // (stages + 1)
    done = 0
    lag = stages
    for at in range(pieces + lag):
        small.tick(image_ticks[at] if at < len(image_ticks) else 1)
        for late in range(stages):
            i = at - late
            if 0 <= i < pieces:
                s = stages - 1 - late
                land(i, s)
                if s > 0:
                    send(i, s - 1)
        if at == image_gather:
            gather()
        if done < 2 * pieces:
            stop = min(2 * pieces, done + first)
            lax.fori_loop(done, stop, own_step, 0)
            done = stop
        i = at - lag
        if 0 <= i < pieces:
            lax.fori_loop(done, 2 * pieces, own_step, 0)
            done = 2 * pieces
            start = 2 * pieces + i * 2 * (rows - 1)
            lax.fori_loop(start, start + 2 * (rows - 1), other_step, 0)
    small.rest()
    upper, lower = split(full[...])
    total = image[...] + mul(grads_ref[...], upper, cols_cols) + mul(grads_ref[...], lower, cols_cols)
    upper, lower = split(total.T)
    out_ref[:rank] = upper
    out_ref[rank:] = lower

    tokens.drain()
    for i in range(pieces):
        for s in range(stages):
            for j in range(g.count(s)):
                stage_copy(i, s, j, g.r).wait_send()
                pair_copy(g.block(s, j, g.peer_row(s)), i).wait_send()
    for s in range(stages):
        for j in range(g.count(s)):
            for w in range(g.chips - 1):
                share_copy(s, j, w, g.z).wait_send()


def image_pair(accumulated, seed, grads, acts, rows, cols, collective_id):
    rank = seed.shape[1]
    height, width = accumulated.shape
    blk = 256 if seed.shape[0] % 512 == 0 else seed.shape[0] // 2
    total = width // blk
    pieces = total // (2 * rows)
    return pl.pallas_call(
        functools.partial(image_kernel, rows, cols),
        out_shape=jax.ShapeDtypeStruct((2 * rank, height), bf16),
        in_specs=[ANY, VMEM, VMEM, VMEM],
        out_specs=VMEM,
        scratch_shapes=[
            pltpu.VMEM((4, height, blk), f32),
            pltpu.VMEM((height, rank), f32),
            pltpu.VMEM((total, 2, blk, rank), bf16),
            DMA((4,)),
            DMA((2, pieces * rows)),
            DMA((2, pieces * (rows - 1))),
            DMA((2, (cols // 2 - 1) * (rows - 1))),
            *ChipsFirst.scratch(rank, acts.shape[1], rows, cols // 2),
        ],
        compiler_params=pltpu.CompilerParams(
            collective_id=collective_id, has_side_effects=True, vmem_limit_bytes=vmem_bytes
        ),
        name="image_pair",
    )(accumulated, seed, grads, acts)


def project_kernel(
    rows, cols, acc, basis_ref, turned_ref, grads_ref, acts_ref, out_ref, full_ref,
    tiles, tile_sem, pair_sems, stage_sems, chip_sems, *reduce_scratch,
):
    g = Grid(rows, cols)
    chips, stages = g.chips, g.stages
    blk = basis_ref.shape[0]
    count = chips * rows

    def chip_of(w):
        return (g.z + chips - w) % chips

    def at_of(rp, w, core):
        at = ((rp * chips + chip_of(w)) * 2 + core) * blk
        return full_ref.at[pl.ds(pl.multiple_of(at, blk), blk)]

    def fetch(t):
        w, rp = t // rows, t % rows
        at = (rp * chips + chip_of(w)) * 2 * blk
        columns = pl.ds(pl.multiple_of(at, 2 * blk), 2 * blk)
        return pltpu.make_async_copy(acc.at[:, columns], tiles.at[t % 2], tile_sem.at[t % 2])

    fetch(0).start()
    fetch(1).start()
    g.greet()
    own_rows = pl.ds(pl.multiple_of(((g.r * chips + g.z) * 2 + g.k) * blk, blk), blk)
    full_ref[own_rows] = basis_ref[...]

    def pair_copy(rp, w):
        i = w * rows + rp
        ref = at_of(rp, w, g.k)
        return remote(ref, ref, pair_sems.at[0, i], pair_sems.at[1, i], g.partner)

    def pair_wait(rp, w):
        i = w * rows + rp
        ref = at_of(rp, w, 1 - g.k)
        remote(ref, ref, pair_sems.at[0, i], pair_sems.at[1, i], g.partner).wait_recv()

    def stage_copy(w, s, j, base):
        i = w * (rows - 1) + rows - 2 ** (stages - s) + j
        ref = at_of(g.block(s, j, base), w, g.k)
        return remote(ref, ref, stage_sems.at[0, i], stage_sems.at[1, i], g.peer(s))

    def chip_copy(w, z):
        at = ((g.r * chips + z) * 2 + g.k) * blk
        ref = full_ref.at[pl.ds(pl.multiple_of(at, blk), blk)]
        device = g.chip_device(g.chip(w)[0])
        return remote(ref, ref, chip_sems.at[0, w], chip_sems.at[1, w], device)

    def enter(w):
        if w > 0:
            chip_copy(w - 1, chip_of(w)).wait_recv()
        stage_copy(w, stages - 1, 0, g.r).start()
        pair_copy(g.r, w).start()

    def land(w, s):
        for j in range(g.count(s)):
            stage_copy(w, s, j, g.peer_row(s)).wait_recv()
        if s > 0:
            for j in range(g.count(s - 1)):
                stage_copy(w, s - 1, j, g.r).start()
        for j in range(g.count(s)):
            pair_copy(g.block(s, j, g.peer_row(s)), w).start()

    for w in range(chips - 1):
        chip_copy(w, g.z).start()
    part, full, *rest = reduce_scratch
    enter(0)
    part[...] = mul(turned_ref[...], acts_ref[...], rows_cols)
    tokens = AllReduce(g, part, full, *rest)
    small = Interleaved(tokens.phases)
    small.tick()
    out_ref[...] = jnp.zeros_like(out_ref)

    def step(t, carry):
        w, rp = t // rows, t % rows
        fetch(t).wait()
        pair_wait(rp, w)
        at = (rp * chips + chip_of(w)) * 2 * blk
        block = full_ref[pl.ds(pl.multiple_of(at, 2 * blk), 2 * blk)]
        out_ref[...] += mul(tiles[t % 2].astype(bf16), block, rows_cols)

        @pl.when(t + 2 < count)
        def _():
            fetch(t + 2).start()

        return carry

    for at in range(chips + stages + 1):
        small.tick()
        for late in range(stages + 1):
            w = at - late
            if 0 <= w < chips:
                if late == 0:
                    if w > 0:
                        enter(w)
                else:
                    land(w, stages - late)
        w = at - stages
        if 0 <= w < chips:
            lax.fori_loop(w * rows, (w + 1) * rows, step, 0)
    small.rest()
    upper, lower = split(full[...])
    out_ref[...] += mul(grads_ref[...], upper, cols_cols) + mul(grads_ref[...], lower, cols_cols)

    tokens.drain()
    for w in range(chips - 1):
        chip_copy(w, g.z).wait_send()
    for w in range(chips):
        pair_copy(g.r, w).wait_send()
        for s in range(stages):
            for j in range(g.count(s)):
                stage_copy(w, s, j, g.r).wait_send()
                pair_copy(g.block(s, j, g.peer_row(s)), w).wait_send()


def project(accumulated, basis, turned, grads, acts, rows, cols, collective_id):
    height, width = accumulated.shape
    blk, rank = basis.shape
    chips = cols // 2
    return pl.pallas_call(
        functools.partial(project_kernel, rows, cols),
        out_shape=(
            jax.ShapeDtypeStruct((height, rank), f32),
            jax.ShapeDtypeStruct((width, rank), bf16),
        ),
        in_specs=[ANY, VMEM, VMEM, VMEM, VMEM],
        out_specs=(VMEM, VMEM),
        scratch_shapes=[
            pltpu.VMEM((2, height, 2 * blk), f32),
            DMA((2,)),
            DMA((2, chips * rows)),
            DMA((2, chips * (rows - 1))),
            DMA((2, chips - 1)),
            *AllReduce.scratch(rank, acts.shape[1], rows, chips),
        ],
        compiler_params=pltpu.CompilerParams(
            collective_id=collective_id, has_side_effects=True, vmem_limit_bytes=vmem_bytes
        ),
        name="project",
    )(accumulated, basis, turned, grads, acts)


def orthogonal_kernel(rows, cols, step, power_ref, out_ref, turned_ref, gram, rest, *reduce_scratch):
    g = Grid(rows, cols)
    g.greet()
    part, full, *others = reduce_scratch
    rank = gram.shape[0]
    count = rank // step
    product = mul(power_ref[...], power_ref[...], cols_cols, highest)
    across = part.shape[1] // step
    lower_blocks = [(i, j) for i in range(count) for j in range(i + 1)]

    def cut(n):
        return slice(n * step, (n + 1) * step)

    for n in range(count * across):
        i, j = lower_blocks[n] if n < len(lower_blocks) else (0, 0)
        part[cut(n // across), cut(n % across)] = product[cut(i), cut(j)]
    total = AllReduce(g, part, full, *others)
    for phase in total.phases:
        phase()
    rest[...] = power_ref[...]
    for n, (i, j) in enumerate(lower_blocks):
        gram[cut(i), cut(j)] = full[cut(n // across), cut(n % across)]
        if i > j:
            gram[cut(j), cut(i)] = jnp.zeros((step, step), f32)
    part_step = step // 2
    lanes = lax.broadcasted_iota(jnp.int32, (part_step, part_step), 1)
    lines = lax.broadcasted_iota(jnp.int32, (part_step, part_step), 0)
    eights = lax.broadcasted_iota(jnp.int32, (8, step), 0)

    def invert(block):
        both = jnp.concatenate([block, (lanes == lines).astype(f32)], axis=1)
        parts = [both[8 * i : 8 * i + 8] for i in range(part_step // 8)]
        for n in range(0, part_step, 2):
            q, o = n // 8, n % 8
            wide = (8, step)
            first = jnp.broadcast_to(parts[q][:, n : n + 1], wide)
            second = jnp.broadcast_to(parts[q][:, n + 1 : n + 2], wide)
            row_a = jnp.broadcast_to(parts[q][o : o + 1], wide)
            row_b = jnp.broadcast_to(parts[q][o + 1 : o + 2], wide)
            aa = jnp.broadcast_to(first[o : o + 1], wide)
            ab = jnp.broadcast_to(first[o + 1 : o + 2], wide)
            bb = jnp.broadcast_to(second[o + 1 : o + 2], wide)
            scale = 1.0 / (aa * bb - ab * ab)
            take_a = (row_a * bb - row_b * ab) * scale
            take_b = (row_b * aa - row_a * ab) * scale
            if o < 6:
                later = eights > o + 1
                parts[q] = (
                    parts[q]
                    - jnp.where(later, first, 0.0) * take_a
                    - jnp.where(later, second, 0.0) * take_b
                )
            for i in range(q + 1, part_step // 8):
                parts[i] = (
                    parts[i]
                    - parts[i][:, n : n + 1] * take_a
                    - parts[i][:, n + 1 : n + 2] * take_b
                )
        both = jnp.concatenate(parts, axis=0)
        left, right = both[:, :part_step], both[:, part_step:]
        odd = lines % 2 == 1
        diagonal = jnp.sum(jnp.where(lanes == lines, left, 0.0), axis=1, keepdims=True)
        side = jnp.sum(
            jnp.where(odd & (lanes == lines - 1), left, 0.0), axis=1, keepdims=True
        )
        diagonal = jnp.broadcast_to(diagonal, left.shape)
        side = jnp.broadcast_to(side, left.shape)
        ratio = jnp.where(odd, side / pltpu.roll(diagonal, 1, 0), 0.0)
        right = right - ratio * pltpu.roll(right, 1, 0)
        return right * lax.rsqrt(diagonal - ratio * side)

    def eliminate(j, carry):
        at = pl.ds(pl.multiple_of(j * step, step), step)
        block = gram[at, at]
        first = invert(block[:part_step, :part_step])
        link = mul(block[part_step:, :part_step], first, cols_cols, highest)
        second = invert(block[part_step:, part_step:] - mul(link, link, cols_cols, highest))
        below = -mul(second, mul(link, first, rows_cols, highest), rows_cols, highest)
        above = jnp.zeros_like(below)
        inverse = jnp.concatenate(
            [jnp.concatenate([first, above], axis=1), jnp.concatenate([below, second], axis=1)],
            axis=0,
        )
        panel = mul(gram[:, at], inverse, cols_cols, highest)
        below = lax.broadcasted_iota(jnp.int32, panel.shape, 0) >= (j + 1) * step
        panel = jnp.where(below, panel, 0.0)
        gram[...] -= mul(panel, panel, cols_cols, highest)
        solved = mul(inverse, rest[at], rows_cols, highest)
        rest[...] -= mul(panel, solved, rows_cols, highest)
        turned_ref[at] = solved.astype(bf16)
        return carry

    lax.fori_loop(0, rank // step, eliminate, 0)
    out_ref[...] = turned_ref[...].astype(f32).T.astype(bf16)
    total.drain()


def orthogonal(power_turned, rows, cols, collective_id):
    rank, blk = power_turned.shape
    blocks = rank // 128
    return pl.pallas_call(
        functools.partial(orthogonal_kernel, rows, cols, 128),
        out_shape=(
            jax.ShapeDtypeStruct((blk, rank), bf16),
            jax.ShapeDtypeStruct((rank, blk), bf16),
        ),
        in_specs=[VMEM],
        out_specs=(VMEM, VMEM),
        scratch_shapes=[
            pltpu.VMEM((rank, rank), f32),
            pltpu.VMEM((rank, blk), f32),
            *AllReduce.scratch(rank, 128 * -(-blocks * (blocks + 1) // (2 * blocks)), rows, cols // 2),
        ],
        compiler_params=pltpu.CompilerParams(
            collective_id=collective_id, has_side_effects=True, vmem_limit_bytes=vmem_bytes
        ),
        name="orthogonal",
    )(power_turned)


def solve_lower(gram_matrix, right):
    rank = gram_matrix.shape[0]
    step = 128 if rank % 128 == 0 else rank
    count = rank // step
    cut = lambda n: slice(n * step, (n + 1) * step)
    trailing = {
        (i, j): gram_matrix[cut(i), cut(j)] for i in range(count) for j in range(i + 1)
    }
    rests = [right[cut(i)] for i in range(count)]
    solved = []
    for j in range(count):
        factor = lax.linalg.cholesky(trailing[j, j], symmetrize_input=False)
        inverse = jax.scipy.linalg.solve_triangular(
            factor, jnp.eye(step, dtype=jnp.float32), lower=True
        )
        panel = {
            i: mul(trailing[i, j], inverse, cols_cols, highest) for i in range(j + 1, count)
        }
        solved.append(mul(inverse, rests[j], rows_cols, highest))
        for i in range(j + 1, count):
            rests[i] = rests[i] - mul(panel[i], solved[j], rows_cols, highest)
            for k in range(j + 1, i + 1):
                trailing[i, k] = trailing[i, k] - mul(panel[i], panel[k], cols_cols, highest)
    return jnp.concatenate(solved, axis=0)


def finish(moment_first, moment_second, projected, full_basis):
    first_next = beta_first * moment_first + (1.0 - beta_first) * projected
    second_next = beta_second * moment_second + (1.0 - beta_second) * projected * projected
    direction = (
        first_next / correct_first / (jnp.sqrt(second_next / correct_second) + epsilon_value)
    )
    lifted = lift_scale * mul(direction.astype(bf16), full_basis, cols_cols)
    return first_next, second_next, lifted


def plain_body(activations, out_grads, accumulated, seed_basis, moment_first, moment_second):
    share_rows = activations.shape[0]
    acts = activations.astype(jnp.float32)
    grads = out_grads.astype(jnp.float32)
    own_seed = lax.dynamic_slice_in_dim(
        seed_basis, lax.axis_index("col") * share_rows, share_rows, 0
    )
    full_seed = lax.all_gather(own_seed, every, axis=0, tiled=True)
    seed_tokens = lax.psum(mul(acts, own_seed, rows_rows, highest), every)
    image_rows = mul(accumulated, full_seed, rows_cols, high) + mul(
        grads, seed_tokens, rows_cols, high
    )
    image_tokens = lax.psum(mul(grads, image_rows, rows_rows, high), every)
    power_part = mul(accumulated, image_rows, rows_rows, high)
    power_rows = lax.psum_scatter(
        power_part, every, scatter_dimension=0, tiled=True
    ) + mul(acts, image_tokens, rows_cols, highest)
    gram_matrix = lax.psum(mul(power_rows, power_rows, rows_rows, highest), every)
    gram_matrix, held_acts = lax.optimization_barrier((gram_matrix, activations))
    full_acts = lax.all_gather(held_acts, every, axis=0, tiled=True)
    solved = solve_lower(gram_matrix, power_rows.T)
    basis_rows = solved.T.astype(jnp.bfloat16)
    sent_rows, full_acts = lax.optimization_barrier((basis_rows, full_acts))
    full_basis = lax.all_gather(sent_rows, every, axis=0, tiled=True)
    basis_tokens = mul(full_acts, full_basis, rows_rows)
    projected = mul(accumulated.astype(jnp.bfloat16), full_basis, rows_cols) + mul(
        grads, basis_tokens, rows_cols, high
    )
    return (basis_rows, *finish(moment_first, moment_second, projected, full_basis))


def body(rows, cols, activations, out_grads, accumulated, seed_basis, moment_first, moment_second):
    common = (out_grads, activations, rows, cols)
    pair = image_pair(accumulated, seed_basis, *common, 1)
    power_turned = power_scatter(accumulated, pair, *common, 2)
    basis_rows, turned = orthogonal(power_turned, rows, cols, 3)
    projected, full_basis = project(accumulated, basis_rows, turned, *common, 4)
    return (basis_rows, *finish(moment_first, moment_second, projected, full_basis))


def solution(mesh):
    rows, cols = mesh.shape["row"], mesh.shape["col"]

    def place(activations, *others):
        rank = others[2].shape[1]
        fits = rows & (rows - 1) == 0 and rows > 1 and cols % 2 == 0 and cols > 2
        fits = fits and activations.shape[0] % 128 == 0 and rank % (8 * rows * cols) == 0
        fits = fits and rank % 128 == 0 and 256 % (16 * cols // 2) == 0
        if fits:
            return body(rows, cols, activations, *others)
        return plain_body(activations, *others)

    split_rows = P(("row", "col"), None)
    in_specs = (split_rows, split_rows, split_rows, P("row", None), split_rows, split_rows)
    return jax.shard_map(
        place, mesh=mesh, in_specs=in_specs, out_specs=(split_rows,) * 4, check_vma=False
    )
```

```python
import functools

import jax
import jax.numpy as jnp
from jax import lax
from jax.experimental import pallas as pl
from jax.experimental.pallas import tpu as pltpu
from jax.sharding import PartitionSpec as P

beta_first = 0.9
beta_second = 0.99
correct_first = 1.0 - 0.9**10
correct_second = 1.0 - 0.99**10
epsilon_value = 1e-08
lift_scale = 8.0

every = ("row", "col")
highest = lax.Precision.HIGHEST
high = lax.Precision.HIGH
bf16 = jnp.bfloat16
f32 = jnp.float32
MESH = pl.DeviceIdType.MESH
ANY = pl.BlockSpec(memory_space=pl.ANY)
VMEM = pl.BlockSpec(memory_space=pltpu.VMEM)
DMA = pltpu.SemaphoreType.DMA
vmem_bytes = 63 * 2**20
image_gather = 4
image_ticks = (1, 0, 2, 2, 1, 1)
power_group = 2
power_lag, power_gap, power_ticks = 7, 4, (1, 3, 5, 7, 9, 11, 13, 15, 16)


def mul(left, right, dims, precision=None):
    return lax.dot_general(
        left, right, (dims, ((), ())), precision=precision, preferred_element_type=jnp.float32
    )


rows_cols = ((1,), (0,))
rows_rows = ((0,), (0,))
cols_cols = ((1,), (1,))


def split(value):
    upper = value.astype(bf16)
    return upper, (value - upper.astype(f32)).astype(bf16)


class Grid:
    def __init__(self, rows, cols):
        self.rows, self.chips = rows, cols // 2
        self.stages = rows.bit_length() - 1
        self.r = lax.axis_index("row")
        c = lax.axis_index("col")
        self.z, self.k = c // 2, c % 2
        self.c = c
        self.partner = (self.r, self.z * 2 + 1 - self.k)
        n = self.chips
        self.offsets = sorted(range(1, n), key=lambda d: -min(d, n - d))

    def flip(self, bit):
        return self.r + bit * (1 - 2 * ((self.r // bit) % 2))

    def peer_row(self, s, k=None):
        k = self.k if k is None else k
        low, high_bit = 2**s, 2 ** (self.stages - 1 - s)
        return (1 - k) * self.flip(low) + k * self.flip(high_bit)

    def peer(self, s):
        return (self.peer_row(s), self.c)

    def count(self, s):
        return 2 ** (self.stages - 1 - s)

    def block(self, s, j, base, k=None):
        k = self.k if k is None else k
        n = self.count(s)
        first = base % 2 ** (s + 1) + j * 2 ** (s + 1)
        second = (base // n) * n + j
        return (1 - k) * first + k * second

    def chip(self, w, far_first=False):
        n, step = self.chips, self.offsets[w] if far_first else w + 1
        return (self.z + step) % n, (self.z + n - step) % n

    def chip_device(self, z):
        return (self.r, z * 2 + self.k)

    def greet(self):
        barrier = pltpu.get_barrier_semaphore()
        peers = [self.partner]
        peers += [self.peer(s) for s in range(self.stages)]
        peers += [self.chip_device(self.chip(w)[0]) for w in range(self.chips - 1)]
        for peer in peers:
            pl.semaphore_signal(barrier, inc=1, device_id=peer, device_id_type=MESH)
        pl.semaphore_wait(barrier, len(peers))


def remote(source, target, send, recv, device):
    return pltpu.make_async_remote_copy(
        src_ref=source, dst_ref=target, send_sem=send, recv_sem=recv,
        device_id=device, device_id_type=MESH,
    )


class AllReduce:
    def __init__(self, grid, part, full, half_in, stage_in, chip_in, send, recv):
        self.g, self.part, self.full = grid, part, full
        self.half_in, self.stage_in, self.chip_in = half_in, stage_in, chip_in
        self.send, self.recv = send, recv
        self.half = part.shape[0] // 2
        self.chunk = self.half // grid.rows
        self.unit = self.chunk // grid.chips
        self.pending = []
        self.used = 0
        self.phases = (
            [self.pair_out]
            + [functools.partial(self.halve, s) for s in range(grid.stages)]
            + [self.chips_out, self.chips_back]
            + [functools.partial(self.double, s) for s in reversed(range(grid.stages))]
            + [self.pair_back, self.finish]
        )
        self.arrived = []

    @staticmethod
    def scratch(rows, width, grid_rows, chips):
        half = rows // 2
        chunk = half // grid_rows
        stages = grid_rows.bit_length() - 1
        copies = 2 + 2 * (grid_rows - 1) + 2 * (chips - 1)
        return [
            pltpu.VMEM((rows, width), f32),
            pltpu.VMEM((rows, width), f32),
            pltpu.VMEM((half, width), f32),
            pltpu.VMEM((grid_rows - 1, chunk, width), f32),
            pltpu.VMEM((chips - 1, chunk // chips, width), f32),
            DMA((copies,)),
            DMA((copies,)),
        ]

    def start(self, source, target, device):
        i = self.used
        self.used += 1
        copy = remote(source, target, self.send.at[i], self.recv.at[i], device)
        copy.start()
        self.pending.append(copy)
        self.arrived.append(copy)

    def landed(self):
        arrived, self.arrived = self.arrived, []
        for copy in arrived:
            copy.wait_recv()

    def rows_of(self, r):
        return pl.ds(pl.multiple_of((self.g.k * self.g.rows + r) * self.chunk, self.chunk), self.chunk)

    def unit_of(self, r, z):
        at = ((self.g.k * self.g.rows + r) * self.g.chips + z) * self.unit
        return pl.ds(pl.multiple_of(at, self.unit), self.unit)

    def pair_out(self):
        g = self.g
        other = pl.ds(pl.multiple_of((1 - g.k) * self.half, self.half), self.half)
        self.start(self.part.at[other], self.half_in, g.partner)

    def stage_base(self, s):
        return self.g.rows - 2 ** (self.g.stages - s)

    def halve(self, s):
        g = self.g
        self.landed()
        if s == 0:
            mine = pl.ds(pl.multiple_of(g.k * self.half, self.half), self.half)
            self.part[mine] += self.half_in[...]
        else:
            self.take(s - 1)
        for j in range(g.count(s)):
            rows = self.rows_of(g.block(s, j, g.peer_row(s)))
            self.start(self.part.at[rows], self.stage_in.at[self.stage_base(s) + j], g.peer(s))

    def take(self, s):
        g = self.g
        for j in range(g.count(s)):
            self.part[self.rows_of(g.block(s, j, g.r))] += self.stage_in[self.stage_base(s) + j]

    def chips_out(self):
        g = self.g
        self.landed()
        self.take(g.stages - 1)
        for w in range(g.chips - 1):
            z = g.chip(w)[0]
            self.start(self.part.at[self.unit_of(g.r, z)], self.chip_in.at[w], g.chip_device(z))

    def chips_back(self):
        g = self.g
        self.landed()
        own = self.unit_of(g.r, g.z)
        total = self.part[own]
        for w in range(g.chips - 1):
            total = total + self.chip_in[w]
        self.full[own] = total
        for w in range(g.chips - 1):
            self.start(self.full.at[own], self.full.at[own], g.chip_device(g.chip(w)[0]))

    def double(self, s):
        g = self.g
        self.landed()
        for j in range(g.count(s)):
            rows = self.rows_of(g.block(s, j, g.r))
            self.start(self.full.at[rows], self.full.at[rows], g.peer(s))

    def pair_back(self):
        g = self.g
        self.landed()
        mine = pl.ds(pl.multiple_of(g.k * self.half, self.half), self.half)
        self.start(self.full.at[mine], self.full.at[mine], g.partner)

    def finish(self):
        self.landed()

    def drain(self):
        for copy in self.pending:
            copy.wait_send()


class ChipsFirst(AllReduce):
    def __init__(self, grid, *refs):
        super().__init__(grid, *refs)
        self.chunk = self.half // grid.chips
        self.unit = self.chunk // grid.rows
        self.phases = (
            [self.pair_out, self.chips_out]
            + [functools.partial(self.halve, s) for s in range(grid.stages)]
            + [functools.partial(self.double, s) for s in reversed(range(grid.stages))]
            + [self.chips_back, self.pair_back, self.finish]
        )

    @staticmethod
    def scratch(rows, width, grid_rows, chips):
        shapes = AllReduce.scratch(rows, width, grid_rows, chips)
        half = rows // 2
        unit = half // (chips * grid_rows)
        shapes[3] = pltpu.VMEM((grid_rows - 1, unit, width), f32)
        shapes[4] = pltpu.VMEM((chips - 1, half // chips, width), f32)
        return shapes

    def rows_of(self, r):
        at = ((self.g.k * self.g.chips + self.g.z) * self.g.rows + r) * self.unit
        return pl.ds(pl.multiple_of(at, self.unit), self.unit)

    def chunk_of(self, z):
        at = (self.g.k * self.g.chips + z) * self.chunk
        return pl.ds(pl.multiple_of(at, self.chunk), self.chunk)

    def chips_out(self):
        g = self.g
        self.landed()
        mine = pl.ds(pl.multiple_of(g.k * self.half, self.half), self.half)
        self.part[mine] += self.half_in[...]
        for w in range(g.chips - 1):
            z = g.chip(w)[0]
            self.start(self.part.at[self.chunk_of(z)], self.chip_in.at[w], g.chip_device(z))

    def halve(self, s):
        g = self.g
        self.landed()
        if s == 0:
            own = self.chunk_of(g.z)
            total = self.part[own]
            for w in range(g.chips - 1):
                total = total + self.chip_in[w]
            self.part[own] = total
        else:
            self.take(s - 1)
        for j in range(g.count(s)):
            rows = self.rows_of(g.block(s, j, g.peer_row(s)))
            self.start(self.part.at[rows], self.stage_in.at[self.stage_base(s) + j], g.peer(s))

    def double(self, s):
        g = self.g
        if s == g.stages - 1:
            self.landed()
            self.take(s)
            self.full[self.rows_of(g.r)] = self.part[self.rows_of(g.r)]
        super().double(s)

    def chips_back(self):
        g = self.g
        self.landed()
        own = self.chunk_of(g.z)
        for w in range(g.chips - 1):
            self.start(self.full.at[own], self.full.at[own], g.chip_device(g.chip(w)[0]))


def reduce_kernel(rows, cols, part_ref, out_ref, *scratch):
    grid = Grid(rows, cols)
    grid.greet()
    part, full, *rest = scratch
    part[...] = part_ref[...]
    total = AllReduce(grid, part, full, *rest)
    for phase in total.phases:
        phase()
    out_ref[...] = full[...]
    total.drain()


def all_reduce(value, rows, cols, collective_id):
    return pl.pallas_call(
        functools.partial(reduce_kernel, rows, cols),
        out_shape=jax.ShapeDtypeStruct(value.shape, f32),
        in_specs=[VMEM],
        out_specs=VMEM,
        scratch_shapes=AllReduce.scratch(*value.shape, rows, cols // 2),
        compiler_params=pltpu.CompilerParams(
            collective_id=collective_id, has_side_effects=True, vmem_limit_bytes=vmem_bytes
        ),
        name="all_reduce",
    )(value)


def power_kernel(
    rows, cols, acc, pair_ref, grads_ref, acts_ref, out_ref,
    tiles, held, pair_in, stage_in, chip_in,
    tile_sem, pair_sems, stage_sems, chip_sems, *reduce_scratch,
):
    g = Grid(rows, cols)
    blk = acts_ref.shape[0]
    rank = out_ref.shape[0]
    chips, stages = g.chips, g.stages

    half = g.count(0)

    def chip_of(w):
        if isinstance(w, int):
            return g.chip(w, True)[0] if w < chips - 1 else g.z
        far = g.z
        for i, step in enumerate(g.offsets):
            far = jnp.where(w == i, (g.z + step) % chips, far)
        return far

    mine = chips * rows

    def core_of(kind):
        return 1 - g.k + kind * (2 * g.k - 1)

    def block_of(t, kind=1):
        w, i = t // rows, t % rows
        core = core_of(kind)
        return w, g.block(0, i % half, jnp.where(i < half, g.peer_row(0, core), g.r), core)

    def fetch(t, kind):
        w, rp = block_of(t, kind)
        core = core_of(kind)
        at = ((rp * chips + chip_of(w)) * 2 + core) * blk
        columns = pl.ds(pl.multiple_of(at, blk), blk)
        slot = kind * 2 + t % 2
        return pltpu.make_async_copy(acc.at[:, columns], tiles.at[slot], tile_sem.at[slot])

    for t in range(2):
        fetch(t, 0).start()
        fetch(t, 1).start()
    g.greet()

    def product(slot):
        upper, lower = split(tiles[slot])
        both = mul(pair_ref[...], upper, rows_cols)
        return both[:rank] + both[rank:] + mul(pair_ref[:rank], lower, rows_cols)

    def pair_copy(w, rp):
        i = w * rows + rp
        return remote(held.at[i], pair_in.at[i], pair_sems.at[0, i], pair_sems.at[1, i], g.partner)

    def stage_copy(w, s, j):
        i = w * (rows - 1) + rows - 2 ** (stages - s) + j
        source = held.at[mine + w * rows + g.block(s, j, g.peer_row(s))]
        return remote(source, stage_in.at[i], stage_sems.at[0, i], stage_sems.at[1, i], g.peer(s))

    def chip_copy(w):
        return remote(
            held.at[mine + w * rows + g.r], chip_in.at[w], chip_sems.at[0, w], chip_sems.at[1, w],
            g.chip_device(chip_of(w)),
        )

    def compute(t):
        def one(kind, carry):
            w, rp = block_of(t, kind)
            fetch(t, kind).wait()
            held[kind * mine + w * rows + rp] = product(kind * 2 + t % 2)

            @pl.when(kind == 0)
            def _():
                pair_copy(w, rp).start()

            @pl.when(t + 2 < chips * rows)
            def _():
                fetch(t + 2, kind).start()

            return carry

        lax.fori_loop(0, 2, one, 0)

    def pair(t):
        w, rp = block_of(t)
        pair_copy(w, rp).wait_recv()
        held[mine + w * rows + rp] += pair_in[w * rows + rp]

        @pl.when(t % rows < half)
        def _():
            stage_copy(w, 0, t % rows).start()

    def halve(w, s):
        for j in range(g.count(s - 1)):
            i = w * (rows - 1) + rows - 2 ** (stages - s + 1) + j
            stage_copy(w, s - 1, j).wait_recv()
            held[mine + w * rows + g.block(s - 1, j, g.r)] += stage_in[i]
        for j in range(g.count(s)):
            stage_copy(w, s, j).start()

    def leave(w):
        i = w * (rows - 1) + rows - 2
        stage_copy(w, stages - 1, 0).wait_recv()
        held[mine + w * rows + g.r] += stage_in[i]
        if w < chips - 1:
            chip_copy(w).start()

    part, full, *rest = reduce_scratch

    part[...] = mul(pair_ref[:rank], grads_ref[...], rows_cols) + mul(
        pair_ref[rank:], grads_ref[...], rows_cols
    )
    tokens = AllReduce(g, part, full, *rest)
    phases = iter(tokens.phases)

    def tick():
        phase = next(phases, None)
        if phase is not None:
            phase()

    tick()
    steps = chips * rows
    lag, gap, ticks = power_lag, power_gap, power_ticks
    later = {}
    for w in range(chips):
        for s in range(1, stages):
            later.setdefault(min(lag + gap * w + 3 * (s - 1), steps + 2 * w + s), []).append(
                functools.partial(halve, w, s)
            )
    for w in range(chips):
        later.setdefault(min(lag + gap * w + gap, steps + 2 * w + 3), []).append(
            functools.partial(leave, w)
        )
    def both(t, carry):
        compute(t)

        @pl.when(t > 0)
        def _():
            pair(t - 1)

        return carry

    for t in range(0, max(max(later), steps) + power_group, power_group):
        for _ in range(sum(t <= at < t + power_group for at in ticks)):
            tick()
        if t < steps:
            lax.fori_loop(t, min(steps, t + power_group), both, 0)
        if steps <= t < steps + power_group:
            pair(steps - 1)
        for at in range(t, t + power_group):
            for event in later.get(at, ()):
                event()
    for phase in phases:
        phase()
    upper, lower = split(full[...])
    total = mul(upper, acts_ref[...], cols_cols) + mul(lower, acts_ref[...], cols_cols)
    total = total + held[mine + (chips - 1) * rows + g.r]
    for w in range(chips - 1):
        chip_copy(w).wait_recv()
        total = total + chip_in[w]
    out_ref[...] = total

    tokens.drain()
    for w in range(chips):
        def done(rp, carry):
            pair_copy(w, rp).wait_send()
            return carry

        lax.fori_loop(0, rows, done, 0)
        for s in range(stages):
            for j in range(g.count(s)):
                stage_copy(w, s, j).wait_send()
        if w < chips - 1:
            chip_copy(w).wait_send()


def power_scatter(accumulated, pair, grads, acts, rows, cols, collective_id):
    rank = pair.shape[0] // 2
    blk = acts.shape[0]
    chips = cols // 2
    blocks = chips * rows
    passed = chips * (rows - 1)
    return pl.pallas_call(
        functools.partial(power_kernel, rows, cols),
        out_shape=jax.ShapeDtypeStruct((rank, blk), f32),
        in_specs=[ANY, VMEM, VMEM, VMEM],
        out_specs=VMEM,
        scratch_shapes=[
            pltpu.VMEM((4, accumulated.shape[0], blk), f32),
            pltpu.VMEM((2 * blocks, rank, blk), f32),
            pltpu.VMEM((blocks, rank, blk), f32),
            pltpu.VMEM((passed, rank, blk), f32),
            pltpu.VMEM((chips - 1, rank, blk), f32),
            DMA((4,)),
            DMA((2, blocks)),
            DMA((2, passed)),
            DMA((2, chips - 1)),
            *AllReduce.scratch(rank, acts.shape[1], rows, chips),
        ],
        compiler_params=pltpu.CompilerParams(
            collective_id=collective_id, has_side_effects=True, vmem_limit_bytes=vmem_bytes
        ),
        name="power_scatter",
    )(accumulated, pair, grads, acts)


class Interleaved:
    def __init__(self, phases):
        self.left = list(phases)

    def tick(self, count=1):
        for _ in range(count):
            if self.left:
                self.left.pop(0)()

    def rest(self):
        self.tick(len(self.left))


def image_kernel(
    rows, cols, acc, seed_ref, grads_ref, acts_ref, out_ref,
    tiles, image, seeds, tile_sem, pair_sems, stage_sems, share_sems, *reduce_scratch,
):
    g = Grid(rows, cols)
    stages = g.stages
    blk, rank = seeds.shape[2], seeds.shape[3]
    own_rows = seed_ref.shape[0]
    pieces = own_rows // (2 * blk)
    tokens_rows = acts_ref.shape[0]

    def piece(rp, h, i):
        return (rp * 2 + h) * pieces + i

    def fetch(p, slot):
        columns = pl.ds(pl.multiple_of(p * blk, blk), blk)
        return pltpu.make_async_copy(acc.at[:, columns], tiles.at[slot], tile_sem.at[slot])

    def order(t):
        u = t - 2 * pieces
        wave = u // (2 * (rows - 1))
        inner = u % (2 * (rows - 1))
        other = piece((g.r + 1 + inner // 2) % rows, inner % 2, (wave + 1) % pieces)
        own = piece(g.r, t // pieces, t % pieces)
        return jnp.where(t < 2 * pieces, own, other)

    count = 2 * pieces * rows
    depth = tiles.shape[0]
    for t in range(depth - 1):
        fetch(order(t), t).start()
    g.greet()

    def spread(q):
        at = pl.ds(pl.multiple_of(q * blk, blk), blk)
        upper, lower = split(seed_ref[at])
        target = g.r * 2 * pieces + q
        seeds[target, 0] = upper
        seeds[target, 1] = lower

    share = blk // g.chips

    def shared(p, z):
        return seeds.at[p, :, pl.ds(pl.multiple_of(z * share, share), share)]

    def share_copy(s, j, w, z):
        at = (rows - 2 ** (stages - s) + j) * (g.chips - 1) + w
        ref = shared(piece(g.block(s, j, g.peer_row(s)), g.k, 0), z)
        device = g.chip_device(g.chip(w)[0])
        return remote(ref, ref, share_sems.at[0, at], share_sems.at[1, at], device)

    def pair_copy(rp, i):
        p = piece(rp, g.k, i)
        at = i * rows + rp
        return remote(seeds.at[p], seeds.at[p], pair_sems.at[0, at], pair_sems.at[1, at], g.partner)

    def pair_wait(rp, i):
        at = i * rows + rp
        p = piece(rp, 1 - g.k, i)
        remote(seeds.at[p], seeds.at[p], pair_sems.at[0, at], pair_sems.at[1, at], g.partner).wait_recv()

    def stage_copy(i, s, j, base):
        at = i * (rows - 1) + rows - 2 ** (stages - s) + j
        p = piece(g.block(s, j, base), g.k, i)
        ref = seeds.at[p] if i else shared(p, g.z)
        return remote(ref, ref, stage_sems.at[0, at], stage_sems.at[1, at], g.peer(s))

    def send(i, s):
        for j in range(g.count(s)):
            stage_copy(i, s, j, g.r).start()

    def land(i, s):
        for j in range(g.count(s)):
            stage_copy(i, s, j, g.peer_row(s)).wait_recv()
            if i:
                pair_copy(g.block(s, j, g.peer_row(s)), i).start()
            else:
                for w in range(g.chips - 1):
                    share_copy(s, j, w, g.z).start()

    def gather():
        for s in reversed(range(stages)):
            for j in range(g.count(s)):
                for w in range(g.chips - 1):
                    share_copy(s, j, w, g.chip(w)[1]).wait_recv()
                pair_copy(g.block(s, j, g.peer_row(s)), 0).start()

    def compute(t):
        slot = t % depth
        p = order(t)
        fetch(p, slot).wait()

        @pl.when(t + depth - 1 < count)
        def _():
            fetch(order(t + depth - 1), (t + depth - 1) % depth).start()

        upper, lower = split(tiles[slot])
        image[...] += (
            mul(upper, seeds[p, 0], rows_cols)
            + mul(lower, seeds[p, 0], rows_cols)
            + mul(upper, seeds[p, 1], rows_cols)
        )

    def own_step(t, carry):
        compute(t)
        return carry

    def other_step(t, carry):
        inner = (t - 2 * pieces) % (2 * (rows - 1))
        wave = (t - 2 * pieces) // (2 * (rows - 1))
        rp = (g.r + 1 + inner // 2) % rows

        @pl.when(inner % 2 == 1 - g.k)
        def _():
            pair_wait(rp, (wave + 1) % pieces)

        compute(t)
        return carry

    for i in range(pieces):
        spread(g.k * pieces + i)
        send(i, stages - 1)
    own = pl.ds(pl.multiple_of(g.c * tokens_rows, tokens_rows), tokens_rows)
    turned = seed_ref[own].T
    part, full, *rest = reduce_scratch
    upper, lower = split(turned)
    part[...] = mul(upper, acts_ref[...], rows_cols) + mul(lower, acts_ref[...], rows_cols)
    tokens = ChipsFirst(g, part, full, *rest)
    small = Interleaved(tokens.phases)
    small.tick()

    def spread_other(i, carry):
        spread((1 - g.k) * pieces + i)
        return carry

    lax.fori_loop(0, pieces, spread_other, 0)
    image[...] = jnp.zeros_like(image)
    first = 2 * pieces // (stages + 1)
    done = 0
    lag = stages
    for at in range(pieces + lag):
        small.tick(image_ticks[at] if at < len(image_ticks) else 1)
        for late in range(stages):
            i = at - late
            if 0 <= i < pieces:
                s = stages - 1 - late
                land(i, s)
                if s > 0:
                    send(i, s - 1)
        if at == image_gather:
            gather()
        if done < 2 * pieces:
            stop = min(2 * pieces, done + first)
            lax.fori_loop(done, stop, own_step, 0)
            done = stop
        i = at - lag
        if 0 <= i < pieces:
            lax.fori_loop(done, 2 * pieces, own_step, 0)
            done = 2 * pieces
            start = 2 * pieces + i * 2 * (rows - 1)
            lax.fori_loop(start, start + 2 * (rows - 1), other_step, 0)
    small.rest()
    upper, lower = split(full[...])
    total = image[...] + mul(grads_ref[...], upper, cols_cols) + mul(grads_ref[...], lower, cols_cols)
    upper, lower = split(total.T)
    out_ref[:rank] = upper
    out_ref[rank:] = lower

    tokens.drain()
    for i in range(pieces):
        for s in range(stages):
            for j in range(g.count(s)):
                stage_copy(i, s, j, g.r).wait_send()
                pair_copy(g.block(s, j, g.peer_row(s)), i).wait_send()
    for s in range(stages):
        for j in range(g.count(s)):
            for w in range(g.chips - 1):
                share_copy(s, j, w, g.z).wait_send()


def image_pair(accumulated, seed, grads, acts, rows, cols, collective_id):
    rank = seed.shape[1]
    height, width = accumulated.shape
    blk = 256 if seed.shape[0] % 512 == 0 else seed.shape[0] // 2
    total = width // blk
    pieces = total // (2 * rows)
    return pl.pallas_call(
        functools.partial(image_kernel, rows, cols),
        out_shape=jax.ShapeDtypeStruct((2 * rank, height), bf16),
        in_specs=[ANY, VMEM, VMEM, VMEM],
        out_specs=VMEM,
        scratch_shapes=[
            pltpu.VMEM((4, height, blk), f32),
            pltpu.VMEM((height, rank), f32),
            pltpu.VMEM((total, 2, blk, rank), bf16),
            DMA((4,)),
            DMA((2, pieces * rows)),
            DMA((2, pieces * (rows - 1))),
            DMA((2, (cols // 2 - 1) * (rows - 1))),
            *ChipsFirst.scratch(rank, acts.shape[1], rows, cols // 2),
        ],
        compiler_params=pltpu.CompilerParams(
            collective_id=collective_id, has_side_effects=True, vmem_limit_bytes=vmem_bytes
        ),
        name="image_pair",
    )(accumulated, seed, grads, acts)


def project_kernel(
    rows, cols, acc, basis_ref, turned_ref, grads_ref, acts_ref, out_ref, full_ref,
    tiles, tile_sem, pair_sems, stage_sems, chip_sems, *reduce_scratch,
):
    g = Grid(rows, cols)
    chips, stages = g.chips, g.stages
    blk = basis_ref.shape[0]
    count = chips * rows

    def chip_of(w):
        return (g.z + chips - w) % chips

    def at_of(rp, w, core):
        at = ((rp * chips + chip_of(w)) * 2 + core) * blk
        return full_ref.at[pl.ds(pl.multiple_of(at, blk), blk)]

    def fetch(t):
        w, rp = t // rows, t % rows
        at = (rp * chips + chip_of(w)) * 2 * blk
        columns = pl.ds(pl.multiple_of(at, 2 * blk), 2 * blk)
        return pltpu.make_async_copy(acc.at[:, columns], tiles.at[t % 2], tile_sem.at[t % 2])

    fetch(0).start()
    fetch(1).start()
    g.greet()
    own_rows = pl.ds(pl.multiple_of(((g.r * chips + g.z) * 2 + g.k) * blk, blk), blk)
    full_ref[own_rows] = basis_ref[...]

    def pair_copy(rp, w):
        i = w * rows + rp
        ref = at_of(rp, w, g.k)
        return remote(ref, ref, pair_sems.at[0, i], pair_sems.at[1, i], g.partner)

    def pair_wait(rp, w):
        i = w * rows + rp
        ref = at_of(rp, w, 1 - g.k)
        remote(ref, ref, pair_sems.at[0, i], pair_sems.at[1, i], g.partner).wait_recv()

    def stage_copy(w, s, j, base):
        i = w * (rows - 1) + rows - 2 ** (stages - s) + j
        ref = at_of(g.block(s, j, base), w, g.k)
        return remote(ref, ref, stage_sems.at[0, i], stage_sems.at[1, i], g.peer(s))

    def chip_copy(w, z):
        at = ((g.r * chips + z) * 2 + g.k) * blk
        ref = full_ref.at[pl.ds(pl.multiple_of(at, blk), blk)]
        device = g.chip_device(g.chip(w)[0])
        return remote(ref, ref, chip_sems.at[0, w], chip_sems.at[1, w], device)

    def enter(w):
        if w > 0:
            chip_copy(w - 1, chip_of(w)).wait_recv()
        stage_copy(w, stages - 1, 0, g.r).start()
        pair_copy(g.r, w).start()

    def land(w, s):
        for j in range(g.count(s)):
            stage_copy(w, s, j, g.peer_row(s)).wait_recv()
        if s > 0:
            for j in range(g.count(s - 1)):
                stage_copy(w, s - 1, j, g.r).start()
        for j in range(g.count(s)):
            pair_copy(g.block(s, j, g.peer_row(s)), w).start()

    for w in range(chips - 1):
        chip_copy(w, g.z).start()
    part, full, *rest = reduce_scratch
    enter(0)
    part[...] = mul(turned_ref[...], acts_ref[...], rows_cols)
    tokens = AllReduce(g, part, full, *rest)
    small = Interleaved(tokens.phases)
    small.tick()
    out_ref[...] = jnp.zeros_like(out_ref)

    def step(t, carry):
        w, rp = t // rows, t % rows
        fetch(t).wait()
        pair_wait(rp, w)
        at = (rp * chips + chip_of(w)) * 2 * blk
        block = full_ref[pl.ds(pl.multiple_of(at, 2 * blk), 2 * blk)]
        out_ref[...] += mul(tiles[t % 2].astype(bf16), block, rows_cols)

        @pl.when(t + 2 < count)
        def _():
            fetch(t + 2).start()

        return carry

    for at in range(chips + stages + 1):
        small.tick()
        for late in range(stages + 1):
            w = at - late
            if 0 <= w < chips:
                if late == 0:
                    if w > 0:
                        enter(w)
                else:
                    land(w, stages - late)
        w = at - stages
        if 0 <= w < chips:
            lax.fori_loop(w * rows, (w + 1) * rows, step, 0)
    small.rest()
    upper, lower = split(full[...])
    out_ref[...] += mul(grads_ref[...], upper, cols_cols) + mul(grads_ref[...], lower, cols_cols)

    tokens.drain()
    for w in range(chips - 1):
        chip_copy(w, g.z).wait_send()
    for w in range(chips):
        pair_copy(g.r, w).wait_send()
        for s in range(stages):
            for j in range(g.count(s)):
                stage_copy(w, s, j, g.r).wait_send()
                pair_copy(g.block(s, j, g.peer_row(s)), w).wait_send()


def project(accumulated, basis, turned, grads, acts, rows, cols, collective_id):
    height, width = accumulated.shape
    blk, rank = basis.shape
    chips = cols // 2
    return pl.pallas_call(
        functools.partial(project_kernel, rows, cols),
        out_shape=(
            jax.ShapeDtypeStruct((height, rank), f32),
            jax.ShapeDtypeStruct((width, rank), bf16),
        ),
        in_specs=[ANY, VMEM, VMEM, VMEM, VMEM],
        out_specs=(VMEM, VMEM),
        scratch_shapes=[
            pltpu.VMEM((2, height, 2 * blk), f32),
            DMA((2,)),
            DMA((2, chips * rows)),
            DMA((2, chips * (rows - 1))),
            DMA((2, chips - 1)),
            *AllReduce.scratch(rank, acts.shape[1], rows, chips),
        ],
        compiler_params=pltpu.CompilerParams(
            collective_id=collective_id, has_side_effects=True, vmem_limit_bytes=vmem_bytes
        ),
        name="project",
    )(accumulated, basis, turned, grads, acts)


def orthogonal_kernel(rows, cols, step, power_ref, out_ref, turned_ref, gram, rest, *reduce_scratch):
    g = Grid(rows, cols)
    g.greet()
    part, full, *others = reduce_scratch
    rank = gram.shape[0]
    count = rank // step
    product = mul(power_ref[...], power_ref[...], cols_cols, highest)
    across = part.shape[1] // step
    lower_blocks = [(i, j) for i in range(count) for j in range(i + 1)]

    def cut(n):
        return slice(n * step, (n + 1) * step)

    for n in range(count * across):
        i, j = lower_blocks[n] if n < len(lower_blocks) else (0, 0)
        part[cut(n // across), cut(n % across)] = product[cut(i), cut(j)]
    total = AllReduce(g, part, full, *others)
    for phase in total.phases:
        phase()
    rest[...] = power_ref[...]
    for n, (i, j) in enumerate(lower_blocks):
        gram[cut(i), cut(j)] = full[cut(n // across), cut(n % across)]
        if i > j:
            gram[cut(j), cut(i)] = jnp.zeros((step, step), f32)
    part_step = step // 2
    lanes = lax.broadcasted_iota(jnp.int32, (part_step, part_step), 1)
    lines = lax.broadcasted_iota(jnp.int32, (part_step, part_step), 0)
    eights = lax.broadcasted_iota(jnp.int32, (8, step), 0)

    def invert(block):
        both = jnp.concatenate([block, (lanes == lines).astype(f32)], axis=1)
        parts = [both[8 * i : 8 * i + 8] for i in range(part_step // 8)]
        for n in range(0, part_step, 2):
            q, o = n // 8, n % 8
            wide = (8, step)
            first = jnp.broadcast_to(parts[q][:, n : n + 1], wide)
            second = jnp.broadcast_to(parts[q][:, n + 1 : n + 2], wide)
            row_a = jnp.broadcast_to(parts[q][o : o + 1], wide)
            row_b = jnp.broadcast_to(parts[q][o + 1 : o + 2], wide)
            aa = jnp.broadcast_to(first[o : o + 1], wide)
            ab = jnp.broadcast_to(first[o + 1 : o + 2], wide)
            bb = jnp.broadcast_to(second[o + 1 : o + 2], wide)
            scale = 1.0 / (aa * bb - ab * ab)
            take_a = (row_a * bb - row_b * ab) * scale
            take_b = (row_b * aa - row_a * ab) * scale
            if o < 6:
                later = eights > o + 1
                parts[q] = (
                    parts[q]
                    - jnp.where(later, first, 0.0) * take_a
                    - jnp.where(later, second, 0.0) * take_b
                )
            for i in range(q + 1, part_step // 8):
                parts[i] = (
                    parts[i]
                    - parts[i][:, n : n + 1] * take_a
                    - parts[i][:, n + 1 : n + 2] * take_b
                )
        both = jnp.concatenate(parts, axis=0)
        left, right = both[:, :part_step], both[:, part_step:]
        odd = lines % 2 == 1
        diagonal = jnp.sum(jnp.where(lanes == lines, left, 0.0), axis=1, keepdims=True)
        side = jnp.sum(
            jnp.where(odd & (lanes == lines - 1), left, 0.0), axis=1, keepdims=True
        )
        diagonal = jnp.broadcast_to(diagonal, left.shape)
        side = jnp.broadcast_to(side, left.shape)
        ratio = jnp.where(odd, side / pltpu.roll(diagonal, 1, 0), 0.0)
        right = right - ratio * pltpu.roll(right, 1, 0)
        return right * lax.rsqrt(diagonal - ratio * side)

    def eliminate(j, carry):
        at = pl.ds(pl.multiple_of(j * step, step), step)
        block = gram[at, at]
        first = invert(block[:part_step, :part_step])
        link = mul(block[part_step:, :part_step], first, cols_cols, highest)
        second = invert(block[part_step:, part_step:] - mul(link, link, cols_cols, highest))
        below = -mul(second, mul(link, first, rows_cols, highest), rows_cols, highest)
        above = jnp.zeros_like(below)
        inverse = jnp.concatenate(
            [jnp.concatenate([first, above], axis=1), jnp.concatenate([below, second], axis=1)],
            axis=0,
        )
        panel = mul(gram[:, at], inverse, cols_cols, highest)
        below = lax.broadcasted_iota(jnp.int32, panel.shape, 0) >= (j + 1) * step
        panel = jnp.where(below, panel, 0.0)
        gram[...] -= mul(panel, panel, cols_cols, highest)
        solved = mul(inverse, rest[at], rows_cols, highest)
        rest[...] -= mul(panel, solved, rows_cols, highest)
        turned_ref[at] = solved.astype(bf16)
        return carry

    lax.fori_loop(0, rank // step, eliminate, 0)
    out_ref[...] = turned_ref[...].astype(f32).T.astype(bf16)
    total.drain()


def orthogonal(power_turned, rows, cols, collective_id):
    rank, blk = power_turned.shape
    blocks = rank // 128
    return pl.pallas_call(
        functools.partial(orthogonal_kernel, rows, cols, 128),
        out_shape=(
            jax.ShapeDtypeStruct((blk, rank), bf16),
            jax.ShapeDtypeStruct((rank, blk), bf16),
        ),
        in_specs=[VMEM],
        out_specs=(VMEM, VMEM),
        scratch_shapes=[
            pltpu.VMEM((rank, rank), f32),
            pltpu.VMEM((rank, blk), f32),
            *AllReduce.scratch(rank, 128 * -(-blocks * (blocks + 1) // (2 * blocks)), rows, cols // 2),
        ],
        compiler_params=pltpu.CompilerParams(
            collective_id=collective_id, has_side_effects=True, vmem_limit_bytes=vmem_bytes
        ),
        name="orthogonal",
    )(power_turned)


def solve_lower(gram_matrix, right):
    rank = gram_matrix.shape[0]
    step = 128 if rank % 128 == 0 else rank
    count = rank // step
    cut = lambda n: slice(n * step, (n + 1) * step)
    trailing = {
        (i, j): gram_matrix[cut(i), cut(j)] for i in range(count) for j in range(i + 1)
    }
    rests = [right[cut(i)] for i in range(count)]
    solved = []
    for j in range(count):
        factor = lax.linalg.cholesky(trailing[j, j], symmetrize_input=False)
        inverse = jax.scipy.linalg.solve_triangular(
            factor, jnp.eye(step, dtype=jnp.float32), lower=True
        )
        panel = {
            i: mul(trailing[i, j], inverse, cols_cols, highest) for i in range(j + 1, count)
        }
        solved.append(mul(inverse, rests[j], rows_cols, highest))
        for i in range(j + 1, count):
            rests[i] = rests[i] - mul(panel[i], solved[j], rows_cols, highest)
            for k in range(j + 1, i + 1):
                trailing[i, k] = trailing[i, k] - mul(panel[i], panel[k], cols_cols, highest)
    return jnp.concatenate(solved, axis=0)


def finish(moment_first, moment_second, projected, full_basis):
    first_next = beta_first * moment_first + (1.0 - beta_first) * projected
    second_next = beta_second * moment_second + (1.0 - beta_second) * projected * projected
    direction = (
        first_next / correct_first / (jnp.sqrt(second_next / correct_second) + epsilon_value)
    )
    lifted = lift_scale * mul(direction.astype(bf16), full_basis, cols_cols)
    return first_next, second_next, lifted


def plain_body(activations, out_grads, accumulated, seed_basis, moment_first, moment_second):
    share_rows = activations.shape[0]
    acts = activations.astype(jnp.float32)
    grads = out_grads.astype(jnp.float32)
    own_seed = lax.dynamic_slice_in_dim(
        seed_basis, lax.axis_index("col") * share_rows, share_rows, 0
    )
    full_seed = lax.all_gather(own_seed, every, axis=0, tiled=True)
    seed_tokens = lax.psum(mul(acts, own_seed, rows_rows, highest), every)
    image_rows = mul(accumulated, full_seed, rows_cols, high) + mul(
        grads, seed_tokens, rows_cols, high
    )
    image_tokens = lax.psum(mul(grads, image_rows, rows_rows, high), every)
    power_part = mul(accumulated, image_rows, rows_rows, high)
    power_rows = lax.psum_scatter(
        power_part, every, scatter_dimension=0, tiled=True
    ) + mul(acts, image_tokens, rows_cols, highest)
    gram_matrix = lax.psum(mul(power_rows, power_rows, rows_rows, highest), every)
    gram_matrix, held_acts = lax.optimization_barrier((gram_matrix, activations))
    full_acts = lax.all_gather(held_acts, every, axis=0, tiled=True)
    solved = solve_lower(gram_matrix, power_rows.T)
    basis_rows = solved.T.astype(jnp.bfloat16)
    sent_rows, full_acts = lax.optimization_barrier((basis_rows, full_acts))
    full_basis = lax.all_gather(sent_rows, every, axis=0, tiled=True)
    basis_tokens = mul(full_acts, full_basis, rows_rows)
    projected = mul(accumulated.astype(jnp.bfloat16), full_basis, rows_cols) + mul(
        grads, basis_tokens, rows_cols, high
    )
    return (basis_rows, *finish(moment_first, moment_second, projected, full_basis))


def body(rows, cols, activations, out_grads, accumulated, seed_basis, moment_first, moment_second):
    common = (out_grads, activations, rows, cols)
    pair = image_pair(accumulated, seed_basis, *common, 1)
    power_turned = power_scatter(accumulated, pair, *common, 2)
    basis_rows, turned = orthogonal(power_turned, rows, cols, 3)
    projected, full_basis = project(accumulated, basis_rows, turned, *common, 4)
    return (basis_rows, *finish(moment_first, moment_second, projected, full_basis))


def solution(mesh):
    rows, cols = mesh.shape["row"], mesh.shape["col"]

    def place(activations, *others):
        rank = others[2].shape[1]
        fits = rows & (rows - 1) == 0 and rows > 1 and cols % 2 == 0 and cols > 2
        fits = fits and activations.shape[0] % 128 == 0 and rank % (8 * rows * cols) == 0
        fits = fits and rank % 128 == 0 and 256 % (16 * cols // 2) == 0
        if fits:
            return body(rows, cols, activations, *others)
        return plain_body(activations, *others)

    split_rows = P(("row", "col"), None)
    in_specs = (split_rows, split_rows, split_rows, P("row", None), split_rows, split_rows)
    return jax.shard_map(
        place, mesh=mesh, in_specs=in_specs, out_specs=(split_rows,) * 4, check_vma=False
    )
```

```python
import functools

import jax
import jax.numpy as jnp
from jax import lax
from jax.experimental import pallas as pl
from jax.experimental.pallas import tpu as pltpu
from jax.sharding import PartitionSpec as P

beta_first = 0.9
beta_second = 0.99
correct_first = 1.0 - 0.9**10
correct_second = 1.0 - 0.99**10
epsilon_value = 1e-08
lift_scale = 8.0

every = ("row", "col")
highest = lax.Precision.HIGHEST
high = lax.Precision.HIGH
bf16 = jnp.bfloat16
f32 = jnp.float32
MESH = pl.DeviceIdType.MESH
ANY = pl.BlockSpec(memory_space=pl.ANY)
VMEM = pl.BlockSpec(memory_space=pltpu.VMEM)
DMA = pltpu.SemaphoreType.DMA
vmem_bytes = 63 * 2**20
project_ticks = (1, 1, 1, 1, 1, 1, 1)
image_gather = 4
image_ticks = (1, 0, 2, 1, 2, 1)
power_group = 2
power_lag, power_gap, power_ticks = 7, 4, (1, 3, 5, 7, 9, 11, 13, 15, 16)


def mul(left, right, dims, precision=None):
    return lax.dot_general(
        left, right, (dims, ((), ())), precision=precision, preferred_element_type=jnp.float32
    )


rows_cols = ((1,), (0,))
rows_rows = ((0,), (0,))
cols_cols = ((1,), (1,))


def split(value):
    upper = value.astype(bf16)
    return upper, (value - upper.astype(f32)).astype(bf16)


class Grid:
    def __init__(self, rows, cols):
        self.rows, self.chips = rows, cols // 2
        self.stages = rows.bit_length() - 1
        self.r = lax.axis_index("row")
        c = lax.axis_index("col")
        self.z, self.k = c // 2, c % 2
        self.c = c
        self.partner = (self.r, self.z * 2 + 1 - self.k)
        n = self.chips
        self.offsets = sorted(range(1, n), key=lambda d: -min(d, n - d))

    def flip(self, bit):
        return self.r + bit * (1 - 2 * ((self.r // bit) % 2))

    def peer_row(self, s, k=None):
        k = self.k if k is None else k
        low, high_bit = 2**s, 2 ** (self.stages - 1 - s)
        return (1 - k) * self.flip(low) + k * self.flip(high_bit)

    def peer(self, s):
        return (self.peer_row(s), self.c)

    def count(self, s):
        return 2 ** (self.stages - 1 - s)

    def block(self, s, j, base, k=None):
        k = self.k if k is None else k
        n = self.count(s)
        first = base % 2 ** (s + 1) + j * 2 ** (s + 1)
        second = (base // n) * n + j
        return (1 - k) * first + k * second

    def chip(self, w, far_first=False):
        n, step = self.chips, self.offsets[w] if far_first else w + 1
        return (self.z + step) % n, (self.z + n - step) % n

    def chip_device(self, z):
        return (self.r, z * 2 + self.k)

    def greet(self):
        barrier = pltpu.get_barrier_semaphore()
        peers = [self.partner]
        peers += [self.peer(s) for s in range(self.stages)]
        peers += [self.chip_device(self.chip(w)[0]) for w in range(self.chips - 1)]
        for peer in peers:
            pl.semaphore_signal(barrier, inc=1, device_id=peer, device_id_type=MESH)
        pl.semaphore_wait(barrier, len(peers))


def remote(source, target, send, recv, device):
    return pltpu.make_async_remote_copy(
        src_ref=source, dst_ref=target, send_sem=send, recv_sem=recv,
        device_id=device, device_id_type=MESH,
    )


class AllReduce:
    def __init__(self, grid, part, full, half_in, stage_in, chip_in, send, recv):
        self.g, self.part, self.full = grid, part, full
        self.half_in, self.stage_in, self.chip_in = half_in, stage_in, chip_in
        self.send, self.recv = send, recv
        self.half = part.shape[0] // 2
        self.chunk = self.half // grid.rows
        self.unit = self.chunk // grid.chips
        self.pending = []
        self.used = 0
        self.phases = (
            [self.pair_out]
            + [functools.partial(self.halve, s) for s in range(grid.stages)]
            + [self.chips_out, self.chips_back]
            + [functools.partial(self.double, s) for s in reversed(range(grid.stages))]
            + [self.pair_back, self.finish]
        )
        self.arrived = []

    @staticmethod
    def scratch(rows, width, grid_rows, chips):
        half = rows // 2
        chunk = half // grid_rows
        stages = grid_rows.bit_length() - 1
        copies = 2 + 2 * (grid_rows - 1) + 2 * (chips - 1)
        return [
            pltpu.VMEM((rows, width), f32),
            pltpu.VMEM((rows, width), f32),
            pltpu.VMEM((half, width), f32),
            pltpu.VMEM((grid_rows - 1, chunk, width), f32),
            pltpu.VMEM((chips - 1, chunk // chips, width), f32),
            DMA((copies,)),
            DMA((copies,)),
        ]

    def start(self, source, target, device):
        i = self.used
        self.used += 1
        copy = remote(source, target, self.send.at[i], self.recv.at[i], device)
        copy.start()
        self.pending.append(copy)
        self.arrived.append(copy)

    def landed(self):
        arrived, self.arrived = self.arrived, []
        for copy in arrived:
            copy.wait_recv()

    def rows_of(self, r):
        return pl.ds(pl.multiple_of((self.g.k * self.g.rows + r) * self.chunk, self.chunk), self.chunk)

    def unit_of(self, r, z):
        at = ((self.g.k * self.g.rows + r) * self.g.chips + z) * self.unit
        return pl.ds(pl.multiple_of(at, self.unit), self.unit)

    def pair_out(self):
        g = self.g
        other = pl.ds(pl.multiple_of((1 - g.k) * self.half, self.half), self.half)
        self.start(self.part.at[other], self.half_in, g.partner)

    def stage_base(self, s):
        return self.g.rows - 2 ** (self.g.stages - s)

    def halve(self, s):
        g = self.g
        self.landed()
        if s == 0:
            mine = pl.ds(pl.multiple_of(g.k * self.half, self.half), self.half)
            self.part[mine] += self.half_in[...]
        else:
            self.take(s - 1)
        for j in range(g.count(s)):
            rows = self.rows_of(g.block(s, j, g.peer_row(s)))
            self.start(self.part.at[rows], self.stage_in.at[self.stage_base(s) + j], g.peer(s))

    def take(self, s):
        g = self.g
        for j in range(g.count(s)):
            self.part[self.rows_of(g.block(s, j, g.r))] += self.stage_in[self.stage_base(s) + j]

    def chips_out(self):
        g = self.g
        self.landed()
        self.take(g.stages - 1)
        for w in range(g.chips - 1):
            z = g.chip(w)[0]
            self.start(self.part.at[self.unit_of(g.r, z)], self.chip_in.at[w], g.chip_device(z))

    def chips_back(self):
        g = self.g
        self.landed()
        own = self.unit_of(g.r, g.z)
        total = self.part[own]
        for w in range(g.chips - 1):
            total = total + self.chip_in[w]
        self.full[own] = total
        for w in range(g.chips - 1):
            self.start(self.full.at[own], self.full.at[own], g.chip_device(g.chip(w)[0]))

    def double(self, s):
        g = self.g
        self.landed()
        for j in range(g.count(s)):
            rows = self.rows_of(g.block(s, j, g.r))
            self.start(self.full.at[rows], self.full.at[rows], g.peer(s))

    def pair_back(self):
        g = self.g
        self.landed()
        mine = pl.ds(pl.multiple_of(g.k * self.half, self.half), self.half)
        self.start(self.full.at[mine], self.full.at[mine], g.partner)

    def finish(self):
        self.landed()

    def drain(self):
        for copy in self.pending:
            copy.wait_send()


def reduce_kernel(rows, cols, part_ref, out_ref, *scratch):
    grid = Grid(rows, cols)
    grid.greet()
    part, full, *rest = scratch
    part[...] = part_ref[...]
    total = AllReduce(grid, part, full, *rest)
    for phase in total.phases:
        phase()
    out_ref[...] = full[...]
    total.drain()


def all_reduce(value, rows, cols, collective_id):
    return pl.pallas_call(
        functools.partial(reduce_kernel, rows, cols),
        out_shape=jax.ShapeDtypeStruct(value.shape, f32),
        in_specs=[VMEM],
        out_specs=VMEM,
        scratch_shapes=AllReduce.scratch(*value.shape, rows, cols // 2),
        compiler_params=pltpu.CompilerParams(
            collective_id=collective_id, has_side_effects=True, vmem_limit_bytes=vmem_bytes
        ),
        name="all_reduce",
    )(value)


def power_kernel(
    rows, cols, acc, pair_ref, grads_ref, acts_ref, out_ref,
    tiles, held, pair_in, stage_in, chip_in,
    tile_sem, pair_sems, stage_sems, chip_sems, *reduce_scratch,
):
    g = Grid(rows, cols)
    blk = acts_ref.shape[0]
    rank = out_ref.shape[0]
    chips, stages = g.chips, g.stages

    half = g.count(0)

    def chip_of(w):
        if isinstance(w, int):
            return g.chip(w, True)[0] if w < chips - 1 else g.z
        far = g.z
        for i, step in enumerate(g.offsets):
            far = jnp.where(w == i, (g.z + step) % chips, far)
        return far

    mine = chips * rows

    def core_of(kind):
        return 1 - g.k + kind * (2 * g.k - 1)

    def block_of(t, kind=1):
        w, i = t // rows, t % rows
        core = core_of(kind)
        return w, g.block(0, i % half, jnp.where(i < half, g.peer_row(0, core), g.r), core)

    def fetch(t, kind):
        w, rp = block_of(t, kind)
        core = core_of(kind)
        at = ((rp * chips + chip_of(w)) * 2 + core) * blk
        columns = pl.ds(pl.multiple_of(at, blk), blk)
        slot = kind * 2 + t % 2
        return pltpu.make_async_copy(acc.at[:, columns], tiles.at[slot], tile_sem.at[slot])

    for t in range(2):
        fetch(t, 0).start()
        fetch(t, 1).start()
    g.greet()

    def product(slot):
        upper, lower = split(tiles[slot])
        both = mul(pair_ref[...], upper, rows_cols)
        return both[:rank] + both[rank:] + mul(pair_ref[:rank], lower, rows_cols)

    def pair_copy(w, rp):
        i = w * rows + rp
        return remote(held.at[i], pair_in.at[i], pair_sems.at[0, i], pair_sems.at[1, i], g.partner)

    def stage_copy(w, s, j):
        i = w * (rows - 1) + rows - 2 ** (stages - s) + j
        source = held.at[mine + w * rows + g.block(s, j, g.peer_row(s))]
        return remote(source, stage_in.at[i], stage_sems.at[0, i], stage_sems.at[1, i], g.peer(s))

    def chip_copy(w):
        return remote(
            held.at[mine + w * rows + g.r], chip_in.at[w], chip_sems.at[0, w], chip_sems.at[1, w],
            g.chip_device(chip_of(w)),
        )

    def compute(t):
        def one(kind, carry):
            w, rp = block_of(t, kind)
            fetch(t, kind).wait()
            held[kind * mine + w * rows + rp] = product(kind * 2 + t % 2)

            @pl.when(kind == 0)
            def _():
                pair_copy(w, rp).start()

            @pl.when(t + 2 < chips * rows)
            def _():
                fetch(t + 2, kind).start()

            return carry

        lax.fori_loop(0, 2, one, 0)

    def pair(t):
        w, rp = block_of(t)
        pair_copy(w, rp).wait_recv()
        held[mine + w * rows + rp] += pair_in[w * rows + rp]

        @pl.when(t % rows < half)
        def _():
            stage_copy(w, 0, t % rows).start()

    def halve(w, s):
        for j in range(g.count(s - 1)):
            i = w * (rows - 1) + rows - 2 ** (stages - s + 1) + j
            stage_copy(w, s - 1, j).wait_recv()
            held[mine + w * rows + g.block(s - 1, j, g.r)] += stage_in[i]
        for j in range(g.count(s)):
            stage_copy(w, s, j).start()

    def leave(w):
        i = w * (rows - 1) + rows - 2
        stage_copy(w, stages - 1, 0).wait_recv()
        held[mine + w * rows + g.r] += stage_in[i]
        if w < chips - 1:
            chip_copy(w).start()

    part, full, *rest = reduce_scratch

    part[...] = mul(pair_ref[:rank], grads_ref[...], rows_cols) + mul(
        pair_ref[rank:], grads_ref[...], rows_cols
    )
    tokens = AllReduce(g, part, full, *rest)
    phases = iter(tokens.phases)

    def tick():
        phase = next(phases, None)
        if phase is not None:
            phase()

    tick()
    steps = chips * rows
    lag, gap, ticks = power_lag, power_gap, power_ticks
    later = {}
    for w in range(chips):
        for s in range(1, stages):
            later.setdefault(min(lag + gap * w + 3 * (s - 1), steps + 2 * w + s), []).append(
                functools.partial(halve, w, s)
            )
    for w in range(chips):
        later.setdefault(min(lag + gap * w + gap, steps + 2 * w + 3), []).append(
            functools.partial(leave, w)
        )
    def both(t, carry):
        compute(t)

        @pl.when(t > 0)
        def _():
            pair(t - 1)

        return carry

    for t in range(0, max(max(later), steps) + power_group, power_group):
        for _ in range(sum(t <= at < t + power_group for at in ticks)):
            tick()
        if t < steps:
            lax.fori_loop(t, min(steps, t + power_group), both, 0)
        if steps <= t < steps + power_group:
            pair(steps - 1)
        for at in range(t, t + power_group):
            for event in later.get(at, ()):
                event()
    for phase in phases:
        phase()
    upper, lower = split(full[...])
    total = mul(upper, acts_ref[...], cols_cols) + mul(lower, acts_ref[...], cols_cols)
    total = total + held[mine + (chips - 1) * rows + g.r]
    for w in range(chips - 1):
        chip_copy(w).wait_recv()
        total = total + chip_in[w]
    out_ref[...] = total

    tokens.drain()
    for w in range(chips):
        def done(rp, carry):
            pair_copy(w, rp).wait_send()
            return carry

        lax.fori_loop(0, rows, done, 0)
        for s in range(stages):
            for j in range(g.count(s)):
                stage_copy(w, s, j).wait_send()
        if w < chips - 1:
            chip_copy(w).wait_send()


def power_scatter(accumulated, pair, grads, acts, rows, cols, collective_id):
    rank = pair.shape[0] // 2
    blk = acts.shape[0]
    chips = cols // 2
    blocks = chips * rows
    passed = chips * (rows - 1)
    return pl.pallas_call(
        functools.partial(power_kernel, rows, cols),
        out_shape=jax.ShapeDtypeStruct((rank, blk), f32),
        in_specs=[ANY, VMEM, VMEM, VMEM],
        out_specs=VMEM,
        scratch_shapes=[
            pltpu.VMEM((4, accumulated.shape[0], blk), f32),
            pltpu.VMEM((2 * blocks, rank, blk), f32),
            pltpu.VMEM((blocks, rank, blk), f32),
            pltpu.VMEM((passed, rank, blk), f32),
            pltpu.VMEM((chips - 1, rank, blk), f32),
            DMA((4,)),
            DMA((2, blocks)),
            DMA((2, passed)),
            DMA((2, chips - 1)),
            *AllReduce.scratch(rank, acts.shape[1], rows, chips),
        ],
        compiler_params=pltpu.CompilerParams(
            collective_id=collective_id, has_side_effects=True, vmem_limit_bytes=vmem_bytes
        ),
        name="power_scatter",
    )(accumulated, pair, grads, acts)


class Interleaved:
    def __init__(self, phases):
        self.left = list(phases)

    def tick(self, count=1):
        for _ in range(count):
            if self.left:
                self.left.pop(0)()

    def rest(self):
        self.tick(len(self.left))


def image_kernel(
    rows, cols, acc, seed_ref, grads_ref, acts_ref, out_ref,
    tiles, image, seeds, tile_sem, pair_sems, stage_sems, share_sems, *reduce_scratch,
):
    g = Grid(rows, cols)
    stages = g.stages
    blk, rank = seeds.shape[2], seeds.shape[3]
    own_rows = seed_ref.shape[0]
    pieces = own_rows // (2 * blk)
    tokens_rows = acts_ref.shape[0]

    def piece(rp, h, i):
        return (rp * 2 + h) * pieces + i

    def fetch(p, slot):
        columns = pl.ds(pl.multiple_of(p * blk, blk), blk)
        return pltpu.make_async_copy(acc.at[:, columns], tiles.at[slot], tile_sem.at[slot])

    def order(t):
        u = t - 2 * pieces
        wave = u // (2 * (rows - 1))
        inner = u % (2 * (rows - 1))
        other = piece((g.r + 1 + inner // 2) % rows, inner % 2, (wave + 1) % pieces)
        own = piece(g.r, t // pieces, t % pieces)
        return jnp.where(t < 2 * pieces, own, other)

    count = 2 * pieces * rows
    depth = tiles.shape[0]
    for t in range(depth - 1):
        fetch(order(t), t).start()
    g.greet()

    def spread(q):
        at = pl.ds(pl.multiple_of(q * blk, blk), blk)
        upper, lower = split(seed_ref[at])
        target = g.r * 2 * pieces + q
        seeds[target, 0] = upper
        seeds[target, 1] = lower

    share = blk // g.chips

    def shared(p, z):
        return seeds.at[p, :, pl.ds(pl.multiple_of(z * share, share), share)]

    def share_copy(s, j, w, z):
        at = (rows - 2 ** (stages - s) + j) * (g.chips - 1) + w
        ref = shared(piece(g.block(s, j, g.peer_row(s)), g.k, 0), z)
        device = g.chip_device(g.chip(w)[0])
        return remote(ref, ref, share_sems.at[0, at], share_sems.at[1, at], device)

    def pair_copy(rp, i):
        p = piece(rp, g.k, i)
        at = i * rows + rp
        return remote(seeds.at[p], seeds.at[p], pair_sems.at[0, at], pair_sems.at[1, at], g.partner)

    def pair_wait(rp, i):
        at = i * rows + rp
        p = piece(rp, 1 - g.k, i)
        remote(seeds.at[p], seeds.at[p], pair_sems.at[0, at], pair_sems.at[1, at], g.partner).wait_recv()

    def stage_copy(i, s, j, base):
        at = i * (rows - 1) + rows - 2 ** (stages - s) + j
        p = piece(g.block(s, j, base), g.k, i)
        ref = seeds.at[p] if i else shared(p, g.z)
        return remote(ref, ref, stage_sems.at[0, at], stage_sems.at[1, at], g.peer(s))

    def send(i, s):
        for j in range(g.count(s)):
            stage_copy(i, s, j, g.r).start()

    def land(i, s):
        for j in range(g.count(s)):
            stage_copy(i, s, j, g.peer_row(s)).wait_recv()
            if i:
                pair_copy(g.block(s, j, g.peer_row(s)), i).start()
            else:
                for w in range(g.chips - 1):
                    share_copy(s, j, w, g.z).start()

    def gather():
        for s in reversed(range(stages)):
            for j in range(g.count(s)):
                for w in range(g.chips - 1):
                    share_copy(s, j, w, g.chip(w)[1]).wait_recv()
                pair_copy(g.block(s, j, g.peer_row(s)), 0).start()

    def compute(t):
        slot = t % depth
        p = order(t)
        fetch(p, slot).wait()

        @pl.when(t + depth - 1 < count)
        def _():
            fetch(order(t + depth - 1), (t + depth - 1) % depth).start()

        upper, lower = split(tiles[slot])
        image[...] += (
            mul(upper, seeds[p, 0], rows_cols)
            + mul(lower, seeds[p, 0], rows_cols)
            + mul(upper, seeds[p, 1], rows_cols)
        )

    def own_step(t, carry):
        compute(t)
        return carry

    def other_step(t, carry):
        inner = (t - 2 * pieces) % (2 * (rows - 1))
        wave = (t - 2 * pieces) // (2 * (rows - 1))
        rp = (g.r + 1 + inner // 2) % rows

        @pl.when(inner % 2 == 1 - g.k)
        def _():
            pair_wait(rp, (wave + 1) % pieces)

        compute(t)
        return carry

    for i in range(pieces):
        spread(g.k * pieces + i)
        send(i, stages - 1)
    own = pl.ds(pl.multiple_of(g.c * tokens_rows, tokens_rows), tokens_rows)
    turned = seed_ref[own].T
    part, full, *rest = reduce_scratch
    upper, lower = split(turned)
    part[...] = mul(upper, acts_ref[...], rows_cols) + mul(lower, acts_ref[...], rows_cols)
    tokens = AllReduce(g, part, full, *rest)
    small = Interleaved(tokens.phases)
    small.tick()

    def spread_other(i, carry):
        spread((1 - g.k) * pieces + i)
        return carry

    lax.fori_loop(0, pieces, spread_other, 0)
    image[...] = jnp.zeros_like(image)
    first = 2 * pieces // (stages + 1)
    done = 0
    lag = stages
    for at in range(pieces + lag):
        small.tick(image_ticks[at] if at < len(image_ticks) else 1)
        for late in range(stages):
            i = at - late
            if 0 <= i < pieces:
                s = stages - 1 - late
                land(i, s)
                if s > 0:
                    send(i, s - 1)
        if at == image_gather:
            gather()
        if done < 2 * pieces:
            stop = min(2 * pieces, done + first)
            lax.fori_loop(done, stop, own_step, 0)
            done = stop
        i = at - lag
        if 0 <= i < pieces:
            lax.fori_loop(done, 2 * pieces, own_step, 0)
            done = 2 * pieces
            start = 2 * pieces + i * 2 * (rows - 1)
            lax.fori_loop(start, start + 2 * (rows - 1), other_step, 0)
    small.rest()
    upper, lower = split(full[...])
    total = image[...] + mul(grads_ref[...], upper, cols_cols) + mul(grads_ref[...], lower, cols_cols)
    upper, lower = split(total.T)
    out_ref[:rank] = upper
    out_ref[rank:] = lower

    tokens.drain()
    for i in range(pieces):
        for s in range(stages):
            for j in range(g.count(s)):
                stage_copy(i, s, j, g.r).wait_send()
                pair_copy(g.block(s, j, g.peer_row(s)), i).wait_send()
    for s in range(stages):
        for j in range(g.count(s)):
            for w in range(g.chips - 1):
                share_copy(s, j, w, g.z).wait_send()


def image_pair(accumulated, seed, grads, acts, rows, cols, collective_id):
    rank = seed.shape[1]
    height, width = accumulated.shape
    blk = 256 if seed.shape[0] % 512 == 0 else seed.shape[0] // 2
    total = width // blk
    pieces = total // (2 * rows)
    return pl.pallas_call(
        functools.partial(image_kernel, rows, cols),
        out_shape=jax.ShapeDtypeStruct((2 * rank, height), bf16),
        in_specs=[ANY, VMEM, VMEM, VMEM],
        out_specs=VMEM,
        scratch_shapes=[
            pltpu.VMEM((4, height, blk), f32),
            pltpu.VMEM((height, rank), f32),
            pltpu.VMEM((total, 2, blk, rank), bf16),
            DMA((4,)),
            DMA((2, pieces * rows)),
            DMA((2, pieces * (rows - 1))),
            DMA((2, (cols // 2 - 1) * (rows - 1))),
            *AllReduce.scratch(rank, acts.shape[1], rows, cols // 2),
        ],
        compiler_params=pltpu.CompilerParams(
            collective_id=collective_id, has_side_effects=True, vmem_limit_bytes=vmem_bytes
        ),
        name="image_pair",
    )(accumulated, seed, grads, acts)


def project_kernel(
    rows, cols, acc, basis_ref, turned_ref, grads_ref, acts_ref, out_ref, full_ref,
    tiles, tile_sem, pair_sems, stage_sems, chip_sems, *reduce_scratch,
):
    g = Grid(rows, cols)
    chips, stages = g.chips, g.stages
    blk = basis_ref.shape[0]
    count = chips * rows

    def chip_of(w):
        return (g.z + chips - w) % chips

    def at_of(rp, w, core):
        at = ((rp * chips + chip_of(w)) * 2 + core) * blk
        return full_ref.at[pl.ds(pl.multiple_of(at, blk), blk)]

    def fetch(t):
        w, rp = t // rows, t % rows
        at = (rp * chips + chip_of(w)) * 2 * blk
        columns = pl.ds(pl.multiple_of(at, 2 * blk), 2 * blk)
        return pltpu.make_async_copy(acc.at[:, columns], tiles.at[t % 2], tile_sem.at[t % 2])

    fetch(0).start()
    fetch(1).start()
    g.greet()
    own_rows = pl.ds(pl.multiple_of(((g.r * chips + g.z) * 2 + g.k) * blk, blk), blk)
    full_ref[own_rows] = basis_ref[...]

    def pair_copy(rp, w):
        i = w * rows + rp
        ref = at_of(rp, w, g.k)
        return remote(ref, ref, pair_sems.at[0, i], pair_sems.at[1, i], g.partner)

    def pair_wait(rp, w):
        i = w * rows + rp
        ref = at_of(rp, w, 1 - g.k)
        remote(ref, ref, pair_sems.at[0, i], pair_sems.at[1, i], g.partner).wait_recv()

    def stage_copy(w, s, j, base):
        i = w * (rows - 1) + rows - 2 ** (stages - s) + j
        ref = at_of(g.block(s, j, base), w, g.k)
        return remote(ref, ref, stage_sems.at[0, i], stage_sems.at[1, i], g.peer(s))

    def chip_copy(w, z):
        at = ((g.r * chips + z) * 2 + g.k) * blk
        ref = full_ref.at[pl.ds(pl.multiple_of(at, blk), blk)]
        device = g.chip_device(g.chip(w)[0])
        return remote(ref, ref, chip_sems.at[0, w], chip_sems.at[1, w], device)

    def enter(w):
        if w > 0:
            chip_copy(w - 1, chip_of(w)).wait_recv()
        stage_copy(w, stages - 1, 0, g.r).start()
        pair_copy(g.r, w).start()

    def land(w, s):
        for j in range(g.count(s)):
            stage_copy(w, s, j, g.peer_row(s)).wait_recv()
        if s > 0:
            for j in range(g.count(s - 1)):
                stage_copy(w, s - 1, j, g.r).start()
        for j in range(g.count(s)):
            pair_copy(g.block(s, j, g.peer_row(s)), w).start()

    for w in range(chips - 1):
        chip_copy(w, g.z).start()
    part, full, *rest = reduce_scratch
    enter(0)
    part[...] = mul(turned_ref[...], acts_ref[...], rows_cols)
    tokens = AllReduce(g, part, full, *rest)
    small = Interleaved(tokens.phases)
    small.tick()
    out_ref[...] = jnp.zeros_like(out_ref)

    def step(t, carry):
        w, rp = t // rows, t % rows
        fetch(t).wait()
        pair_wait(rp, w)
        at = (rp * chips + chip_of(w)) * 2 * blk
        block = full_ref[pl.ds(pl.multiple_of(at, 2 * blk), 2 * blk)]
        out_ref[...] += mul(tiles[t % 2].astype(bf16), block, rows_cols)

        @pl.when(t + 2 < count)
        def _():
            fetch(t + 2).start()

        return carry

    for at in range(chips + stages + 1):
        small.tick(project_ticks[at] if at < len(project_ticks) else 1)
        for late in range(stages + 1):
            w = at - late
            if 0 <= w < chips:
                if late == 0:
                    if w > 0:
                        enter(w)
                else:
                    land(w, stages - late)
        w = at - stages
        if 0 <= w < chips:
            lax.fori_loop(w * rows, (w + 1) * rows, step, 0)
    small.rest()
    upper, lower = split(full[...])
    out_ref[...] += mul(grads_ref[...], upper, cols_cols) + mul(grads_ref[...], lower, cols_cols)

    tokens.drain()
    for w in range(chips - 1):
        chip_copy(w, g.z).wait_send()
    for w in range(chips):
        pair_copy(g.r, w).wait_send()
        for s in range(stages):
            for j in range(g.count(s)):
                stage_copy(w, s, j, g.r).wait_send()
                pair_copy(g.block(s, j, g.peer_row(s)), w).wait_send()


def project(accumulated, basis, turned, grads, acts, rows, cols, collective_id):
    height, width = accumulated.shape
    blk, rank = basis.shape
    chips = cols // 2
    return pl.pallas_call(
        functools.partial(project_kernel, rows, cols),
        out_shape=(
            jax.ShapeDtypeStruct((height, rank), f32),
            jax.ShapeDtypeStruct((width, rank), bf16),
        ),
        in_specs=[ANY, VMEM, VMEM, VMEM, VMEM],
        out_specs=(VMEM, VMEM),
        scratch_shapes=[
            pltpu.VMEM((2, height, 2 * blk), f32),
            DMA((2,)),
            DMA((2, chips * rows)),
            DMA((2, chips * (rows - 1))),
            DMA((2, chips - 1)),
            *AllReduce.scratch(rank, acts.shape[1], rows, chips),
        ],
        compiler_params=pltpu.CompilerParams(
            collective_id=collective_id, has_side_effects=True, vmem_limit_bytes=vmem_bytes
        ),
        name="project",
    )(accumulated, basis, turned, grads, acts)


def orthogonal_kernel(rows, cols, step, power_ref, out_ref, turned_ref, gram, rest, *reduce_scratch):
    g = Grid(rows, cols)
    g.greet()
    part, full, *others = reduce_scratch
    rank = gram.shape[0]
    count = rank // step
    product = mul(power_ref[...], power_ref[...], cols_cols, highest)
    across = part.shape[1] // step
    lower_blocks = [(i, j) for i in range(count) for j in range(i + 1)]

    def cut(n):
        return slice(n * step, (n + 1) * step)

    for n in range(count * across):
        i, j = lower_blocks[n] if n < len(lower_blocks) else (0, 0)
        part[cut(n // across), cut(n % across)] = product[cut(i), cut(j)]
    total = AllReduce(g, part, full, *others)
    for phase in total.phases:
        phase()
    rest[...] = power_ref[...]
    for n, (i, j) in enumerate(lower_blocks):
        gram[cut(i), cut(j)] = full[cut(n // across), cut(n % across)]
        if i > j:
            gram[cut(j), cut(i)] = jnp.zeros((step, step), f32)
    part_step = step // 2
    lanes = lax.broadcasted_iota(jnp.int32, (part_step, part_step), 1)
    lines = lax.broadcasted_iota(jnp.int32, (part_step, part_step), 0)
    eights = lax.broadcasted_iota(jnp.int32, (8, step), 0)

    def invert(block):
        both = jnp.concatenate([block, (lanes == lines).astype(f32)], axis=1)
        parts = [both[8 * i : 8 * i + 8] for i in range(part_step // 8)]
        for n in range(0, part_step, 2):
            q, o = n // 8, n % 8
            wide = (8, step)
            first = jnp.broadcast_to(parts[q][:, n : n + 1], wide)
            second = jnp.broadcast_to(parts[q][:, n + 1 : n + 2], wide)
            row_a = jnp.broadcast_to(parts[q][o : o + 1], wide)
            row_b = jnp.broadcast_to(parts[q][o + 1 : o + 2], wide)
            aa = jnp.broadcast_to(first[o : o + 1], wide)
            ab = jnp.broadcast_to(first[o + 1 : o + 2], wide)
            bb = jnp.broadcast_to(second[o + 1 : o + 2], wide)
            scale = 1.0 / (aa * bb - ab * ab)
            take_a = (row_a * bb - row_b * ab) * scale
            take_b = (row_b * aa - row_a * ab) * scale
            if o < 6:
                later = eights > o + 1
                parts[q] = (
                    parts[q]
                    - jnp.where(later, first, 0.0) * take_a
                    - jnp.where(later, second, 0.0) * take_b
                )
            for i in range(q + 1, part_step // 8):
                parts[i] = (
                    parts[i]
                    - parts[i][:, n : n + 1] * take_a
                    - parts[i][:, n + 1 : n + 2] * take_b
                )
        both = jnp.concatenate(parts, axis=0)
        left, right = both[:, :part_step], both[:, part_step:]
        odd = lines % 2 == 1
        diagonal = jnp.sum(jnp.where(lanes == lines, left, 0.0), axis=1, keepdims=True)
        side = jnp.sum(
            jnp.where(odd & (lanes == lines - 1), left, 0.0), axis=1, keepdims=True
        )
        diagonal = jnp.broadcast_to(diagonal, left.shape)
        side = jnp.broadcast_to(side, left.shape)
        ratio = jnp.where(odd, side / pltpu.roll(diagonal, 1, 0), 0.0)
        right = right - ratio * pltpu.roll(right, 1, 0)
        return right * lax.rsqrt(diagonal - ratio * side)

    def eliminate(j, carry):
        at = pl.ds(pl.multiple_of(j * step, step), step)
        block = gram[at, at]
        first = invert(block[:part_step, :part_step])
        link = mul(block[part_step:, :part_step], first, cols_cols, highest)
        second = invert(block[part_step:, part_step:] - mul(link, link, cols_cols, highest))
        below = -mul(second, mul(link, first, rows_cols, highest), rows_cols, highest)
        above = jnp.zeros_like(below)
        inverse = jnp.concatenate(
            [jnp.concatenate([first, above], axis=1), jnp.concatenate([below, second], axis=1)],
            axis=0,
        )
        panel = mul(gram[:, at], inverse, cols_cols, highest)
        below = lax.broadcasted_iota(jnp.int32, panel.shape, 0) >= (j + 1) * step
        panel = jnp.where(below, panel, 0.0)
        gram[...] -= mul(panel, panel, cols_cols, highest)
        solved = mul(inverse, rest[at], rows_cols, highest)
        rest[...] -= mul(panel, solved, rows_cols, highest)
        turned_ref[at] = solved.astype(bf16)
        return carry

    lax.fori_loop(0, rank // step, eliminate, 0)
    out_ref[...] = turned_ref[...].astype(f32).T.astype(bf16)
    total.drain()


def orthogonal(power_turned, rows, cols, collective_id):
    rank, blk = power_turned.shape
    blocks = rank // 128
    return pl.pallas_call(
        functools.partial(orthogonal_kernel, rows, cols, 128),
        out_shape=(
            jax.ShapeDtypeStruct((blk, rank), bf16),
            jax.ShapeDtypeStruct((rank, blk), bf16),
        ),
        in_specs=[VMEM],
        out_specs=(VMEM, VMEM),
        scratch_shapes=[
            pltpu.VMEM((rank, rank), f32),
            pltpu.VMEM((rank, blk), f32),
            *AllReduce.scratch(rank, 128 * -(-blocks * (blocks + 1) // (2 * blocks)), rows, cols // 2),
        ],
        compiler_params=pltpu.CompilerParams(
            collective_id=collective_id, has_side_effects=True, vmem_limit_bytes=vmem_bytes
        ),
        name="orthogonal",
    )(power_turned)


def solve_lower(gram_matrix, right):
    rank = gram_matrix.shape[0]
    step = 128 if rank % 128 == 0 else rank
    count = rank // step
    cut = lambda n: slice(n * step, (n + 1) * step)
    trailing = {
        (i, j): gram_matrix[cut(i), cut(j)] for i in range(count) for j in range(i + 1)
    }
    rests = [right[cut(i)] for i in range(count)]
    solved = []
    for j in range(count):
        factor = lax.linalg.cholesky(trailing[j, j], symmetrize_input=False)
        inverse = jax.scipy.linalg.solve_triangular(
            factor, jnp.eye(step, dtype=jnp.float32), lower=True
        )
        panel = {
            i: mul(trailing[i, j], inverse, cols_cols, highest) for i in range(j + 1, count)
        }
        solved.append(mul(inverse, rests[j], rows_cols, highest))
        for i in range(j + 1, count):
            rests[i] = rests[i] - mul(panel[i], solved[j], rows_cols, highest)
            for k in range(j + 1, i + 1):
                trailing[i, k] = trailing[i, k] - mul(panel[i], panel[k], cols_cols, highest)
    return jnp.concatenate(solved, axis=0)


def finish(moment_first, moment_second, projected, full_basis):
    first_next = beta_first * moment_first + (1.0 - beta_first) * projected
    second_next = beta_second * moment_second + (1.0 - beta_second) * projected * projected
    direction = (
        first_next / correct_first / (jnp.sqrt(second_next / correct_second) + epsilon_value)
    )
    lifted = lift_scale * mul(direction.astype(bf16), full_basis, cols_cols)
    return first_next, second_next, lifted


def plain_body(activations, out_grads, accumulated, seed_basis, moment_first, moment_second):
    share_rows = activations.shape[0]
    acts = activations.astype(jnp.float32)
    grads = out_grads.astype(jnp.float32)
    own_seed = lax.dynamic_slice_in_dim(
        seed_basis, lax.axis_index("col") * share_rows, share_rows, 0
    )
    full_seed = lax.all_gather(own_seed, every, axis=0, tiled=True)
    seed_tokens = lax.psum(mul(acts, own_seed, rows_rows, highest), every)
    image_rows = mul(accumulated, full_seed, rows_cols, high) + mul(
        grads, seed_tokens, rows_cols, high
    )
    image_tokens = lax.psum(mul(grads, image_rows, rows_rows, high), every)
    power_part = mul(accumulated, image_rows, rows_rows, high)
    power_rows = lax.psum_scatter(
        power_part, every, scatter_dimension=0, tiled=True
    ) + mul(acts, image_tokens, rows_cols, highest)
    gram_matrix = lax.psum(mul(power_rows, power_rows, rows_rows, highest), every)
    gram_matrix, held_acts = lax.optimization_barrier((gram_matrix, activations))
    full_acts = lax.all_gather(held_acts, every, axis=0, tiled=True)
    solved = solve_lower(gram_matrix, power_rows.T)
    basis_rows = solved.T.astype(jnp.bfloat16)
    sent_rows, full_acts = lax.optimization_barrier((basis_rows, full_acts))
    full_basis = lax.all_gather(sent_rows, every, axis=0, tiled=True)
    basis_tokens = mul(full_acts, full_basis, rows_rows)
    projected = mul(accumulated.astype(jnp.bfloat16), full_basis, rows_cols) + mul(
        grads, basis_tokens, rows_cols, high
    )
    return (basis_rows, *finish(moment_first, moment_second, projected, full_basis))


def body(rows, cols, activations, out_grads, accumulated, seed_basis, moment_first, moment_second):
    common = (out_grads, activations, rows, cols)
    pair = image_pair(accumulated, seed_basis, *common, 1)
    power_turned = power_scatter(accumulated, pair, *common, 2)
    basis_rows, turned = orthogonal(power_turned, rows, cols, 3)
    projected, full_basis = project(accumulated, basis_rows, turned, *common, 4)
    return (basis_rows, *finish(moment_first, moment_second, projected, full_basis))


def solution(mesh):
    rows, cols = mesh.shape["row"], mesh.shape["col"]

    def place(activations, *others):
        rank = others[2].shape[1]
        fits = rows & (rows - 1) == 0 and rows > 1 and cols % 2 == 0 and cols > 2
        fits = fits and activations.shape[0] % 128 == 0 and rank % (8 * rows * cols) == 0
        fits = fits and rank % 128 == 0 and 256 % (16 * cols // 2) == 0
        if fits:
            return body(rows, cols, activations, *others)
        return plain_body(activations, *others)

    split_rows = P(("row", "col"), None)
    in_specs = (split_rows, split_rows, split_rows, P("row", None), split_rows, split_rows)
    return jax.shard_map(
        place, mesh=mesh, in_specs=in_specs, out_specs=(split_rows,) * 4, check_vma=False
    )
```

```python
import functools

import jax
import jax.numpy as jnp
from jax import lax
from jax.experimental import pallas as pl
from jax.experimental.pallas import tpu as pltpu
from jax.sharding import PartitionSpec as P

beta_first = 0.9
beta_second = 0.99
correct_first = 1.0 - 0.9**10
correct_second = 1.0 - 0.99**10
epsilon_value = 1e-08
lift_scale = 8.0

every = ("row", "col")
highest = lax.Precision.HIGHEST
high = lax.Precision.HIGH
bf16 = jnp.bfloat16
f32 = jnp.float32
MESH = pl.DeviceIdType.MESH
ANY = pl.BlockSpec(memory_space=pl.ANY)
VMEM = pl.BlockSpec(memory_space=pltpu.VMEM)
DMA = pltpu.SemaphoreType.DMA
vmem_bytes = 63 * 2**20
project_ticks = (1, 1, 1, 1, 1, 1, 1)
image_gather = 4
image_ticks = (1, 0, 2, 1, 2, 1)
power_group = 2
power_lag, power_gap, power_ticks = 7, 4, (1, 5, 7, 9, 11, 13, 15, 17, 17)


def mul(left, right, dims, precision=None):
    return lax.dot_general(
        left, right, (dims, ((), ())), precision=precision, preferred_element_type=jnp.float32
    )


rows_cols = ((1,), (0,))
rows_rows = ((0,), (0,))
cols_cols = ((1,), (1,))


def split(value):
    upper = value.astype(bf16)
    return upper, (value - upper.astype(f32)).astype(bf16)


class Grid:
    def __init__(self, rows, cols):
        self.rows, self.chips = rows, cols // 2
        self.stages = rows.bit_length() - 1
        self.r = lax.axis_index("row")
        c = lax.axis_index("col")
        self.z, self.k = c // 2, c % 2
        self.c = c
        self.partner = (self.r, self.z * 2 + 1 - self.k)
        n = self.chips
        self.offsets = sorted(range(1, n), key=lambda d: -min(d, n - d))

    def flip(self, bit):
        return self.r + bit * (1 - 2 * ((self.r // bit) % 2))

    def peer_row(self, s, k=None):
        k = self.k if k is None else k
        low, high_bit = 2**s, 2 ** (self.stages - 1 - s)
        return (1 - k) * self.flip(low) + k * self.flip(high_bit)

    def peer(self, s):
        return (self.peer_row(s), self.c)

    def count(self, s):
        return 2 ** (self.stages - 1 - s)

    def block(self, s, j, base, k=None):
        k = self.k if k is None else k
        n = self.count(s)
        first = base % 2 ** (s + 1) + j * 2 ** (s + 1)
        second = (base // n) * n + j
        return (1 - k) * first + k * second

    def chip(self, w, far_first=False):
        n, step = self.chips, self.offsets[w] if far_first else w + 1
        return (self.z + step) % n, (self.z + n - step) % n

    def chip_device(self, z):
        return (self.r, z * 2 + self.k)

    def greet(self):
        barrier = pltpu.get_barrier_semaphore()
        peers = [self.partner]
        peers += [self.peer(s) for s in range(self.stages)]
        peers += [self.chip_device(self.chip(w)[0]) for w in range(self.chips - 1)]
        for peer in peers:
            pl.semaphore_signal(barrier, inc=1, device_id=peer, device_id_type=MESH)
        pl.semaphore_wait(barrier, len(peers))


def remote(source, target, send, recv, device):
    return pltpu.make_async_remote_copy(
        src_ref=source, dst_ref=target, send_sem=send, recv_sem=recv,
        device_id=device, device_id_type=MESH,
    )


class AllReduce:
    def __init__(self, grid, part, full, half_in, stage_in, chip_in, send, recv):
        self.g, self.part, self.full = grid, part, full
        self.half_in, self.stage_in, self.chip_in = half_in, stage_in, chip_in
        self.send, self.recv = send, recv
        self.half = part.shape[0] // 2
        self.chunk = self.half // grid.rows
        self.unit = self.chunk // grid.chips
        self.pending = []
        self.used = 0
        self.phases = (
            [self.pair_out]
            + [functools.partial(self.halve, s) for s in range(grid.stages)]
            + [self.chips_out, self.chips_back]
            + [functools.partial(self.double, s) for s in reversed(range(grid.stages))]
            + [self.pair_back, self.finish]
        )
        self.arrived = []

    @staticmethod
    def scratch(rows, width, grid_rows, chips):
        half = rows // 2
        chunk = half // grid_rows
        stages = grid_rows.bit_length() - 1
        copies = 2 + 2 * (grid_rows - 1) + 2 * (chips - 1)
        return [
            pltpu.VMEM((rows, width), f32),
            pltpu.VMEM((rows, width), f32),
            pltpu.VMEM((half, width), f32),
            pltpu.VMEM((grid_rows - 1, chunk, width), f32),
            pltpu.VMEM((chips - 1, chunk // chips, width), f32),
            DMA((copies,)),
            DMA((copies,)),
        ]

    def start(self, source, target, device):
        i = self.used
        self.used += 1
        copy = remote(source, target, self.send.at[i], self.recv.at[i], device)
        copy.start()
        self.pending.append(copy)
        self.arrived.append(copy)

    def landed(self):
        arrived, self.arrived = self.arrived, []
        for copy in arrived:
            copy.wait_recv()

    def rows_of(self, r):
        return pl.ds(pl.multiple_of((self.g.k * self.g.rows + r) * self.chunk, self.chunk), self.chunk)

    def unit_of(self, r, z):
        at = ((self.g.k * self.g.rows + r) * self.g.chips + z) * self.unit
        return pl.ds(pl.multiple_of(at, self.unit), self.unit)

    def pair_out(self):
        g = self.g
        other = pl.ds(pl.multiple_of((1 - g.k) * self.half, self.half), self.half)
        self.start(self.part.at[other], self.half_in, g.partner)

    def stage_base(self, s):
        return self.g.rows - 2 ** (self.g.stages - s)

    def halve(self, s):
        g = self.g
        self.landed()
        if s == 0:
            mine = pl.ds(pl.multiple_of(g.k * self.half, self.half), self.half)
            self.part[mine] += self.half_in[...]
        else:
            self.take(s - 1)
        for j in range(g.count(s)):
            rows = self.rows_of(g.block(s, j, g.peer_row(s)))
            self.start(self.part.at[rows], self.stage_in.at[self.stage_base(s) + j], g.peer(s))

    def take(self, s):
        g = self.g
        for j in range(g.count(s)):
            self.part[self.rows_of(g.block(s, j, g.r))] += self.stage_in[self.stage_base(s) + j]

    def chips_out(self):
        g = self.g
        self.landed()
        self.take(g.stages - 1)
        for w in range(g.chips - 1):
            z = g.chip(w)[0]
            self.start(self.part.at[self.unit_of(g.r, z)], self.chip_in.at[w], g.chip_device(z))

    def chips_back(self):
        g = self.g
        self.landed()
        own = self.unit_of(g.r, g.z)
        total = self.part[own]
        for w in range(g.chips - 1):
            total = total + self.chip_in[w]
        self.full[own] = total
        for w in range(g.chips - 1):
            self.start(self.full.at[own], self.full.at[own], g.chip_device(g.chip(w)[0]))

    def double(self, s):
        g = self.g
        self.landed()
        for j in range(g.count(s)):
            rows = self.rows_of(g.block(s, j, g.r))
            self.start(self.full.at[rows], self.full.at[rows], g.peer(s))

    def pair_back(self):
        g = self.g
        self.landed()
        mine = pl.ds(pl.multiple_of(g.k * self.half, self.half), self.half)
        self.start(self.full.at[mine], self.full.at[mine], g.partner)

    def finish(self):
        self.landed()

    def drain(self):
        for copy in self.pending:
            copy.wait_send()


def reduce_kernel(rows, cols, part_ref, out_ref, *scratch):
    grid = Grid(rows, cols)
    grid.greet()
    part, full, *rest = scratch
    part[...] = part_ref[...]
    total = AllReduce(grid, part, full, *rest)
    for phase in total.phases:
        phase()
    out_ref[...] = full[...]
    total.drain()


def all_reduce(value, rows, cols, collective_id):
    return pl.pallas_call(
        functools.partial(reduce_kernel, rows, cols),
        out_shape=jax.ShapeDtypeStruct(value.shape, f32),
        in_specs=[VMEM],
        out_specs=VMEM,
        scratch_shapes=AllReduce.scratch(*value.shape, rows, cols // 2),
        compiler_params=pltpu.CompilerParams(
            collective_id=collective_id, has_side_effects=True, vmem_limit_bytes=vmem_bytes
        ),
        name="all_reduce",
    )(value)


def power_kernel(
    rows, cols, acc, pair_ref, grads_ref, acts_ref, out_ref,
    tiles, held, pair_in, stage_in, chip_in,
    tile_sem, pair_sems, stage_sems, chip_sems, *reduce_scratch,
):
    g = Grid(rows, cols)
    blk = acts_ref.shape[0]
    rank = out_ref.shape[0]
    chips, stages = g.chips, g.stages

    half = g.count(0)

    def chip_of(w):
        if isinstance(w, int):
            return g.chip(w, True)[0] if w < chips - 1 else g.z
        far = g.z
        for i, step in enumerate(g.offsets):
            far = jnp.where(w == i, (g.z + step) % chips, far)
        return far

    mine = chips * rows

    def core_of(kind):
        return 1 - g.k + kind * (2 * g.k - 1)

    def block_of(t, kind=1):
        w, i = t // rows, t % rows
        core = core_of(kind)
        return w, g.block(0, i % half, jnp.where(i < half, g.peer_row(0, core), g.r), core)

    def fetch(t, kind):
        w, rp = block_of(t, kind)
        core = core_of(kind)
        at = ((rp * chips + chip_of(w)) * 2 + core) * blk
        columns = pl.ds(pl.multiple_of(at, blk), blk)
        slot = kind * 2 + t % 2
        return pltpu.make_async_copy(acc.at[:, columns], tiles.at[slot], tile_sem.at[slot])

    for t in range(2):
        fetch(t, 0).start()
        fetch(t, 1).start()
    g.greet()

    def product(slot):
        upper, lower = split(tiles[slot])
        both = mul(pair_ref[...], upper, rows_cols)
        return both[:rank] + both[rank:] + mul(pair_ref[:rank], lower, rows_cols)

    def pair_copy(w, rp):
        i = w * rows + rp
        return remote(held.at[i], pair_in.at[i], pair_sems.at[0, i], pair_sems.at[1, i], g.partner)

    def stage_copy(w, s, j):
        i = w * (rows - 1) + rows - 2 ** (stages - s) + j
        source = held.at[mine + w * rows + g.block(s, j, g.peer_row(s))]
        return remote(source, stage_in.at[i], stage_sems.at[0, i], stage_sems.at[1, i], g.peer(s))

    def chip_copy(w):
        return remote(
            held.at[mine + w * rows + g.r], chip_in.at[w], chip_sems.at[0, w], chip_sems.at[1, w],
            g.chip_device(chip_of(w)),
        )

    def compute(t):
        def one(kind, carry):
            w, rp = block_of(t, kind)
            fetch(t, kind).wait()
            held[kind * mine + w * rows + rp] = product(kind * 2 + t % 2)

            @pl.when(kind == 0)
            def _():
                pair_copy(w, rp).start()

            @pl.when(t + 2 < chips * rows)
            def _():
                fetch(t + 2, kind).start()

            return carry

        lax.fori_loop(0, 2, one, 0)

    def pair(t):
        w, rp = block_of(t)
        pair_copy(w, rp).wait_recv()
        held[mine + w * rows + rp] += pair_in[w * rows + rp]

        @pl.when(t % rows < half)
        def _():
            stage_copy(w, 0, t % rows).start()

    def halve(w, s):
        for j in range(g.count(s - 1)):
            i = w * (rows - 1) + rows - 2 ** (stages - s + 1) + j
            stage_copy(w, s - 1, j).wait_recv()
            held[mine + w * rows + g.block(s - 1, j, g.r)] += stage_in[i]
        for j in range(g.count(s)):
            stage_copy(w, s, j).start()

    def leave(w):
        i = w * (rows - 1) + rows - 2
        stage_copy(w, stages - 1, 0).wait_recv()
        held[mine + w * rows + g.r] += stage_in[i]
        if w < chips - 1:
            chip_copy(w).start()

    part, full, *rest = reduce_scratch

    part[...] = mul(pair_ref[:rank], grads_ref[...], rows_cols) + mul(
        pair_ref[rank:], grads_ref[...], rows_cols
    )
    tokens = AllReduce(g, part, full, *rest)
    phases = iter(tokens.phases)

    def tick():
        phase = next(phases, None)
        if phase is not None:
            phase()

    tick()
    steps = chips * rows
    lag, gap, ticks = power_lag, power_gap, power_ticks
    later = {}
    for w in range(chips):
        for s in range(1, stages):
            later.setdefault(min(lag + gap * w + 3 * (s - 1), steps + 2 * w + s), []).append(
                functools.partial(halve, w, s)
            )
    for w in range(chips):
        later.setdefault(min(lag + gap * w + gap, steps + 2 * w + 3), []).append(
            functools.partial(leave, w)
        )
    def both(t, carry):
        compute(t)

        @pl.when(t > 0)
        def _():
            pair(t - 1)

        return carry

    for t in range(0, max(max(later), steps) + power_group, power_group):
        for _ in range(sum(t <= at < t + power_group for at in ticks)):
            tick()
        if t < steps:
            lax.fori_loop(t, min(steps, t + power_group), both, 0)
        if steps <= t < steps + power_group:
            pair(steps - 1)
        for at in range(t, t + power_group):
            for event in later.get(at, ()):
                event()
    for phase in phases:
        phase()
    upper, lower = split(full[...])
    total = mul(upper, acts_ref[...], cols_cols) + mul(lower, acts_ref[...], cols_cols)
    total = total + held[mine + (chips - 1) * rows + g.r]
    for w in range(chips - 1):
        chip_copy(w).wait_recv()
        total = total + chip_in[w]
    out_ref[...] = total

    tokens.drain()
    for w in range(chips):
        def done(rp, carry):
            pair_copy(w, rp).wait_send()
            return carry

        lax.fori_loop(0, rows, done, 0)
        for s in range(stages):
            for j in range(g.count(s)):
                stage_copy(w, s, j).wait_send()
        if w < chips - 1:
            chip_copy(w).wait_send()


def power_scatter(accumulated, pair, grads, acts, rows, cols, collective_id):
    rank = pair.shape[0] // 2
    blk = acts.shape[0]
    chips = cols // 2
    blocks = chips * rows
    passed = chips * (rows - 1)
    return pl.pallas_call(
        functools.partial(power_kernel, rows, cols),
        out_shape=jax.ShapeDtypeStruct((rank, blk), f32),
        in_specs=[ANY, VMEM, VMEM, VMEM],
        out_specs=VMEM,
        scratch_shapes=[
            pltpu.VMEM((4, accumulated.shape[0], blk), f32),
            pltpu.VMEM((2 * blocks, rank, blk), f32),
            pltpu.VMEM((blocks, rank, blk), f32),
            pltpu.VMEM((passed, rank, blk), f32),
            pltpu.VMEM((chips - 1, rank, blk), f32),
            DMA((4,)),
            DMA((2, blocks)),
            DMA((2, passed)),
            DMA((2, chips - 1)),
            *AllReduce.scratch(rank, acts.shape[1], rows, chips),
        ],
        compiler_params=pltpu.CompilerParams(
            collective_id=collective_id, has_side_effects=True, vmem_limit_bytes=vmem_bytes
        ),
        name="power_scatter",
    )(accumulated, pair, grads, acts)


class Interleaved:
    def __init__(self, phases):
        self.left = list(phases)

    def tick(self, count=1):
        for _ in range(count):
            if self.left:
                self.left.pop(0)()

    def rest(self):
        self.tick(len(self.left))


def image_kernel(
    rows, cols, acc, seed_ref, grads_ref, acts_ref, out_ref,
    tiles, image, seeds, tile_sem, pair_sems, stage_sems, share_sems, *reduce_scratch,
):
    g = Grid(rows, cols)
    stages = g.stages
    blk, rank = seeds.shape[2], seeds.shape[3]
    own_rows = seed_ref.shape[0]
    pieces = own_rows // (2 * blk)
    tokens_rows = acts_ref.shape[0]

    def piece(rp, h, i):
        return (rp * 2 + h) * pieces + i

    def fetch(p, slot):
        columns = pl.ds(pl.multiple_of(p * blk, blk), blk)
        return pltpu.make_async_copy(acc.at[:, columns], tiles.at[slot], tile_sem.at[slot])

    def order(t):
        u = t - 2 * pieces
        wave = u // (2 * (rows - 1))
        inner = u % (2 * (rows - 1))
        other = piece((g.r + 1 + inner // 2) % rows, inner % 2, (wave + 1) % pieces)
        own = piece(g.r, t // pieces, t % pieces)
        return jnp.where(t < 2 * pieces, own, other)

    count = 2 * pieces * rows
    depth = tiles.shape[0]
    for t in range(depth - 1):
        fetch(order(t), t).start()
    g.greet()

    def spread(q):
        at = pl.ds(pl.multiple_of(q * blk, blk), blk)
        upper, lower = split(seed_ref[at])
        target = g.r * 2 * pieces + q
        seeds[target, 0] = upper
        seeds[target, 1] = lower

    share = blk // g.chips

    def shared(p, z):
        return seeds.at[p, :, pl.ds(pl.multiple_of(z * share, share), share)]

    def share_copy(s, j, w, z):
        at = (rows - 2 ** (stages - s) + j) * (g.chips - 1) + w
        ref = shared(piece(g.block(s, j, g.peer_row(s)), g.k, 0), z)
        device = g.chip_device(g.chip(w)[0])
        return remote(ref, ref, share_sems.at[0, at], share_sems.at[1, at], device)

    def pair_copy(rp, i):
        p = piece(rp, g.k, i)
        at = i * rows + rp
        return remote(seeds.at[p], seeds.at[p], pair_sems.at[0, at], pair_sems.at[1, at], g.partner)

    def pair_wait(rp, i):
        at = i * rows + rp
        p = piece(rp, 1 - g.k, i)
        remote(seeds.at[p], seeds.at[p], pair_sems.at[0, at], pair_sems.at[1, at], g.partner).wait_recv()

    def stage_copy(i, s, j, base):
        at = i * (rows - 1) + rows - 2 ** (stages - s) + j
        p = piece(g.block(s, j, base), g.k, i)
        ref = seeds.at[p] if i else shared(p, g.z)
        return remote(ref, ref, stage_sems.at[0, at], stage_sems.at[1, at], g.peer(s))

    def send(i, s):
        for j in range(g.count(s)):
            stage_copy(i, s, j, g.r).start()

    def land(i, s):
        for j in range(g.count(s)):
            stage_copy(i, s, j, g.peer_row(s)).wait_recv()
            if i:
                pair_copy(g.block(s, j, g.peer_row(s)), i).start()
            else:
                for w in range(g.chips - 1):
                    share_copy(s, j, w, g.z).start()

    def gather():
        for s in reversed(range(stages)):
            for j in range(g.count(s)):
                for w in range(g.chips - 1):
                    share_copy(s, j, w, g.chip(w)[1]).wait_recv()
                pair_copy(g.block(s, j, g.peer_row(s)), 0).start()

    def compute(t):
        slot = t % depth
        p = order(t)
        fetch(p, slot).wait()

        @pl.when(t + depth - 1 < count)
        def _():
            fetch(order(t + depth - 1), (t + depth - 1) % depth).start()

        upper, lower = split(tiles[slot])
        image[...] += (
            mul(upper, seeds[p, 0], rows_cols)
            + mul(lower, seeds[p, 0], rows_cols)
            + mul(upper, seeds[p, 1], rows_cols)
        )

    def own_step(t, carry):
        compute(t)
        return carry

    def other_step(t, carry):
        inner = (t - 2 * pieces) % (2 * (rows - 1))
        wave = (t - 2 * pieces) // (2 * (rows - 1))
        rp = (g.r + 1 + inner // 2) % rows

        @pl.when(inner % 2 == 1 - g.k)
        def _():
            pair_wait(rp, (wave + 1) % pieces)

        compute(t)
        return carry

    for i in range(pieces):
        spread(g.k * pieces + i)
        send(i, stages - 1)
    own = pl.ds(pl.multiple_of(g.c * tokens_rows, tokens_rows), tokens_rows)
    turned = seed_ref[own].T
    part, full, *rest = reduce_scratch
    upper, lower = split(turned)
    part[...] = mul(upper, acts_ref[...], rows_cols) + mul(lower, acts_ref[...], rows_cols)
    tokens = AllReduce(g, part, full, *rest)
    small = Interleaved(tokens.phases)
    small.tick()

    def spread_other(i, carry):
        spread((1 - g.k) * pieces + i)
        return carry

    lax.fori_loop(0, pieces, spread_other, 0)
    image[...] = jnp.zeros_like(image)
    first = 2 * pieces // (stages + 1)
    done = 0
    lag = stages
    for at in range(pieces + lag):
        small.tick(image_ticks[at] if at < len(image_ticks) else 1)
        for late in range(stages):
            i = at - late
            if 0 <= i < pieces:
                s = stages - 1 - late
                land(i, s)
                if s > 0:
                    send(i, s - 1)
        if at == image_gather:
            gather()
        if done < 2 * pieces:
            stop = min(2 * pieces, done + first)
            lax.fori_loop(done, stop, own_step, 0)
            done = stop
        i = at - lag
        if 0 <= i < pieces:
            lax.fori_loop(done, 2 * pieces, own_step, 0)
            done = 2 * pieces
            start = 2 * pieces + i * 2 * (rows - 1)
            lax.fori_loop(start, start + 2 * (rows - 1), other_step, 0)
    small.rest()
    upper, lower = split(full[...])
    total = image[...] + mul(grads_ref[...], upper, cols_cols) + mul(grads_ref[...], lower, cols_cols)
    upper, lower = split(total.T)
    out_ref[:rank] = upper
    out_ref[rank:] = lower

    tokens.drain()
    for i in range(pieces):
        for s in range(stages):
            for j in range(g.count(s)):
                stage_copy(i, s, j, g.r).wait_send()
                pair_copy(g.block(s, j, g.peer_row(s)), i).wait_send()
    for s in range(stages):
        for j in range(g.count(s)):
            for w in range(g.chips - 1):
                share_copy(s, j, w, g.z).wait_send()


def image_pair(accumulated, seed, grads, acts, rows, cols, collective_id):
    rank = seed.shape[1]
    height, width = accumulated.shape
    blk = 256 if seed.shape[0] % 512 == 0 else seed.shape[0] // 2
    total = width // blk
    pieces = total // (2 * rows)
    return pl.pallas_call(
        functools.partial(image_kernel, rows, cols),
        out_shape=jax.ShapeDtypeStruct((2 * rank, height), bf16),
        in_specs=[ANY, VMEM, VMEM, VMEM],
        out_specs=VMEM,
        scratch_shapes=[
            pltpu.VMEM((4, height, blk), f32),
            pltpu.VMEM((height, rank), f32),
            pltpu.VMEM((total, 2, blk, rank), bf16),
            DMA((4,)),
            DMA((2, pieces * rows)),
            DMA((2, pieces * (rows - 1))),
            DMA((2, (cols // 2 - 1) * (rows - 1))),
            *AllReduce.scratch(rank, acts.shape[1], rows, cols // 2),
        ],
        compiler_params=pltpu.CompilerParams(
            collective_id=collective_id, has_side_effects=True, vmem_limit_bytes=vmem_bytes
        ),
        name="image_pair",
    )(accumulated, seed, grads, acts)


def project_kernel(
    rows, cols, acc, basis_ref, turned_ref, grads_ref, acts_ref, out_ref, full_ref,
    tiles, tile_sem, pair_sems, stage_sems, chip_sems, *reduce_scratch,
):
    g = Grid(rows, cols)
    chips, stages = g.chips, g.stages
    blk = basis_ref.shape[0]
    count = chips * rows

    def chip_of(w):
        return (g.z + chips - w) % chips

    def at_of(rp, w, core):
        at = ((rp * chips + chip_of(w)) * 2 + core) * blk
        return full_ref.at[pl.ds(pl.multiple_of(at, blk), blk)]

    def fetch(t):
        w, rp = t // rows, t % rows
        at = (rp * chips + chip_of(w)) * 2 * blk
        columns = pl.ds(pl.multiple_of(at, 2 * blk), 2 * blk)
        return pltpu.make_async_copy(acc.at[:, columns], tiles.at[t % 2], tile_sem.at[t % 2])

    fetch(0).start()
    fetch(1).start()
    g.greet()
    own_rows = pl.ds(pl.multiple_of(((g.r * chips + g.z) * 2 + g.k) * blk, blk), blk)
    full_ref[own_rows] = basis_ref[...]

    def pair_copy(rp, w):
        i = w * rows + rp
        ref = at_of(rp, w, g.k)
        return remote(ref, ref, pair_sems.at[0, i], pair_sems.at[1, i], g.partner)

    def pair_wait(rp, w):
        i = w * rows + rp
        ref = at_of(rp, w, 1 - g.k)
        remote(ref, ref, pair_sems.at[0, i], pair_sems.at[1, i], g.partner).wait_recv()

    def stage_copy(w, s, j, base):
        i = w * (rows - 1) + rows - 2 ** (stages - s) + j
        ref = at_of(g.block(s, j, base), w, g.k)
        return remote(ref, ref, stage_sems.at[0, i], stage_sems.at[1, i], g.peer(s))

    def chip_copy(w, z):
        at = ((g.r * chips + z) * 2 + g.k) * blk
        ref = full_ref.at[pl.ds(pl.multiple_of(at, blk), blk)]
        device = g.chip_device(g.chip(w)[0])
        return remote(ref, ref, chip_sems.at[0, w], chip_sems.at[1, w], device)

    def enter(w):
        if w > 0:
            chip_copy(w - 1, chip_of(w)).wait_recv()
        stage_copy(w, stages - 1, 0, g.r).start()
        pair_copy(g.r, w).start()

    def land(w, s):
        for j in range(g.count(s)):
            stage_copy(w, s, j, g.peer_row(s)).wait_recv()
        if s > 0:
            for j in range(g.count(s - 1)):
                stage_copy(w, s - 1, j, g.r).start()
        for j in range(g.count(s)):
            pair_copy(g.block(s, j, g.peer_row(s)), w).start()

    for w in range(chips - 1):
        chip_copy(w, g.z).start()
    part, full, *rest = reduce_scratch
    enter(0)
    part[...] = mul(turned_ref[...], acts_ref[...], rows_cols)
    tokens = AllReduce(g, part, full, *rest)
    small = Interleaved(tokens.phases)
    small.tick()
    out_ref[...] = jnp.zeros_like(out_ref)

    def step(t, carry):
        w, rp = t // rows, t % rows
        fetch(t).wait()
        pair_wait(rp, w)
        at = (rp * chips + chip_of(w)) * 2 * blk
        block = full_ref[pl.ds(pl.multiple_of(at, 2 * blk), 2 * blk)]
        out_ref[...] += mul(tiles[t % 2].astype(bf16), block, rows_cols)

        @pl.when(t + 2 < count)
        def _():
            fetch(t + 2).start()

        return carry

    for at in range(chips + stages + 1):
        small.tick(project_ticks[at] if at < len(project_ticks) else 1)
        for late in range(stages + 1):
            w = at - late
            if 0 <= w < chips:
                if late == 0:
                    if w > 0:
                        enter(w)
                else:
                    land(w, stages - late)
        w = at - stages
        if 0 <= w < chips:
            lax.fori_loop(w * rows, (w + 1) * rows, step, 0)
    small.rest()
    upper, lower = split(full[...])
    out_ref[...] += mul(grads_ref[...], upper, cols_cols) + mul(grads_ref[...], lower, cols_cols)

    tokens.drain()
    for w in range(chips - 1):
        chip_copy(w, g.z).wait_send()
    for w in range(chips):
        pair_copy(g.r, w).wait_send()
        for s in range(stages):
            for j in range(g.count(s)):
                stage_copy(w, s, j, g.r).wait_send()
                pair_copy(g.block(s, j, g.peer_row(s)), w).wait_send()


def project(accumulated, basis, turned, grads, acts, rows, cols, collective_id):
    height, width = accumulated.shape
    blk, rank = basis.shape
    chips = cols // 2
    return pl.pallas_call(
        functools.partial(project_kernel, rows, cols),
        out_shape=(
            jax.ShapeDtypeStruct((height, rank), f32),
            jax.ShapeDtypeStruct((width, rank), bf16),
        ),
        in_specs=[ANY, VMEM, VMEM, VMEM, VMEM],
        out_specs=(VMEM, VMEM),
        scratch_shapes=[
            pltpu.VMEM((2, height, 2 * blk), f32),
            DMA((2,)),
            DMA((2, chips * rows)),
            DMA((2, chips * (rows - 1))),
            DMA((2, chips - 1)),
            *AllReduce.scratch(rank, acts.shape[1], rows, chips),
        ],
        compiler_params=pltpu.CompilerParams(
            collective_id=collective_id, has_side_effects=True, vmem_limit_bytes=vmem_bytes
        ),
        name="project",
    )(accumulated, basis, turned, grads, acts)


def orthogonal_kernel(rows, cols, step, power_ref, out_ref, turned_ref, gram, rest, *reduce_scratch):
    g = Grid(rows, cols)
    g.greet()
    part, full, *others = reduce_scratch
    rank = gram.shape[0]
    count = rank // step
    product = mul(power_ref[...], power_ref[...], cols_cols, highest)
    across = part.shape[1] // step
    lower_blocks = [(i, j) for i in range(count) for j in range(i + 1)]

    def cut(n):
        return slice(n * step, (n + 1) * step)

    for n in range(count * across):
        i, j = lower_blocks[n] if n < len(lower_blocks) else (0, 0)
        part[cut(n // across), cut(n % across)] = product[cut(i), cut(j)]
    total = AllReduce(g, part, full, *others)
    for phase in total.phases:
        phase()
    rest[...] = power_ref[...]
    for n, (i, j) in enumerate(lower_blocks):
        gram[cut(i), cut(j)] = full[cut(n // across), cut(n % across)]
        if i > j:
            gram[cut(j), cut(i)] = jnp.zeros((step, step), f32)
    part_step = step // 2
    lanes = lax.broadcasted_iota(jnp.int32, (part_step, part_step), 1)
    lines = lax.broadcasted_iota(jnp.int32, (part_step, part_step), 0)
    eights = lax.broadcasted_iota(jnp.int32, (8, step), 0)

    def invert(block):
        both = jnp.concatenate([block, (lanes == lines).astype(f32)], axis=1)
        parts = [both[8 * i : 8 * i + 8] for i in range(part_step // 8)]
        for n in range(0, part_step, 2):
            q, o = n // 8, n % 8
            wide = (8, step)
            first = jnp.broadcast_to(parts[q][:, n : n + 1], wide)
            second = jnp.broadcast_to(parts[q][:, n + 1 : n + 2], wide)
            row_a = jnp.broadcast_to(parts[q][o : o + 1], wide)
            row_b = jnp.broadcast_to(parts[q][o + 1 : o + 2], wide)
            aa = jnp.broadcast_to(first[o : o + 1], wide)
            ab = jnp.broadcast_to(first[o + 1 : o + 2], wide)
            bb = jnp.broadcast_to(second[o + 1 : o + 2], wide)
            scale = 1.0 / (aa * bb - ab * ab)
            take_a = (row_a * bb - row_b * ab) * scale
            take_b = (row_b * aa - row_a * ab) * scale
            if o < 6:
                later = eights > o + 1
                parts[q] = (
                    parts[q]
                    - jnp.where(later, first, 0.0) * take_a
                    - jnp.where(later, second, 0.0) * take_b
                )
            for i in range(q + 1, part_step // 8):
                parts[i] = (
                    parts[i]
                    - parts[i][:, n : n + 1] * take_a
                    - parts[i][:, n + 1 : n + 2] * take_b
                )
        both = jnp.concatenate(parts, axis=0)
        left, right = both[:, :part_step], both[:, part_step:]
        odd = lines % 2 == 1
        diagonal = jnp.sum(jnp.where(lanes == lines, left, 0.0), axis=1, keepdims=True)
        side = jnp.sum(
            jnp.where(odd & (lanes == lines - 1), left, 0.0), axis=1, keepdims=True
        )
        diagonal = jnp.broadcast_to(diagonal, left.shape)
        side = jnp.broadcast_to(side, left.shape)
        ratio = jnp.where(odd, side / pltpu.roll(diagonal, 1, 0), 0.0)
        right = right - ratio * pltpu.roll(right, 1, 0)
        return right * lax.rsqrt(diagonal - ratio * side)

    def eliminate(j, carry):
        at = pl.ds(pl.multiple_of(j * step, step), step)
        block = gram[at, at]
        first = invert(block[:part_step, :part_step])
        link = mul(block[part_step:, :part_step], first, cols_cols, highest)
        second = invert(block[part_step:, part_step:] - mul(link, link, cols_cols, highest))
        below = -mul(second, mul(link, first, rows_cols, highest), rows_cols, highest)
        above = jnp.zeros_like(below)
        inverse = jnp.concatenate(
            [jnp.concatenate([first, above], axis=1), jnp.concatenate([below, second], axis=1)],
            axis=0,
        )
        panel = mul(gram[:, at], inverse, cols_cols, highest)
        below = lax.broadcasted_iota(jnp.int32, panel.shape, 0) >= (j + 1) * step
        panel = jnp.where(below, panel, 0.0)
        gram[...] -= mul(panel, panel, cols_cols, highest)
        solved = mul(inverse, rest[at], rows_cols, highest)
        rest[...] -= mul(panel, solved, rows_cols, highest)
        turned_ref[at] = solved.astype(bf16)
        return carry

    lax.fori_loop(0, rank // step, eliminate, 0)
    out_ref[...] = turned_ref[...].astype(f32).T.astype(bf16)
    total.drain()


def orthogonal(power_turned, rows, cols, collective_id):
    rank, blk = power_turned.shape
    blocks = rank // 128
    return pl.pallas_call(
        functools.partial(orthogonal_kernel, rows, cols, 128),
        out_shape=(
            jax.ShapeDtypeStruct((blk, rank), bf16),
            jax.ShapeDtypeStruct((rank, blk), bf16),
        ),
        in_specs=[VMEM],
        out_specs=(VMEM, VMEM),
        scratch_shapes=[
            pltpu.VMEM((rank, rank), f32),
            pltpu.VMEM((rank, blk), f32),
            *AllReduce.scratch(rank, 128 * -(-blocks * (blocks + 1) // (2 * blocks)), rows, cols // 2),
        ],
        compiler_params=pltpu.CompilerParams(
            collective_id=collective_id, has_side_effects=True, vmem_limit_bytes=vmem_bytes
        ),
        name="orthogonal",
    )(power_turned)


def solve_lower(gram_matrix, right):
    rank = gram_matrix.shape[0]
    step = 128 if rank % 128 == 0 else rank
    count = rank // step
    cut = lambda n: slice(n * step, (n + 1) * step)
    trailing = {
        (i, j): gram_matrix[cut(i), cut(j)] for i in range(count) for j in range(i + 1)
    }
    rests = [right[cut(i)] for i in range(count)]
    solved = []
    for j in range(count):
        factor = lax.linalg.cholesky(trailing[j, j], symmetrize_input=False)
        inverse = jax.scipy.linalg.solve_triangular(
            factor, jnp.eye(step, dtype=jnp.float32), lower=True
        )
        panel = {
            i: mul(trailing[i, j], inverse, cols_cols, highest) for i in range(j + 1, count)
        }
        solved.append(mul(inverse, rests[j], rows_cols, highest))
        for i in range(j + 1, count):
            rests[i] = rests[i] - mul(panel[i], solved[j], rows_cols, highest)
            for k in range(j + 1, i + 1):
                trailing[i, k] = trailing[i, k] - mul(panel[i], panel[k], cols_cols, highest)
    return jnp.concatenate(solved, axis=0)


def finish(moment_first, moment_second, projected, full_basis):
    first_next = beta_first * moment_first + (1.0 - beta_first) * projected
    second_next = beta_second * moment_second + (1.0 - beta_second) * projected * projected
    direction = (
        first_next / correct_first / (jnp.sqrt(second_next / correct_second) + epsilon_value)
    )
    lifted = lift_scale * mul(direction.astype(bf16), full_basis, cols_cols)
    return first_next, second_next, lifted


def plain_body(activations, out_grads, accumulated, seed_basis, moment_first, moment_second):
    share_rows = activations.shape[0]
    acts = activations.astype(jnp.float32)
    grads = out_grads.astype(jnp.float32)
    own_seed = lax.dynamic_slice_in_dim(
        seed_basis, lax.axis_index("col") * share_rows, share_rows, 0
    )
    full_seed = lax.all_gather(own_seed, every, axis=0, tiled=True)
    seed_tokens = lax.psum(mul(acts, own_seed, rows_rows, highest), every)
    image_rows = mul(accumulated, full_seed, rows_cols, high) + mul(
        grads, seed_tokens, rows_cols, high
    )
    image_tokens = lax.psum(mul(grads, image_rows, rows_rows, high), every)
    power_part = mul(accumulated, image_rows, rows_rows, high)
    power_rows = lax.psum_scatter(
        power_part, every, scatter_dimension=0, tiled=True
    ) + mul(acts, image_tokens, rows_cols, highest)
    gram_matrix = lax.psum(mul(power_rows, power_rows, rows_rows, highest), every)
    gram_matrix, held_acts = lax.optimization_barrier((gram_matrix, activations))
    full_acts = lax.all_gather(held_acts, every, axis=0, tiled=True)
    solved = solve_lower(gram_matrix, power_rows.T)
    basis_rows = solved.T.astype(jnp.bfloat16)
    sent_rows, full_acts = lax.optimization_barrier((basis_rows, full_acts))
    full_basis = lax.all_gather(sent_rows, every, axis=0, tiled=True)
    basis_tokens = mul(full_acts, full_basis, rows_rows)
    projected = mul(accumulated.astype(jnp.bfloat16), full_basis, rows_cols) + mul(
        grads, basis_tokens, rows_cols, high
    )
    return (basis_rows, *finish(moment_first, moment_second, projected, full_basis))


def body(rows, cols, activations, out_grads, accumulated, seed_basis, moment_first, moment_second):
    common = (out_grads, activations, rows, cols)
    pair = image_pair(accumulated, seed_basis, *common, 1)
    power_turned = power_scatter(accumulated, pair, *common, 2)
    basis_rows, turned = orthogonal(power_turned, rows, cols, 3)
    projected, full_basis = project(accumulated, basis_rows, turned, *common, 4)
    return (basis_rows, *finish(moment_first, moment_second, projected, full_basis))


def solution(mesh):
    rows, cols = mesh.shape["row"], mesh.shape["col"]

    def place(activations, *others):
        rank = others[2].shape[1]
        fits = rows & (rows - 1) == 0 and rows > 1 and cols % 2 == 0 and cols > 2
        fits = fits and activations.shape[0] % 128 == 0 and rank % (8 * rows * cols) == 0
        fits = fits and rank % 128 == 0 and 256 % (16 * cols // 2) == 0
        if fits:
            return body(rows, cols, activations, *others)
        return plain_body(activations, *others)

    split_rows = P(("row", "col"), None)
    in_specs = (split_rows, split_rows, split_rows, P("row", None), split_rows, split_rows)
    return jax.shard_map(
        place, mesh=mesh, in_specs=in_specs, out_specs=(split_rows,) * 4, check_vma=False
    )
```
